32 devices in a mesh: tiles: 16 (over z, y, x), chan: 2 (over core).
Axes of the slice: x: 2, y: 2, z: 4, core: 2. Of those that a mesh axis runs over, the one named last changes fastest.
Arguments:
- features: bfloat16 [64, 2048, 256], P('chan', 'tiles'), may hold values from -6 to 6
- tile_valid: int32 [256, 32], P('tiles'), may hold values 0 or 1
- parent_owner: int32 [2048], P('tiles'), may hold values from 0 to 15, as said below
- w_first: bfloat16 [9, 64, 64], P(None, 'chan'), may hold values from -0.25 to 0.25
- w_second: bfloat16 [9, 64, 64], P(None, 'chan'), may hold values from -0.25 to 0.25
- w_merge: bfloat16 [4, 64, 64], P(None, None, 'chan'), may hold values from -0.375 to 0.375
Outputs:
- enhanced: bfloat16 [64, 2048, 256], P('chan', 'tiles')
- parents: bfloat16 [64, 3072, 64], P('chan', 'tiles')
The draws below stay inside these ranges and needn't reach their ends.
Inputs may be any that keep to these rules, and one draw needn't show every extreme that they name: `parent_owner`: within the 128 parents whose children lie on one index of tiles, no owner appears more than 16 times, and some owner appears exactly 16 times for some index. Half of the owners own 3 * 64 parents in all, the other half 128 / 2.
All inputs are finite; a program needn't handle non-finite values. No bound on the sum of `tile_valid` on one device may be relied on, other than what follows from the above.
Results may differ from the reference program's by a relative error of at most 0.0052.
Values may be sent and summed in bfloat16 or wider, within the bound.
No kernel may reach another device: no remote copies, remote signals or barrier semaphores. Data moves between devices by JAX's collectives and lax.ppermute only.
A program may use at most 128 MiB of HBM per device.

```python
import jax
import jax.numpy as jnp
from jax import lax

C = 64
TS = 8
NB = 32
GD = 16
W = 256
NG = 256
H = 2048
PD = 128
OWN_CAP = 192
N_TILES = 16


def draw_parent_owner(key, part):
    devices = N_TILES
    half_devices = devices // 2
    key_kind, key_label, key_shuffle = jax.random.split(key, 3)
    kind_order = jax.random.permutation(key_kind, devices).astype(jnp.int32)
    position = jnp.argsort(kind_order, stable=True).astype(jnp.int32)
    spread_kind = position < half_devices
    sub_index = jnp.where(spread_kind, position, position - half_devices)
    row_ids = jnp.arange(PD, dtype=jnp.int32)
    spread_owner = (sub_index[:, None] * PD + row_ids[None, :]) % devices
    heavy_owner = (sub_index[:, None] * (PD // 2) + row_ids[None, :] // 2) % half_devices
    virtual = jnp.where(spread_kind[:, None], spread_owner, heavy_owner)
    labels = jax.random.permutation(key_label, devices).astype(jnp.int32)
    owner_rows = jnp.take(labels, virtual)
    shuffle_keys = jax.random.split(key_shuffle, devices)
    shuffles = jax.vmap(lambda one_key: jax.random.permutation(one_key, PD))(shuffle_keys)
    shuffled = jnp.take_along_axis(owner_rows, shuffles, axis=1)
    return shuffled.reshape(-1).astype(jnp.int32)


def place_ends(result, stream_key, smallest, high):
    longest = result.shape.index(max(result.shape))
    spots = []
    for shift in (0, 1):
        where = [jax.random.randint(jax.random.fold_in(stream_key, axis), (), 0, length) for axis, length in enumerate(result.shape)]
        where[longest] = (where[longest] + shift) % result.shape[longest]
        spots.append(tuple(where))
    return result.at[spots[0]].set(smallest).at[spots[1]].set(high)


def level_of(stream_key, dims, cuts, low, largest):
    factor_of, own = 1.0, jax.random.fold_in(stream_key, 6)
    for axis_at, blocks in cuts:
        steps = jnp.exp(jax.random.uniform(jax.random.fold_in(own, axis_at), (blocks,), jnp.float32, low / len(cuts), largest / len(cuts)))
        factor_of = factor_of * jnp.repeat(steps, dims[axis_at] // blocks).reshape([-1 if axis == axis_at else 1 for axis in range(len(dims))])
    return factor_of


def centred(stream_key, dims, scale, reach, cuts=(), held_as=jnp.bfloat16):
    gain = level_of(stream_key, dims, cuts, -0.22, 0.18) if cuts else 1.0
    drawn = jax.random.normal(stream_key, dims, jnp.float32) * scale * gain
    return jnp.minimum(jnp.maximum(drawn, -reach), reach).astype(held_as)


def setup_inputs(seed: int = 0) -> dict:
    key_list = jax.random.split(jax.random.key(seed), 7)
    return {
        "features": centred(key_list[0], (C, H, W), 1.0, 6.0, ((0, 2), (1, 16))),
        "tile_valid": place_ends((jax.random.randint(key_list[1], (NG, NB), 0, 8) < 7).astype(jnp.int32), jax.random.fold_in(key_list[1], 1), 0, 1),
        "parent_owner": draw_parent_owner(jax.random.fold_in(key_list[6], 71), 0),
        "w_first": centred(key_list[3], (9, C, C), (9 * C) ** -0.5, 0.25, ((1, 2),)),
        "w_second": centred(key_list[4], (9, C, C), (9 * C) ** -0.5, 0.25, ((1, 2),)),
        "w_merge": centred(key_list[5], (4, C, C), (4 * C) ** -0.5, 0.375, ((2, 2),)),
    }


def dilated(source, weights, dilation):
    kernel = weights.reshape(3, 3, weights.shape[1], weights.shape[2]).transpose(2, 3, 0, 1)
    return lax.conv_general_dilated(source[None], kernel, (1, 1), ((0, 0), (dilation, dilation)), rhs_dilation=(dilation, dilation), dimension_numbers=("NCHW", "OIHW", "NCHW"), preferred_element_type=jnp.float32)[0]


def reference(features, tile_valid, parent_owner, w_first, w_second, w_merge):
    channels = features.shape[0]
    row_count = GD * TS
    col_count = NB * TS
    cell_mask = jnp.broadcast_to(tile_valid.astype(jnp.float32)[:, None, :, None], (tile_valid.shape[0], TS, NB, TS)).reshape(-1, col_count)
    padded = jnp.pad(features, ((0, 0), (3, 3), (0, 0)))
    mask_pad = jnp.pad(cell_mask, ((3, 3), (0, 0)))

    def one_block(block_index):
        offset = (block_index * row_count).astype(jnp.int32)
        row_slab = lax.dynamic_slice_in_dim(padded, offset, row_count + 6, 1)
        mask_slab = lax.dynamic_slice_in_dim(mask_pad, offset, row_count + 6, 0)
        first_out = dilated(row_slab, w_first, 1)
        hidden = jnp.maximum(first_out * mask_slab[None, 1:-1], 0.0).astype(jnp.bfloat16)
        second_out = dilated(hidden, w_second, 2)
        enhanced = (mask_slab[None, 3:-3] * (row_slab[:, 3:-3].astype(jnp.float32) + second_out)).astype(jnp.bfloat16)
        taps_view = enhanced.astype(jnp.float32).reshape(channels, row_count // 2, 2, col_count // 2, 2)
        merged = jnp.zeros((channels, row_count // 2, col_count // 2), jnp.float32)
        for row_tap in range(2):
            for col_tap in range(2):
                merged = merged + jnp.einsum("oi,irc->orc", w_merge[2 * row_tap + col_tap].astype(jnp.float32), taps_view[:, :, row_tap, :, col_tap], precision=lax.Precision.HIGHEST)
        return enhanced, merged.astype(jnp.bfloat16)

    enhanced, merged = lax.map(one_block, jnp.arange(N_TILES, dtype=jnp.int32))
    enhanced_whole = enhanced.transpose(1, 0, 2, 3).reshape(channels, N_TILES * row_count, col_count)
    parent_tiles = merged.reshape(N_TILES, channels, GD // 2, TS, NB // 2, TS).transpose(1, 0, 2, 4, 3, 5).reshape(channels, -1, TS * TS)
    parent_count = parent_owner.shape[0]
    sorted_order = jnp.argsort(parent_owner, stable=True).astype(jnp.int32)
    counts = jax.ops.segment_sum(jnp.ones((parent_count,), jnp.int32), parent_owner, num_segments=N_TILES)
    starts = jnp.cumsum(counts) - counts
    sorted_owner = parent_owner[sorted_order]
    rank_sorted = jnp.arange(parent_count, dtype=jnp.int32) - starts[sorted_owner].astype(jnp.int32)
    rank_in_owner = jnp.zeros((parent_count,), jnp.int32).at[sorted_order].set(rank_sorted.astype(jnp.int32))
    slot_index = parent_owner * OWN_CAP + rank_in_owner
    parents = jnp.zeros((channels, N_TILES * OWN_CAP, TS * TS), jnp.bfloat16).at[:, slot_index].set(parent_tiles)
    return enhanced_whole, parents
```

```python
import functools

import jax
import jax.numpy as jnp
from jax import lax
from jax.experimental import pallas as pl
from jax.experimental.pallas import tpu as pltpu
from jax.sharding import PartitionSpec as P

BF = jnp.bfloat16
F32 = jnp.float32
HALO = 4
BLK = 16


def iota(shape, dim):
    return lax.broadcasted_iota(jnp.int32, shape, dim)


def ones_where(cond):
    return jnp.where(cond, 1.0, 0.0).astype(BF)


def mm(a, b):
    return jnp.dot(a, b, preferred_element_type=F32)


def mm_nt(a, b):
    return lax.dot_general(a, b, (((1,), (1,)), ((), ())), preferred_element_type=F32)


def swap_matrix(outer, inner):
    n = outer * inner
    row, col = iota((n, n), 0), iota((n, n), 1)
    return ones_where((row % inner == col // outer) & (row // inner == col % outer))


def shifted(x, amount):
    cols = x.shape[1]
    lane = iota(x.shape, 1)
    rolled = pltpu.roll(x, amount % cols, 1)
    inside = lane >= amount if amount > 0 else lane < cols + amount
    return jnp.where(inside, rolled, 0.0)


def conv_kernel(
    side,
    core_ref,
    feat_hbm,
    recv_ref,
    mid_own_ref,
    mid_oth_ref,
    out_own_ref,
    out_oth_ref,
    valid_ref,
    wown_ref,
    woth_ref,
    eown_ref,
    eoth_ref,
    mown_ref,
    moth_ref,
    feat,
    xs,
    hs,
    es,
    mask,
    w1,
    w2,
    wm,
    pa_ref,
    pb_ref,
    sem,
):
    core = core_ref[0]
    chans, rows, cols = recv_ref.shape
    allc = 2 * chans
    copy = pltpu.make_async_copy(
        feat_hbm.at[:, pl.ds(pl.multiple_of(core * rows, rows), rows), :], feat, sem
    )
    copy.start()

    for dst, base in ((w1, 0), (w2, 9)):
        total = None
        for b in range(3):
            tall = jnp.concatenate(
                [ref[base + 3 * a + b] for a in range(3) for ref in (wown_ref, woth_ref)], axis=0
            )
            src, pos = iota((allc, 3 * allc), 0), iota((allc, 3 * allc), 1)
            place = ones_where(pos == b * allc + (src + chans * core) % allc)
            part = mm(tall, place)
            total = part if total is None else total + part
        dst[...] = total.astype(BF)
    tall = jnp.concatenate(
        [ref[18 + 2 * a + b] for b in range(2) for a in range(2) for ref in (wown_ref, woth_ref)],
        axis=0,
    )
    order = ones_where(iota((allc, allc), 1) == (iota((allc, allc), 0) + chans * core) % allc)
    wm[...] = mm_nt(order, tall).astype(BF)

    tiles_r, tiles_c = valid_ref.shape
    widen = ones_where(iota((tiles_c, cols), 1) // side == iota((tiles_c, cols), 0))
    mask[pl.ds(side, tiles_r), :] = mm(valid_ref[...].astype(F32).astype(BF), widen)

    def put(dst, index, x, amount):
        dst[index, 0:allc, :] = shifted(x, amount).astype(BF)
        dst[index, allc : 2 * allc, :] = x.astype(BF)
        dst[index, 2 * allc : 3 * allc, :] = shifted(x, -amount).astype(BF)

    turn4 = swap_matrix(HALO, chans)
    first_row = 5
    for own_ref, oth_ref, outer in ((mid_own_ref, mid_oth_ref, False), (out_own_ref, out_oth_ref, True)):
        own, oth = mm(turn4, own_ref[...]), mm(turn4, oth_ref[...])
        low = core == 0 if outer else core == 1
        start = jnp.where(low, first_row - HALO, first_row + rows)
        for r in range(HALO):
            x = jnp.concatenate(
                [own[r * chans : (r + 1) * chans], oth[r * chans : (r + 1) * chans]], axis=0
            )
            put(xs, start + r, x, 1)
        if outer:
            top = own[0:1, :]
            bottom = own[(HALO - 1) * chans : (HALO - 1) * chans + 1, :]

            @pl.when(core == 0)
            def _():
                mask[pl.ds(side - 1, 1), :] = top

            @pl.when(core == 1)
            def _():
                mask[pl.ds(side + tiles_r, 1), :] = bottom

    xs[0] = jnp.zeros(xs.shape[1:], BF)
    turn = swap_matrix(BLK, BLK)
    copy.wait()

    def lay(step, carry):
        at = pl.multiple_of(step * BLK, BLK)
        parts = []
        for ref in (feat, recv_ref):
            for ch in range(0, chans, BLK):
                block = ref[ch : ch + BLK, pl.ds(at, BLK), :].reshape(BLK * BLK, cols)
                parts.append(mm(turn, block))
        for r in range(BLK):
            x = jnp.concatenate([p[r * BLK : (r + 1) * BLK] for p in parts], axis=0)
            put(xs, first_row + at + r, x, 1)
        return carry

    lax.fori_loop(0, rows // BLK, lay, 0)

    base = side + core * (rows // side)
    steps = rows // side + 1
    for i in range(2):
        pa_ref[i] = jnp.zeros((allc, cols), F32)
        pb_ref[i] = jnp.zeros((allc, cols), F32)

    def first(step, carry):
        pa, pb = pa_ref[0], pb_ref[0]
        m0 = mask[pl.ds(base + step - 1, 1), :]
        m1 = mask[pl.ds(base + step, 1), :]
        for j in range(side):
            q = step * side + j
            y = mm(w1[...], xs[q])
            total = pa + y[2 * allc :]
            pa = pb + y[allc : 2 * allc]
            pb = y[:allc]
            h = jnp.maximum(total * (m0 if j < 6 else m1), 0.0)
            put(hs, q, h, 2)
        pa_ref[0] = pa
        pb_ref[0] = pb
        return carry

    lax.fori_loop(0, steps, first, 0)

    pa_ref[0] = jnp.zeros((allc, cols), F32)
    pb_ref[0] = jnp.zeros((allc, cols), F32)
    half = cols // 2
    pick = ones_where(iota((cols, cols), 0) == 2 * (iota((cols, cols), 1) % half) + iota((cols, cols), 1) // half)

    def second(step, carry):
        pa, pb = [pa_ref[0], pa_ref[1]], [pb_ref[0], pb_ref[1]]
        m0 = mask[pl.ds(base + step - 1, 1), :]
        rows_e = []
        for j in range(side):
            q = step * side + j
            i = j % 2
            z = mm(w2[...], hs[q])
            total = pa[i] + z[2 * allc :]
            pa[i] = pb[i] + z[allc : 2 * allc]
            pb[i] = z[:allc]
            x = xs[jnp.maximum(q - 3, 0), allc : 2 * allc, :].astype(F32)
            e = (m0 * (x + total)).astype(BF)
            es[q] = e
            rows_e.append(e)
        for i in range(2):
            pa_ref[i] = pa[i]
            pb_ref[i] = pb[i]

        @pl.when(step > 0)
        def _():
            tile = step - 1
            s = mm(jnp.concatenate(rows_e, axis=0), pick).astype(BF)
            pairs = []
            for k in range(side // 2):
                sp = s[k * 2 * allc : (k + 1) * 2 * allc]
                pairs.append(jnp.concatenate([sp[:, :half], sp[:, half:]], axis=0))
            for k in range(0, side // 2, 2):
                both = mm(wm[...], jnp.concatenate(pairs[k : k + 2], axis=1)).astype(BF)
                for n in range(2):
                    u = (side // 2) * (tile % 2) + k + n
                    at_u = pl.ds(pl.multiple_of(u * chans, chans), chans)
                    at_g = pl.ds(pl.multiple_of((tile // 2) * half, half), half)
                    piece = both[:, n * half : (n + 1) * half]
                    mown_ref[at_u, at_g] = piece[:chans]
                    moth_ref[at_u, at_g] = piece[chans:]

        return carry

    lax.fori_loop(0, steps, second, 0)

    def unlay(step, carry):
        at = pl.multiple_of(step * BLK, BLK)
        for n, ref in ((0, eown_ref), (1, eoth_ref)):
            for ch in range(0, chans, BLK):
                c0 = n * chans + ch
                block = es[pl.ds(side + at, BLK), c0 : c0 + BLK, :].reshape(BLK * BLK, cols)
                ref[ch : ch + BLK, pl.ds(at, BLK), :] = (
                    mm(turn, block).astype(BF).reshape(BLK, BLK, cols)
                )
        return carry

    lax.fori_loop(0, rows // BLK, unlay, 0)


def pack_kernel(side, slots, core_ref, owner_ref, mown_ref, mrecv_ref, out_ref, code_ref):
    core = core_ref[0]
    count = owner_ref.shape[0]
    rows, width = mown_ref.shape
    blocks, all_rows, lanes = out_ref.shape
    per = side * slots
    owner = jnp.broadcast_to(owner_ref[...], (count, lanes))
    is_owner = owner == iota((count, lanes), 1)
    lower = ones_where(iota((count, count), 0) > iota((count, count), 1))
    earlier = mm(lower, ones_where(is_owner))
    within = jnp.sum(jnp.where(is_owner, earlier, 0.0), axis=1, keepdims=True)
    code = (owner * per).astype(F32) + within
    wide = jnp.broadcast_to(code[:, None, :], (count, side, lanes))
    step_v = (iota((count, side, lanes), 1) * slots).astype(F32)
    code_ref[...] = (wide + step_v).reshape(count * side, lanes).astype(jnp.int32)
    mine = pl.multiple_of(core * width, width)
    other = pl.multiple_of((1 - core) * width, width)

    def block(step, carry):
        outs = []
        for ref, at in ((mown_ref, mine), (mrecv_ref, other)):
            code = code_ref[pl.ds(at, width), :]
            cols = []
            for n in range(2):
                lane = iota((width, lanes), 1) + (2 * step + n) * lanes
                cols.append(ones_where(code == lane))
            outs.append(mm(ref[...], jnp.concatenate(cols, axis=1)))
        total = (outs[0] + outs[1]).astype(BF)
        for n in range(2):
            at = 2 * step + n
            out_ref[at, 0:rows, :] = total[:, n * lanes : (n + 1) * lanes]
            goal = (iota((count, lanes), 1) + at * lanes) // per
            tally = mm(jnp.ones((all_rows - rows, count), BF), ones_where(owner == goal))
            out_ref[at, rows:all_rows, :] = tally.astype(BF)
        return carry

    lax.fori_loop(0, blocks // 2, block, 0)


def unpack_kernel(side, slots, got_ref, out_ref, where_ref, *wide_refs):
    blocks, all_rows, lanes = got_ref.shape
    chans, cells, cap = out_ref.shape
    rows = side * chans
    per = side * slots
    lane0, lane1 = iota((lanes, lanes), 0), iota((lanes, lanes), 1)
    heads = lane0 % per == 0
    before = ones_where(heads & (lane0 // per < lane1 // per))
    every = ones_where(heads)
    room = where_ref.shape[0]
    slot = (iota((room, lanes), 1) % slots).astype(F32)
    goal = iota((room, lanes), 0).astype(F32)
    running = jnp.zeros((1, lanes), F32)
    for b in range(blocks):
        tally = got_ref[b, rows:all_rows, :]
        inside = mm(tally, before)[0:1]
        whole = mm(tally, every)[0:1]
        first = running + inside
        live = slot < jnp.broadcast_to(tally.astype(F32)[0:1], (room, lanes))
        where_ref[:, b * lanes : (b + 1) * lanes] = ones_where(live & (goal == first + slot))
        running = running + whole

    def column(v, carry):
        keep = iota((rows, lanes), 1) % per // slots == v
        total = None
        for b in range(0, blocks, 2):
            pair = [
                jnp.where(keep, got_ref[b + n, 0:rows, :], jnp.zeros((rows, lanes), BF))
                for n in range(2)
            ]
            part = mm_nt(
                jnp.concatenate(pair, axis=1), where_ref[:, b * lanes : (b + 2) * lanes]
            )
            total = part if total is None else total + part
        for u in range(side):
            piece = total[u * chans : (u + 1) * chans]
            for n, ref in enumerate(wide_refs):
                ref[pl.ds(u * side + v, chans, stride=cells), :] = piece[:, n * lanes : (n + 1) * lanes]
        return carry

    lax.fori_loop(0, side, column, 0)
    for n, ref in enumerate(wide_refs):
        keep = min(lanes, cap - n * lanes)
        full = ref[...].astype(BF).reshape(chans, cells, lanes)
        out_ref[:, :, n * lanes : n * lanes + keep] = full[:, :, :keep]


def on_device(features, tile_valid, parent_owner, w_first, w_second, w_merge):
    chans, row_count, col_count = features.shape
    tile_rows, tile_cols = tile_valid.shape
    side = row_count // tile_rows
    parents_dev = parent_owner.shape[0]
    devices = lax.axis_size("tiles")
    slots = 2 * max(1, parents_dev // devices)
    own_cap = 3 * parents_dev // 2
    rows = row_count // 2
    core = lax.axis_index("chan")
    core1 = jnp.reshape(core, (1,)).astype(jnp.int32)
    swap = [(0, 1), (1, 0)]

    flat = chans * HALO
    send_main = lax.dynamic_slice_in_dim(features, (1 - core) * rows, rows, 1)
    mid_send = lax.dynamic_slice_in_dim(features, rows - HALO + HALO * core, HALO, 1)
    mid_own = lax.dynamic_slice_in_dim(features, rows - HALO * core, HALO, 1)
    flags = jnp.repeat(tile_valid[jnp.array([0, tile_rows - 1])].astype(BF), side, axis=1)
    flags = jnp.broadcast_to(flags[:, None, :], (2, chans, col_count))
    head = jnp.concatenate([features[:, : HALO - 1], flags[0][:, None]], axis=1)
    tail = jnp.concatenate([flags[1][:, None], features[:, row_count - HALO + 1 :]], axis=1)
    head, tail = head.reshape(flat, col_count), tail.reshape(flat, col_count)
    down_up = [(2 * t, 2 * t + 2) for t in range(devices - 1)]
    down_up += [(2 * t + 1, 2 * t - 1) for t in range(1, devices)]
    cross = [(2 * t + 1, 2 * t + 2) for t in range(devices - 1)]
    cross += [(2 * t, 2 * t - 1) for t in range(1, devices)]
    both = ("tiles", "chan")
    outer_own = lax.ppermute(jnp.where(core == 0, tail, head), both, down_up)
    outer_oth = lax.ppermute(jnp.where(core == 0, head, tail), both, cross)
    w_own = jnp.concatenate([w_first, w_second, jnp.swapaxes(w_merge, 1, 2)], axis=0)
    w_oth = lax.ppermute(w_own, "chan", swap)
    mid_oth = lax.ppermute(mid_send.reshape(flat, col_count), "chan", swap)
    recv = lax.ppermute(send_main, "chan", swap)

    vmem = pl.BlockSpec(memory_space=pltpu.VMEM)
    smem = pl.BlockSpec(memory_space=pltpu.SMEM)
    allc = 2 * chans
    width = parents_dev * side // 2
    e_own, e_oth, m_own, m_oth = pl.pallas_call(
        functools.partial(conv_kernel, side),
        out_shape=(
            jax.ShapeDtypeStruct((chans, rows, col_count), BF),
            jax.ShapeDtypeStruct((chans, rows, col_count), BF),
            jax.ShapeDtypeStruct((side * chans, width), BF),
            jax.ShapeDtypeStruct((side * chans, width), BF),
        ),
        in_specs=[smem, pl.BlockSpec(memory_space=pl.ANY)] + [vmem] * 8,
        out_specs=(vmem,) * 4,
        scratch_shapes=[
            pltpu.VMEM((chans, rows, col_count), BF),
            pltpu.VMEM((rows + 16, 3 * allc, col_count), BF),
            pltpu.VMEM((rows + side, 3 * allc, col_count), BF),
            pltpu.VMEM((rows + side, allc, col_count), BF),
            pltpu.VMEM((tile_rows + 2 * side, col_count), F32),
            pltpu.VMEM((3 * allc, 3 * allc), BF),
            pltpu.VMEM((3 * allc, 3 * allc), BF),
            pltpu.VMEM((allc, 4 * allc), BF),
            pltpu.VMEM((2, allc, col_count), F32),
            pltpu.VMEM((2, allc, col_count), F32),
            pltpu.SemaphoreType.DMA,
        ],
        name="conv",
    )(core1, features, recv, mid_own.reshape(flat, col_count), mid_oth, outer_own, outer_oth, tile_valid, w_own, w_oth)

    m_recv = lax.ppermute(m_oth, "chan", swap)
    e_recv = lax.ppermute(e_oth, "chan", swap)
    lanes = 128
    blocks = devices * slots * side // lanes
    all_rows = side * chans + 8
    packed = pl.pallas_call(
        functools.partial(pack_kernel, side, slots),
        out_shape=jax.ShapeDtypeStruct((blocks, all_rows, lanes), BF),
        in_specs=[smem, vmem, vmem, vmem],
        out_specs=vmem,
        scratch_shapes=[pltpu.VMEM((parents_dev * side, lanes), jnp.int32)],
        name="pack",
    )(core1, parent_owner[:, None], m_own, m_recv)

    def to_peers(x):
        fold = devices // blocks
        if fold > 1:
            x = x.reshape(blocks, all_rows, fold, lanes // fold)
            x = x.transpose(0, 2, 1, 3).reshape(devices, all_rows, lanes // fold)
        x = lax.all_to_all(x, "tiles", split_axis=0, concat_axis=0, tiled=True)
        if fold > 1:
            x = x.reshape(blocks, fold, all_rows, lanes // fold)
            x = x.transpose(0, 2, 1, 3).reshape(blocks, all_rows, lanes)
        return x

    got = to_peers(packed)
    cells = side * side
    room = pl.cdiv(own_cap, lanes) * lanes
    parents = pl.pallas_call(
        functools.partial(unpack_kernel, side, slots),
        out_shape=jax.ShapeDtypeStruct((chans, cells, own_cap), BF),
        in_specs=[vmem],
        out_specs=vmem,
        scratch_shapes=[
            pltpu.VMEM((room, blocks * lanes), BF),
        ]
        + [pltpu.VMEM((chans * cells, lanes), F32)] * (room // lanes),
        name="unpack",
    )(got)
    enhanced = jnp.where(
        core == 0,
        jnp.concatenate([e_own, e_recv], axis=1),
        jnp.concatenate([e_recv, e_own], axis=1),
    )
    return enhanced, jnp.swapaxes(parents, 1, 2)


def solution(mesh):
    return jax.shard_map(
        on_device,
        mesh=mesh,
        in_specs=(
            P("chan", "tiles", None),
            P("tiles", None),
            P("tiles"),
            P(None, "chan", None),
            P(None, "chan", None),
            P(None, None, "chan"),
        ),
        out_specs=(P("chan", "tiles", None), P("chan", "tiles", None)),
        check_vma=False,
    )
```

```python
import functools

import jax
import jax.numpy as jnp
from jax import lax
from jax.experimental import pallas as pl
from jax.experimental.pallas import tpu as pltpu
from jax.sharding import PartitionSpec as P

BF = jnp.bfloat16
F32 = jnp.float32
HALO = 4
BLK = 16


def iota(shape, dim):
    return lax.broadcasted_iota(jnp.int32, shape, dim)


def ones_where(cond):
    return jnp.where(cond, 1.0, 0.0).astype(BF)


def mm(a, b):
    return jnp.dot(a, b, preferred_element_type=F32)


def mm_nt(a, b):
    return lax.dot_general(a, b, (((1,), (1,)), ((), ())), preferred_element_type=F32)


def swap_matrix(outer, inner):
    n = outer * inner
    row, col = iota((n, n), 0), iota((n, n), 1)
    return ones_where((row % inner == col // outer) & (row // inner == col % outer))


def shifted(x, amount):
    lanes = 128
    parts = [x[:, at : at + lanes] for at in range(0, x.shape[1], lanes)]
    turned = [pltpu.roll(p, amount % lanes, 1) for p in parts]
    lane = iota(parts[0].shape, 1)
    zero = jnp.zeros_like(parts[0])
    outs = []
    for n in range(len(parts)):
        if amount > 0:
            edge = turned[n - 1] if n else zero
            outs.append(jnp.where(lane < amount, edge, turned[n]))
        else:
            edge = turned[n + 1] if n + 1 < len(parts) else zero
            outs.append(jnp.where(lane >= lanes + amount, edge, turned[n]))
    return jnp.concatenate(outs, axis=1)


def widen_matrix(tiles_c, cols, side):
    return ones_where(iota((tiles_c, cols), 1) // side == iota((tiles_c, cols), 0))


def as_bf(x):
    return x.astype(F32).astype(BF)


def edges_kernel(side, place_ref, feat_hbm, valid_ref, one_ref, two_ref, edge, sems):
    core = place_ref[0]
    chans, rows, cols = feat_hbm.shape
    copies = []
    for n, at in enumerate((0, rows - BLK)):
        copies.append(pltpu.make_async_copy(feat_hbm.at[:, at : at + BLK, :], edge.at[n], sems.at[n]))
        copies[-1].start()
    tiles_r, tiles_c = valid_ref.shape
    masks = mm(as_bf(valid_ref[...]), widen_matrix(tiles_c, cols, side))
    flat = chans * HALO
    row, col = iota((flat, chans * BLK), 0), iota((flat, chans * BLK), 1)
    same = row // HALO == col // BLK
    spot = iota((flat, cols), 0) % HALO
    made = []
    for n in range(2):
        if n == 0:
            hit = same & (row % HALO == col % BLK) & (row % HALO < HALO - 1)
            flag, line = spot == HALO - 1, masks[0:1]
        else:
            hit = same & (row % HALO + BLK - HALO == col % BLK) & (row % HALO > 0)
            flag, line = spot == 0, masks[tiles_r - 1 : tiles_r]
        take = ones_where(hit)
        copies[n].wait()
        body = mm(take, edge[n].reshape(chans * BLK, cols))
        made.append(jnp.where(flag, jnp.broadcast_to(line, (flat, cols)), body).astype(BF))
    low = core == 0
    one_ref[...] = jnp.where(low, made[1], made[0])
    two_ref[...] = jnp.where(low, made[0], made[1])


def weights_kernel(place_ref, wown_ref, woth_ref, w1_ref, w2_ref, wm_ref):
    core = place_ref[0]
    chans, allc = wown_ref.shape[1:]
    for dst, base in ((w1_ref, 0), (w2_ref, 9)):
        total = None
        for b in range(3):
            tall = jnp.concatenate(
                [ref[base + 3 * a + b] for a in range(3) for ref in (wown_ref, woth_ref)], axis=0
            )
            src, pos = iota((allc, 3 * allc), 0), iota((allc, 3 * allc), 1)
            place = ones_where(pos == b * allc + (src + chans * core) % allc)
            part = mm(tall, place)
            total = part if total is None else total + part
        dst[...] = total.astype(BF)
    tall = jnp.concatenate(
        [ref[18 + 2 * a + b] for b in range(2) for a in range(2) for ref in (wown_ref, woth_ref)],
        axis=0,
    )
    order = ones_where(iota((allc, allc), 1) == (iota((allc, allc), 0) + chans * core) % allc)
    wm_ref[...] = mm_nt(order, tall).astype(BF)


def conv_kernel(
    side,
    place_ref,
    own_hbm,
    oth_hbm,
    out_own_ref,
    out_oth_ref,
    valid_ref,
    w1,
    w2,
    wm,
    es_hbm,
    mown_ref,
    moth_ref,
    feat,
    xs,
    hs,
    es,
    mask,
    pa_ref,
    pb_ref,
    in_sems,
    out_sem,
):
    core = place_ref[0]
    rows, allc, cols = es_hbm.shape
    chans = allc // 2
    main = rows // BLK
    copies = []
    for m in range(main + 1):
        at = rows - BLK * core if m == main else rows * core + BLK * m
        for n, ref in enumerate((own_hbm, oth_hbm)):
            copy = pltpu.make_async_copy(
                ref.at[:, pl.ds(pl.multiple_of(at, BLK), BLK), :], feat.at[n, m], in_sems.at[n, m]
            )
            copy.start()
            copies.append(copy)

    tiles_r, tiles_c = valid_ref.shape
    mask[pl.ds(side, tiles_r), :] = mm(as_bf(valid_ref[...]), widen_matrix(tiles_c, cols, side))

    def put(dst, index, x, amount):
        dst[index, 0:allc, :] = shifted(x, amount)
        dst[index, allc : 2 * allc, :] = x
        dst[index, 2 * allc : 3 * allc, :] = shifted(x, -amount)

    first_row = 5
    turn4 = swap_matrix(HALO, chans)
    own, oth = mm(turn4, out_own_ref[...]), mm(turn4, out_oth_ref[...])
    start = jnp.where(core == 0, first_row - HALO, first_row + rows)
    for r in range(HALO):
        at = slice(r * chans, (r + 1) * chans)
        put(xs, start + r, jnp.concatenate([own[at], oth[at]], axis=0).astype(BF), 1)
    top = own[0:1, :]
    bottom = own[(HALO - 1) * chans : (HALO - 1) * chans + 1, :]

    @pl.when(core == 0)
    def _():
        mask[pl.ds(side - 1, 1), :] = top

    @pl.when(core == 1)
    def _():
        mask[pl.ds(side + tiles_r, 1), :] = bottom

    xs[0] = jnp.zeros(xs.shape[1:], BF)
    turn = swap_matrix(BLK, BLK)
    few = HALO * BLK
    row, col = iota((few, BLK * BLK), 0), iota((few, BLK * BLK), 1)
    turn_mid = ones_where(
        (row % BLK == col // BLK) & (row // BLK + (BLK - HALO) * core == col % BLK)
    )
    mid_start = jnp.where(core == 0, first_row + rows, first_row - HALO)
    for m in range(main + 1):
        for copy in copies[2 * m : 2 * m + 2]:
            copy.wait()
        parts = []
        for n in range(2):
            for ch in range(0, chans, BLK):
                block = feat[n, m, ch : ch + BLK].reshape(BLK * BLK, cols)
                parts.append(mm(turn_mid if m == main else turn, block).astype(BF))
        at = mid_start if m == main else first_row + m * BLK
        for r in range(HALO if m == main else BLK):
            x = jnp.concatenate([p[r * BLK : (r + 1) * BLK] for p in parts], axis=0)
            put(xs, at + r, x, 1)

    base = side + core * (rows // side)
    total_steps = rows // side + 1
    tiles = 3 if total_steps % 3 == 0 else 1
    group = tiles * side

    def lines(step, ahead):
        return [mask[pl.ds(base + step * tiles + k - 1, 1), :] for k in range(tiles + ahead)]

    pa_ref[...] = jnp.zeros(pa_ref.shape, F32)
    pb_ref[...] = jnp.zeros(pb_ref.shape, F32)

    def first(step, carry):
        pa, pb = pa_ref[0], pb_ref[0]
        flag = lines(step, 1)
        for j in range(group):
            q = step * group + j
            y = mm(w1[...], xs[q])
            total = pa + y[2 * allc :]
            pa = pb + y[allc : 2 * allc]
            pb = y[:allc]
            h = jnp.maximum(total * flag[(j + 2) // side], 0.0)
            put(hs, q, h.astype(BF), 2)
        pa_ref[0] = pa
        pb_ref[0] = pb
        return carry

    lax.fori_loop(0, total_steps // tiles, first, 0)

    pa_ref[0] = jnp.zeros((allc, cols), F32)
    pb_ref[0] = jnp.zeros((allc, cols), F32)
    half = cols // 2
    lane = iota((cols, cols), 1)
    pick = ones_where(iota((cols, cols), 0) == 2 * (lane % half) + lane // half)

    def out_copy(tile):
        at = pl.multiple_of(tile * side, side)
        return pltpu.make_async_copy(
            es.at[pl.ds(at + side, side)], es_hbm.at[pl.ds(at, side)], out_sem
        )

    def second(step, carry):
        pa, pb = [pa_ref[0], pa_ref[1]], [pb_ref[0], pb_ref[1]]
        flag = lines(step, 0)
        for t in range(tiles):
            rows_e = []
            for j in range(t * side, (t + 1) * side):
                q = step * group + j
                i = j % 2
                z = mm(w2[...], hs[q])
                total = pa[i] + z[2 * allc :]
                pa[i] = pb[i] + z[allc : 2 * allc]
                pb[i] = z[:allc]
                x = xs[jnp.maximum(q - 3, 0), allc : 2 * allc, :].astype(F32)
                e = (flag[t] * (x + total)).astype(BF)
                es[q] = e
                rows_e.append(e)
            tile = jnp.maximum(step * tiles + t - 1, 0)
            s = mm(jnp.concatenate(rows_e, axis=0), pick).astype(BF)
            pairs = []
            for k in range(side // 2):
                sp = s[k * 2 * allc : (k + 1) * 2 * allc]
                pairs.append(jnp.concatenate([sp[:, :half], sp[:, half:]], axis=0))
            for k in range(0, side // 2, 2):
                both = mm(wm[...], jnp.concatenate(pairs[k : k + 2], axis=1)).astype(BF)
                for n in range(2):
                    u = (side // 2) * (tile % 2) + k + n
                    at_u = pl.ds(pl.multiple_of(u * chans, chans), chans)
                    at_g = pl.ds(pl.multiple_of((tile // 2) * half, half), half)
                    piece = both[:, n * half : (n + 1) * half]
                    mown_ref[at_u, at_g] = piece[:chans]
                    moth_ref[at_u, at_g] = piece[chans:]
        for i in range(2):
            pa_ref[i] = pa[i]
            pb_ref[i] = pb[i]
        return carry

    lax.fori_loop(0, total_steps // tiles, second, 0)
    whole = pltpu.make_async_copy(es.at[pl.ds(side, rows)], es_hbm, out_sem)
    whole.start()
    whole.wait()


def restore_kernel(place_ref, es_ref, enh_hbm, eoth_ref, own, sem):
    core = place_ref[0]
    rows, allc, cols = es_ref.shape
    chans = allc // 2
    turn = swap_matrix(BLK, BLK)
    for c0 in list(range(chans, allc, BLK)) + list(range(0, chans, BLK)):
        ref = own if c0 < chans else eoth_ref
        ch = c0 % chans
        for at in range(0, rows, BLK):
            block = es_ref[at : at + BLK, c0 : c0 + BLK, :].reshape(BLK * BLK, cols)
            ref[ch : ch + BLK, at : at + BLK, :] = mm(turn, block).astype(BF).reshape(BLK, BLK, cols)
    copy = pltpu.make_async_copy(
        own, enh_hbm.at[:, pl.ds(pl.multiple_of(core * rows, rows), rows), :], sem
    )
    copy.start()
    copy.wait()


def fill_kernel(place_ref, recv_ref, held_hbm, enh_hbm, sem):
    core = place_ref[0]
    rows = recv_ref.shape[1]
    copy = pltpu.make_async_copy(
        recv_ref, enh_hbm.at[:, pl.ds(pl.multiple_of((1 - core) * rows, rows), rows), :], sem
    )
    copy.start()
    copy.wait()


def pack_kernel(side, slots, place_ref, owner_ref, mown_ref, mrecv_ref, out_ref, code_ref):
    core, turn = place_ref[0], place_ref[1]
    count = owner_ref.shape[1]
    rows, width = mown_ref.shape
    blocks, all_rows, lanes = out_ref.shape
    per = side * slots
    row = jnp.broadcast_to(owner_ref[...].astype(F32), (lanes, count))
    owner = jnp.transpose(row).astype(jnp.int32)
    is_owner = owner == iota((count, lanes), 1)
    lower = ones_where(iota((count, count), 0) > iota((count, count), 1))
    earlier = mm(lower, ones_where(is_owner))
    within = jnp.sum(jnp.where(is_owner, earlier, 0.0), axis=1, keepdims=True)
    code = (owner * per).astype(F32) + within
    wide = jnp.broadcast_to(code[:, None, :], (count, side, lanes))
    step_v = ((iota((count, side, lanes), 1) + turn) % side * slots).astype(F32)
    code_ref[...] = (wide + step_v).reshape(count * side, lanes).astype(jnp.int32)
    own_at = pl.multiple_of(core * width, width)
    oth_at = pl.multiple_of((1 - core) * width, width)
    data = jnp.concatenate([mown_ref[...], mrecv_ref[...]], axis=1)
    codes = jnp.concatenate(
        [code_ref[pl.ds(own_at, width), :], code_ref[pl.ds(oth_at, width), :]], axis=0
    )
    code_ref[...] = codes
    lane = iota((2 * width, lanes), 1)
    for step in range(0, blocks, 2):
        codes = code_ref[...]
        spots = [ones_where(codes == lane + at * lanes) for at in (step, step + 1)]
        total = mm(data, jnp.concatenate(spots, axis=1)).astype(BF)
        for n in range(2):
            at = step + n
            out_ref[at, 0:rows, :] = total[:, n * lanes : (n + 1) * lanes]
            goal = (iota((count, lanes), 1) + at * lanes) // per
            tally = mm(jnp.ones((all_rows - rows, count), BF), ones_where(owner == goal))
            out_ref[at, rows:all_rows, :] = tally.astype(BF)


def places(tallies, room, lanes, group, slots):
    lane0, lane1 = iota((lanes, lanes), 0), iota((lanes, lanes), 1)
    heads = lane0 % group == 0
    before = ones_where(heads & (lane0 // group < lane1 // group))
    every = ones_where(heads)
    slot = (iota((room, lanes), 1) % slots).astype(F32)
    goal = iota((room, lanes), 0).astype(F32)
    running = jnp.zeros((1, lanes), F32)
    outs = []
    for tally in tallies:
        inside, whole = mm(tally, before)[0:1], mm(tally, every)[0:1]
        live = slot < jnp.broadcast_to(tally.astype(F32)[0:1], (room, lanes))
        outs.append(jnp.where(live & (goal == running + inside + slot), 1.0, 0.0))
        running = running + whole
    return outs


def unpack_kernel(side, slots, got_ref, out_ref, picked):
    blocks, all_rows, lanes = got_ref.shape
    chans, cells, cap = out_ref.shape
    rows = side * chans
    per = side * slots
    room = picked.shape[2]
    if per == lanes:
        halves = blocks // side
        group = iota((all_rows - rows, lanes), 1) // slots
        tallies = []
        for h in range(halves):
            tally = got_ref[h * side, rows:all_rows, :].astype(F32)
            for s in range(1, side):
                other = got_ref[h * side + s, rows:all_rows, :].astype(F32)
                tally = jnp.where(group == s, other, tally)
            tallies.append(tally.astype(BF))
        spots = places(tallies, room, lanes, slots, slots)
        lane = iota((rows, lanes), 1) // slots
        data = []
        for h in range(halves):
            now = [got_ref[h * side + s, 0:rows, :] for s in range(side)]
            bit = 1
            while bit < side:
                odd = lane // bit % 2 == 1
                now = [jnp.where(odd, now[(j + bit) % side], now[j]) for j in range(side)]
                bit *= 2
            data.append(now)
        for v in range(side):
            lhs = jnp.concatenate([data[h][-v % side] for h in range(halves)], axis=1)
            rhs = [pltpu.roll(s, v * slots, 1) if v else s for s in spots]
            picked[v] = mm_nt(lhs, jnp.concatenate(rhs, axis=1).astype(BF)).astype(BF)
    else:
        tallies = [got_ref[b, rows:all_rows, :] for b in range(blocks)]
        spots = jnp.concatenate(places(tallies, room, lanes, per, slots), axis=1).astype(BF)
        for v in range(side):
            keep = iota((rows, lanes), 1) % per // slots == v
            lhs = jnp.concatenate(
                [jnp.where(keep, got_ref[b, 0:rows, :], jnp.zeros((rows, lanes), BF)) for b in range(blocks)],
                axis=1,
            )
            picked[v] = mm_nt(lhs, spots).astype(BF)
    two = BLK // side
    n = BLK * BLK
    row, col = iota((n, n), 0), iota((n, n), 1)
    turn = ones_where(
        (row // BLK == col % BLK)
        & (row // side % two == col // BLK % two)
        & (row % side == col // (BLK * two))
    )
    for u in range(0, side, two):
        for ch in range(0, chans, BLK):
            block = jnp.concatenate(
                [
                    picked[v, (u + w) * chans + ch : (u + w) * chans + ch + BLK, :]
                    for v in range(side)
                    for w in range(two)
                ],
                axis=0,
            )
            done = mm(turn, block).astype(BF).reshape(BLK, BLK, room)
            out_ref[ch : ch + BLK, u * side : (u + two) * side, :] = done[:, :, :cap]


def on_device(features, tile_valid, parent_owner, w_first, w_second, w_merge):
    chans, row_count, col_count = features.shape
    tile_rows, tile_cols = tile_valid.shape
    side = row_count // tile_rows
    parents_dev = parent_owner.shape[0]
    devices = lax.axis_size("tiles")
    slots = 2 * max(1, parents_dev // devices)
    own_cap = 3 * parents_dev // 2
    rows = row_count // 2
    allc = 2 * chans
    lanes = 128
    blocks = devices * slots * side // lanes
    fold = devices // blocks
    core = lax.axis_index("chan")
    turn = lax.axis_index("tiles") % side if fold == 1 else jnp.zeros_like(core)
    place = jnp.stack([core, turn]).astype(jnp.int32)
    swap = [(0, 1), (1, 0)]
    vmem = pl.BlockSpec(memory_space=pltpu.VMEM)
    smem = pl.BlockSpec(memory_space=pltpu.SMEM)
    hbm = pl.BlockSpec(memory_space=pl.ANY)

    def limit(mib):
        return pltpu.CompilerParams(vmem_limit_bytes=mib << 20)

    flat = chans * HALO
    feat_oth = lax.ppermute(features, "chan", swap)
    w_own = jnp.concatenate([w_first, w_second, jnp.swapaxes(w_merge, 1, 2)], axis=0)
    w_oth = lax.ppermute(w_own, "chan", swap)
    edge_one, edge_two = pl.pallas_call(
        functools.partial(edges_kernel, side),
        out_shape=(jax.ShapeDtypeStruct((flat, col_count), BF),) * 2,
        in_specs=[smem, hbm, vmem],
        out_specs=(vmem,) * 2,
        scratch_shapes=[
            pltpu.VMEM((2, chans, BLK, col_count), BF),
            pltpu.SemaphoreType.DMA((2,)),
        ],
        compiler_params=limit(6),
        name="edges",
    )(place, features, tile_valid)
    down_up = [(2 * t, 2 * t + 2) for t in range(devices - 1)]
    down_up += [(2 * t + 1, 2 * t - 1) for t in range(1, devices)]
    cross = [(2 * t + 1, 2 * t + 2) for t in range(devices - 1)]
    cross += [(2 * t, 2 * t - 1) for t in range(1, devices)]
    out_own = lax.ppermute(edge_one, ("tiles", "chan"), down_up)
    out_oth = lax.ppermute(edge_two, ("tiles", "chan"), cross)
    w1, w2, wm = pl.pallas_call(
        weights_kernel,
        out_shape=(
            jax.ShapeDtypeStruct((3 * allc, 3 * allc), BF),
            jax.ShapeDtypeStruct((3 * allc, 3 * allc), BF),
            jax.ShapeDtypeStruct((allc, 4 * allc), BF),
        ),
        in_specs=[smem, vmem, vmem],
        out_specs=(vmem,) * 3,
        compiler_params=limit(6),
        name="weights",
    )(place, w_own, w_oth)

    width = parents_dev * side // 2
    es, m_own, m_oth = pl.pallas_call(
        functools.partial(conv_kernel, side),
        out_shape=(
            jax.ShapeDtypeStruct((rows, allc, col_count), BF),
            jax.ShapeDtypeStruct((side * chans, width), BF),
            jax.ShapeDtypeStruct((side * chans, width), BF),
        ),
        in_specs=[smem, hbm, hbm] + [vmem] * 6,
        out_specs=(hbm, vmem, vmem),
        scratch_shapes=[
            pltpu.VMEM((2, rows // BLK + 1, chans, BLK, col_count), BF),
            pltpu.VMEM((rows + 16, 3 * allc, col_count), BF),
            pltpu.VMEM((rows + side, 3 * allc, col_count), BF),
            pltpu.VMEM((rows + side, allc, col_count), BF),
            pltpu.VMEM((tile_rows + 2 * side, col_count), F32),
            pltpu.VMEM((2, allc, col_count), F32),
            pltpu.VMEM((2, allc, col_count), F32),
            pltpu.SemaphoreType.DMA((2, rows // BLK + 1)),
            pltpu.SemaphoreType.DMA,
        ],
        compiler_params=limit(36),
        name="conv",
    )(place, features, feat_oth, out_own, out_oth, tile_valid, w1, w2, wm)

    m_recv = lax.ppermute(m_oth, "chan", swap)
    all_rows = side * chans + 8
    packed = pl.pallas_call(
        functools.partial(pack_kernel, side, slots),
        out_shape=jax.ShapeDtypeStruct((blocks, all_rows, lanes), BF),
        in_specs=[smem, vmem, vmem, vmem],
        out_specs=vmem,
        scratch_shapes=[pltpu.VMEM((parents_dev * side, lanes), jnp.int32)],
        compiler_params=limit(16),
        name="pack",
    )(place, parent_owner[None, :], m_own, m_recv)

    def to_peers(x):
        if fold > 1:
            x = x.reshape(blocks, all_rows, fold, lanes // fold)
            x = x.transpose(0, 2, 1, 3).reshape(devices, all_rows, lanes // fold)
        x = lax.all_to_all(x, "tiles", split_axis=0, concat_axis=0, tiled=True)
        if fold > 1:
            x = x.reshape(blocks, fold, all_rows, lanes // fold)
            x = x.transpose(0, 2, 1, 3).reshape(blocks, all_rows, lanes)
        return x

    es, packed = lax.optimization_barrier((es, packed))
    got = to_peers(packed)
    held, e_oth = pl.pallas_call(
        restore_kernel,
        out_shape=(
            jax.ShapeDtypeStruct((chans, row_count, col_count), BF),
            jax.ShapeDtypeStruct((chans, rows, col_count), BF),
        ),
        in_specs=[smem, vmem],
        out_specs=(hbm, vmem),
        scratch_shapes=[pltpu.VMEM((chans, rows, col_count), BF), pltpu.SemaphoreType.DMA],
        compiler_params=limit(12),
        name="restore",
    )(place, es)
    e_recv = lax.ppermute(e_oth, "chan", swap)
    enhanced = pl.pallas_call(
        fill_kernel,
        out_shape=jax.ShapeDtypeStruct((chans, row_count, col_count), BF),
        in_specs=[smem, vmem, hbm],
        out_specs=hbm,
        scratch_shapes=[pltpu.SemaphoreType.DMA],
        input_output_aliases={2: 0},
        compiler_params=limit(6),
        name="fill",
    )(place, e_recv, held)
    room = pl.cdiv(own_cap, lanes) * lanes
    parents = pl.pallas_call(
        functools.partial(unpack_kernel, side, slots),
        out_shape=jax.ShapeDtypeStruct((chans, side * side, own_cap), BF),
        in_specs=[vmem],
        out_specs=vmem,
        scratch_shapes=[pltpu.VMEM((side, side * chans, room), BF)],
        compiler_params=limit(24),
        name="unpack",
    )(got)
    return enhanced, jnp.swapaxes(parents, 1, 2)


def solution(mesh):
    return jax.shard_map(
        on_device,
        mesh=mesh,
        in_specs=(
            P("chan", "tiles", None),
            P("tiles", None),
            P("tiles"),
            P(None, "chan", None),
            P(None, "chan", None),
            P(None, None, "chan"),
        ),
        out_specs=(P("chan", "tiles", None), P("chan", "tiles", None)),
        check_vma=False,
    )
```

```python
import functools

import jax
import jax.numpy as jnp
from jax import lax
from jax.experimental import pallas as pl
from jax.experimental.pallas import tpu as pltpu
from jax.sharding import PartitionSpec as P

BF = jnp.bfloat16
F32 = jnp.float32
HALO = 4
BLK = 16


def iota(shape, dim):
    return lax.broadcasted_iota(jnp.int32, shape, dim)


def div(x, n):
    return x >> (n.bit_length() - 1) if n & (n - 1) == 0 else lax.div(x, jnp.int32(n))


def mod(x, n):
    return x & (n - 1) if n & (n - 1) == 0 else lax.rem(x, jnp.int32(n))


def ones_where(cond):
    return jnp.where(cond, 1.0, 0.0).astype(BF)


def mm(a, b):
    return jnp.dot(a, b, preferred_element_type=F32)


def mm_nt(a, b):
    return lax.dot_general(a, b, (((1,), (1,)), ((), ())), preferred_element_type=F32)


def swap_matrix(outer, inner):
    n = outer * inner
    row, col = iota((n, n), 0), iota((n, n), 1)
    return ones_where((mod(row, inner) == div(col, outer)) & (div(row, inner) == mod(col, outer)))


def shifted(x, amount):
    lanes = 128
    parts = [x[:, at : at + lanes] for at in range(0, x.shape[1], lanes)]
    turned = [pltpu.roll(p, amount % lanes, 1) for p in parts]
    lane = iota(parts[0].shape, 1)
    zero = jnp.zeros_like(parts[0])
    outs = []
    for n in range(len(parts)):
        if amount > 0:
            edge = turned[n - 1] if n else zero
            outs.append(jnp.where(lane < amount, edge, turned[n]))
        else:
            edge = turned[n + 1] if n + 1 < len(parts) else zero
            outs.append(jnp.where(lane >= lanes + amount, edge, turned[n]))
    return jnp.concatenate(outs, axis=1)


def widen_matrix(tiles_c, cols, side):
    return ones_where(div(iota((tiles_c, cols), 1), side) == iota((tiles_c, cols), 0))


def as_bf(x):
    return x.astype(F32).astype(BF)


def edges_kernel(
    side, place_ref, head_ref, tail_ref, valid_ref, wa_ref, wb_ref, wc_ref, send_ref, keep_ref
):
    core = place_ref[0]
    chans, _, cols = head_ref.shape
    flat = chans * HALO
    lanes = send_ref.shape[1]
    at = flat * cols // lanes
    for ref in (wa_ref, wb_ref, wc_ref):
        taps, outs, ins = ref.shape
        body = ref[...].reshape(taps * outs, ins)
        send_ref[at : at + taps * outs, :] = jnp.concatenate(
            [body, jnp.zeros((taps * outs, lanes - ins), BF)], axis=1
        )
        at += taps * outs
    tiles_r, tiles_c = valid_ref.shape
    masks = mm(as_bf(valid_ref[...]), widen_matrix(tiles_c, cols, side))
    row, col = iota((flat, chans * BLK), 0), iota((flat, chans * BLK), 1)
    same = div(row, HALO) == div(col, BLK)
    spot = mod(iota((flat, cols), 0), HALO)
    made = []
    for n, ref in enumerate((head_ref, tail_ref)):
        if n == 0:
            hit = same & (mod(row, HALO) == mod(col, BLK)) & (mod(row, HALO) < HALO - 1)
            flag, line = spot == HALO - 1, masks[0:1]
        else:
            hit = same & (mod(row, HALO) + BLK - HALO == mod(col, BLK)) & (mod(row, HALO) > 0)
            flag, line = spot == 0, masks[tiles_r - 1 : tiles_r]
        take = ones_where(hit)
        body = mm(take, ref[...].reshape(chans * BLK, cols))
        made.append(jnp.where(flag, jnp.broadcast_to(line, (flat, cols)), body).astype(BF))
    low = core == 0
    send = jnp.where(low, made[1], made[0])
    keep = jnp.where(low, made[0], made[1])
    for n in range(cols // lanes):
        send_ref[n * flat : (n + 1) * flat, :] = send[:, n * lanes : (n + 1) * lanes]
        keep_ref[n * flat : (n + 1) * flat, :] = keep[:, n * lanes : (n + 1) * lanes]


def weights_kernel(at, chans, place_ref, own_ref, oth_ref, w1_ref, w2_ref, wm_ref):
    core = place_ref[0]
    allc = 2 * chans

    def tap(k):
        return [ref[at + k * chans : at + (k + 1) * chans, 0:allc] for ref in (own_ref, oth_ref)]

    for dst, base in ((w1_ref, 0), (w2_ref, 9)):
        total = None
        for b in range(3):
            tall = jnp.concatenate(sum([tap(base + 3 * a + b) for a in range(3)], []), axis=0)
            src, pos = iota((allc, 3 * allc), 0), iota((allc, 3 * allc), 1)
            place = ones_where(pos == b * allc + mod(src + chans * core, allc))
            part = mm(tall, place)
            total = part if total is None else total + part
        dst[...] = total.astype(BF)
    tall = jnp.concatenate(
        sum([tap(18 + 2 * a + b) for b in range(2) for a in range(2)], []), axis=0
    )
    order = ones_where(iota((allc, allc), 1) == mod(iota((allc, allc), 0) + chans * core, allc))
    wm_ref[...] = mm_nt(order, tall).astype(BF)


def conv_kernel(
    side,
    place_ref,
    own_hbm,
    oth_hbm,
    outer_ref,
    valid_ref,
    w1,
    w2,
    wm,
    es_hbm,
    mown_ref,
    moth_ref,
    feat,
    xs,
    hs,
    es_ref,
    mask,
    pa_ref,
    pb_ref,
    in_sems,
    out_sem,
):
    core = place_ref[0]
    rows, allc, cols = es_ref.shape
    chans = allc // 2
    main = rows // BLK
    copies = []
    for m in range(main + 1):
        at = rows - BLK * core if m == main else rows * core + BLK * m
        for n, ref in enumerate((own_hbm, oth_hbm)):
            copy = pltpu.make_async_copy(
                ref.at[:, pl.ds(pl.multiple_of(at, BLK), BLK), :], feat.at[n, m], in_sems.at[n, m]
            )
            copy.start()
            copies.append(copy)
    lanes = outer_ref.shape[1]

    tiles_r, tiles_c = valid_ref.shape
    mask[pl.ds(side, tiles_r), :] = mm(as_bf(valid_ref[...]), widen_matrix(tiles_c, cols, side))

    def put(dst, index, x, amount):
        dst[index, 0:allc, :] = shifted(x, amount).astype(BF)
        dst[index, allc : 2 * allc, :] = x.astype(BF)
        dst[index, 2 * allc : 3 * allc, :] = shifted(x, -amount).astype(BF)

    first_row = 5
    turn4 = swap_matrix(HALO, chans)
    flat = HALO * chans
    pieces = [outer_ref[k * flat : (k + 1) * flat, :] for k in range(2 * cols // lanes)]
    oth, own = [
        mm(turn4, jnp.concatenate(pieces[n * cols // lanes : (n + 1) * cols // lanes], axis=1))
        for n in range(2)
    ]
    start = jnp.where(core == 0, first_row - HALO, first_row + rows)
    for r in range(HALO):
        at = slice(r * chans, (r + 1) * chans)
        put(xs, start + r, jnp.concatenate([own[at], oth[at]], axis=0), 1)
    top = own[0:1, :]
    bottom = own[(HALO - 1) * chans : (HALO - 1) * chans + 1, :]

    @pl.when(core == 0)
    def _():
        mask[pl.ds(side - 1, 1), :] = top

    @pl.when(core == 1)
    def _():
        mask[pl.ds(side + tiles_r, 1), :] = bottom

    xs[0] = jnp.zeros(xs.shape[1:], BF)
    turn = swap_matrix(BLK, BLK)
    few = HALO * BLK
    row, col = iota((few, BLK * BLK), 0), iota((few, BLK * BLK), 1)
    turn_mid = ones_where(
        (mod(row, BLK) == div(col, BLK)) & (div(row, BLK) + (BLK - HALO) * core == mod(col, BLK))
    )
    mid_start = jnp.where(core == 0, first_row + rows, first_row - HALO)
    for m in range(main + 1):
        for copy in copies[2 * m : 2 * m + 2]:
            copy.wait()
        parts = []
        for n in range(2):
            for ch in range(0, chans, BLK):
                block = feat[n, m, ch : ch + BLK].reshape(BLK * BLK, cols)
                parts.append(mm(turn_mid if m == main else turn, block))
        at = mid_start if m == main else first_row + m * BLK
        for r in range(HALO if m == main else BLK):
            x = jnp.concatenate([p[r * BLK : (r + 1) * BLK] for p in parts], axis=0)
            put(xs, at + r, x, 1)

    base = side + core * (rows // side)
    total_steps = rows // side + 1
    tiles = 3 if total_steps % 3 == 0 else 1
    group = tiles * side

    def lines(step, ahead):
        return [mask[pl.ds(base + step * tiles + k - 1, 1), :] for k in range(tiles + ahead)]

    pa_ref[...] = jnp.zeros(pa_ref.shape, F32)
    pb_ref[...] = jnp.zeros(pb_ref.shape, F32)

    def first(step, carry):
        pa, pb = pa_ref[0], pb_ref[0]
        flag = lines(step, 1)
        for j in range(group):
            q = step * group + j
            y = mm(w1[...], xs[q])
            total = pa + y[2 * allc :]
            pa = pb + y[allc : 2 * allc]
            pb = y[:allc]
            h = jnp.maximum(total * flag[(j + 2) // side], 0.0)
            put(hs, q, h.astype(BF), 2)
        pa_ref[0] = pa
        pb_ref[0] = pb
        return carry

    lax.fori_loop(0, total_steps // tiles, first, 0)

    pa_ref[0] = jnp.zeros((allc, cols), F32)
    pb_ref[0] = jnp.zeros((allc, cols), F32)

    def second(step, carry):
        pa, pb = [pa_ref[0], pa_ref[1]], [pb_ref[0], pb_ref[1]]
        flag = lines(step, 0)
        for j in range(group):
            q = step * group + j
            i = j % 2
            z = mm(w2[...], hs[q])
            total = pa[i] + z[2 * allc :]
            pa[i] = pb[i] + z[allc : 2 * allc]
            pb[i] = z[:allc]
            x = xs[jnp.maximum(q - 3, 0), allc : 2 * allc, :].astype(F32)
            es_ref[jnp.maximum(q - side, 0)] = (flag[j // side] * (x + total)).astype(BF)
        for i in range(2):
            pa_ref[i] = pa[i]
            pb_ref[i] = pb[i]
        return carry

    lax.fori_loop(0, total_steps // tiles, second, 0)

    out = pltpu.make_async_copy(es_ref, es_hbm, out_sem)
    out.start()

    half = cols // 2
    wide = half // side
    lane = iota((cols, cols), 1)
    spot = mod(lane, half)
    want = 2 * (mod(spot, wide) * side + div(spot, wide)) + div(lane, half)
    pick = ones_where(iota((cols, cols), 0) == want)
    picked = hs.reshape(hs.shape[0] * hs.shape[1], cols)
    for tile in range(rows // side):
        tall = es_ref[tile * side : (tile + 1) * side].reshape(side * allc, cols)
        picked[tile * side * allc : (tile + 1) * side * allc, :] = mm(tall, pick).astype(BF)
    for tile in range(rows // side):
        g = tile // 2 + core * (rows // (2 * side))
        for k in range(0, side // 2, 2):
            pairs = []
            for n in range(2):
                at = (tile * side + 2 * (k + n)) * allc
                sp = picked[at : at + 2 * allc, :]
                pairs.append(jnp.concatenate([sp[:, :half], sp[:, half:]], axis=0))
            both = mm(wm[...], jnp.concatenate(pairs, axis=1))
            for n in range(2):
                u = (side // 2) * (tile % 2) + k + n
                piece = pltpu.roll(both[:, n * half : (n + 1) * half], g * wide, 1).astype(BF)
                mown_ref[tile // 2, u * chans : (u + 1) * chans, :] = piece[:chans]
                moth_ref[tile // 2, u * chans : (u + 1) * chans, :] = piece[chans:]
    out.wait()


def restore_kernel(place_ref, es_ref, after_hbm, enh_hbm, eoth_ref, own, sem):
    core = place_ref[0]
    rows, allc, cols = es_ref.shape
    chans = allc // 2
    turn = swap_matrix(BLK, BLK)
    for c0 in list(range(chans, allc, BLK)) + list(range(0, chans, BLK)):
        ref = own if c0 < chans else eoth_ref
        ch = c0 % chans
        for at in range(0, rows, BLK):
            block = es_ref[at : at + BLK, c0 : c0 + BLK, :].reshape(BLK * BLK, cols)
            ref[ch : ch + BLK, at : at + BLK, :] = mm(turn, block).astype(BF).reshape(BLK, BLK, cols)
    copy = pltpu.make_async_copy(
        own, enh_hbm.at[:, pl.ds(pl.multiple_of(core * rows, rows), rows), :], sem
    )
    copy.start()
    copy.wait()


def fill_kernel(place_ref, recv_ref, held_hbm, enh_hbm, sem):
    core = place_ref[0]
    rows = recv_ref.shape[1]
    copy = pltpu.make_async_copy(
        recv_ref, enh_hbm.at[:, pl.ds(pl.multiple_of((1 - core) * rows, rows), rows), :], sem
    )
    copy.start()
    copy.wait()


def deal(now, width):
    n = len(now)
    group = div(iota(now[0].shape, 1), width)
    bit = 1
    while bit < n:
        odd = group & bit != 0
        now = [jnp.where(odd, now[(j + bit) % n], now[j]) for j in range(n)]
        bit *= 2
    return now


def pack_kernel(
    side, slots, place_ref, owner_ref, mown_ref, mrecv_ref, out_ref, arr, lhs, mid, code_ref
):
    core, tile = place_ref[0], place_ref[1]
    count = owner_ref.shape[1]
    mine, rows, lanes = mown_ref.shape
    blocks, all_rows, _ = out_ref.shape
    per = side * slots
    wide = lanes // side
    for k in range(mine):
        arr[core * mine + k] = mown_ref[k]
        arr[(1 - core) * mine + k] = mrecv_ref[k]
    line = jnp.broadcast_to(owner_ref[...].astype(F32), (lanes, count))
    owner = jnp.transpose(line).astype(jnp.int32)
    is_owner = owner == iota((count, lanes), 1)
    marks = ones_where(is_owner)
    lower = ones_where(iota((count, count), 0) > iota((count, count), 1))
    earlier = mm(lower, marks)
    within = jnp.sum(jnp.where(is_owner, earlier, 0.0), axis=1, keepdims=True).astype(jnp.int32)
    if per == lanes:
        code = (owner * slots + within).astype(F32).astype(BF)
        code_ref[0:count, :] = code
        code_ref[count : 2 * count, :] = code

        def by_column(step, carry):
            at = pl.ds(pl.multiple_of(step * BLK, BLK), BLK)
            done = deal([arr[g, at, :] for g in range(side)], wide)
            for j in range(side):
                lhs[-j % side, at, :] = done[j]
            return carry

        lax.fori_loop(0, rows // BLK, by_column, 0, unroll=4)
        halves = blocks // side
        lane = iota((1, halves * lanes), 1)
        block, group, slot = div(lane, lanes), div(mod(lane, lanes), wide), mod(lane, wide)
        for i in range(side):
            v = lax.rem(i + side - lax.rem(tile, side), side)
            at = pl.multiple_of(count - wide * v, wide)
            codes = code_ref[pl.ds(at, count), :]
            want = (block * side + mod(group - i + side, side)) * slots + slot
            want = jnp.broadcast_to(want.astype(F32).astype(BF), (count, halves * lanes))
            same = jnp.concatenate([codes] * halves, axis=1) == want
            take = jnp.where(same, jnp.ones_like(want), jnp.zeros_like(want))
            got = mm(lhs[v], take).astype(BF)
            for h in range(halves):
                mid[h * side + i] = got[:, h * lanes : (h + 1) * lanes]
        for h in range(halves):

            def by_owner(step, carry, h=h):
                at = pl.ds(pl.multiple_of(step * BLK, BLK), BLK)
                done = deal([mid[h * side + i, at, :] for i in range(side)], wide)
                for j in range(side):
                    out_ref[h * side + -j % side, at, :] = done[j]
                return carry

            lax.fori_loop(0, rows // BLK, by_owner, 0, unroll=4)
        tally = mm(jnp.ones((all_rows - rows, count), BF), marks)
        for d in range(blocks):
            out_ref[d, rows:all_rows, :] = jnp.broadcast_to(
                tally[:, d : d + 1], (all_rows - rows, lanes)
            ).astype(BF)
    else:
        code = owner * per + within
        lane = iota((wide, lanes), 1)
        for g in range(2 * mine):
            for x in range(side):
                at = (g * side + x) * wide
                code_ref[at : at + wide, :] = (
                    code[g * wide : (g + 1) * wide] + (x - g) % side * slots
                )
        data = jnp.concatenate([arr[g] for g in range(2 * mine)], axis=1)
        lane = iota((count * side, lanes), 1)
        for step in range(0, blocks, 2):
            codes = code_ref[...]
            spots = [ones_where(codes == lane + at * lanes) for at in (step, step + 1)]
            total = mm(data, jnp.concatenate(spots, axis=1)).astype(BF)
            for n in range(2):
                at = step + n
                out_ref[at, 0:rows, :] = total[:, n * lanes : (n + 1) * lanes]
                goal = div(iota((count, lanes), 1) + at * lanes, per)
                tally = mm(jnp.ones((all_rows - rows, count), BF), ones_where(owner == goal))
                out_ref[at, rows:all_rows, :] = tally.astype(BF)


def targets(tallies, lanes, group, slots):
    lane0, lane1 = iota((lanes, lanes), 0), iota((lanes, lanes), 1)
    heads = mod(lane0, group) == 0
    before = ones_where(heads & (div(lane0, group) < div(lane1, group)))
    every = ones_where(heads)
    slot = mod(iota((1, lanes), 1), slots).astype(F32)
    running = jnp.zeros((1, lanes), F32)
    outs = []
    for tally in tallies:
        inside, whole = mm(tally, before)[0:1], mm(tally, every)[0:1]
        live = slot < tally.astype(F32)[0:1]
        outs.append(jnp.where(live, running + inside + slot, -1.0))
        running = running + whole
    return outs


def hits(target, room):
    shape = (room, target.shape[1])
    goal = iota(shape, 0).astype(F32).astype(BF)
    same = goal == jnp.broadcast_to(target.astype(BF), shape)
    return jnp.where(same, jnp.ones_like(goal), jnp.zeros_like(goal))


def unpack_kernel(side, slots, place_ref, got_ref, out_ref, picked, data):
    tile = place_ref[1]
    blocks, all_rows, lanes = got_ref.shape
    chans, cells, cap = out_ref.shape
    rows = side * chans
    per = side * slots
    room = picked.shape[2]
    if per == lanes:
        halves = blocks // side
        group = div(iota((all_rows - rows, lanes), 1), slots)
        tallies = []
        for h in range(halves):
            tally = got_ref[h * side, rows:all_rows, :].astype(F32)
            for s in range(1, side):
                other = got_ref[h * side + s, rows:all_rows, :].astype(F32)
                tally = jnp.where(group == s, other, tally)
            tallies.append(tally.astype(BF))
        spots = targets(tallies, lanes, slots, slots)
        for h in range(halves):

            def turn_rows(step, carry, h=h):
                at = pl.ds(pl.multiple_of(step * BLK, BLK), BLK)
                done = deal([got_ref[h * side + s, at, :] for s in range(side)], slots)
                for j in range(side):
                    data[h, j, at, :] = done[j]
                return carry

            lax.fori_loop(0, rows // BLK, turn_rows, 0, unroll=4)
        for j in range(side):
            v = lax.rem(2 * side - j - lax.rem(tile, side), side)
            left = jnp.concatenate([data[h, j] for h in range(halves)], axis=1)
            right = []
            for spot in spots:
                line = jnp.broadcast_to(spot, (side, lanes))
                line = pltpu.roll(line, (side - j) * slots, 1) if j else line
                right.append(hits(line[0:1], room))
            picked[v] = mm_nt(left, jnp.concatenate(right, axis=1)).astype(BF)
    else:
        tallies = [got_ref[b, rows:all_rows, :] for b in range(blocks)]
        spots = [hits(t, room) for t in targets(tallies, lanes, per, slots)]
        spots = jnp.concatenate(spots, axis=1)
        for v in range(side):
            keep = div(mod(iota((rows, lanes), 1), per), slots) == v
            left = jnp.concatenate(
                [jnp.where(keep, got_ref[b, 0:rows, :], jnp.zeros((rows, lanes), BF)) for b in range(blocks)],
                axis=1,
            )
            picked[v] = mm_nt(left, spots).astype(BF)
    two = BLK // side
    n = BLK * BLK
    row, col = iota((n, n), 0), iota((n, n), 1)
    turn = ones_where(
        (div(row, BLK) == mod(col, BLK))
        & (mod(div(row, side), two) == mod(div(col, BLK), two))
        & (mod(row, side) == div(col, BLK * two))
    )
    for u in range(0, side, two):
        for ch in range(0, chans, BLK):
            block = jnp.concatenate(
                [
                    picked[v, (u + w) * chans + ch : (u + w) * chans + ch + BLK, :]
                    for v in range(side)
                    for w in range(two)
                ],
                axis=0,
            )
            done = mm(turn, block).astype(BF).reshape(BLK, BLK, room)
            out_ref[ch : ch + BLK, u * side : (u + two) * side, :] = done[:, :, :cap]


def on_device(features, tile_valid, parent_owner, w_first, w_second, w_merge):
    chans, row_count, col_count = features.shape
    tile_rows, tile_cols = tile_valid.shape
    side = row_count // tile_rows
    parents_dev = parent_owner.shape[0]
    devices = lax.axis_size("tiles")
    slots = 2 * max(1, parents_dev // devices)
    own_cap = 3 * parents_dev // 2
    rows = row_count // 2
    allc = 2 * chans
    lanes = 128
    blocks = devices * slots * side // lanes
    fold = devices // blocks
    core = lax.axis_index("chan")
    place = jnp.stack([core, lax.axis_index("tiles")]).astype(jnp.int32)
    swap = [(0, 1), (1, 0)]
    vmem = pl.BlockSpec(memory_space=pltpu.VMEM)
    smem = pl.BlockSpec(memory_space=pltpu.SMEM)
    hbm = pl.BlockSpec(memory_space=pltpu.HBM)

    def limit(mib):
        return pltpu.CompilerParams(vmem_limit_bytes=mib << 20)

    feat_oth = lax.ppermute(features, "chan", swap)
    w_mergt = jnp.swapaxes(w_merge, 1, 2)
    edge_rows = chans * HALO * col_count // lanes
    tap_rows = (w_first.shape[0] + w_second.shape[0] + w_merge.shape[0]) * chans
    send, keep = pl.pallas_call(
        functools.partial(edges_kernel, side),
        out_shape=(
            jax.ShapeDtypeStruct((edge_rows + tap_rows, lanes), BF),
            jax.ShapeDtypeStruct((edge_rows, lanes), BF),
        ),
        in_specs=[smem] + [vmem] * 6,
        out_specs=(vmem,) * 2,
        compiler_params=limit(6),
        name="edges",
    )(place, features[:, :BLK], features[:, row_count - BLK :], tile_valid, w_first, w_second, w_mergt)
    sent = lax.ppermute(send, "chan", swap)
    cross = [(2 * t + 1, 2 * t + 2) for t in range(devices - 1)]
    cross += [(2 * t, 2 * t - 1) for t in range(1, devices)]
    outer = lax.ppermute(
        jnp.concatenate([keep, sent[:edge_rows]], axis=0), ("tiles", "chan"), cross
    )
    w1, w2, wm = pl.pallas_call(
        functools.partial(weights_kernel, edge_rows, chans),
        out_shape=(
            jax.ShapeDtypeStruct((3 * allc, 3 * allc), BF),
            jax.ShapeDtypeStruct((3 * allc, 3 * allc), BF),
            jax.ShapeDtypeStruct((allc, 4 * allc), BF),
        ),
        in_specs=[smem, vmem, vmem],
        out_specs=(vmem,) * 3,
        compiler_params=limit(6),
        name="weights",
    )(place, send, sent)

    parent_rows = tile_rows // 4
    es, m_own, m_oth = pl.pallas_call(
        functools.partial(conv_kernel, side),
        out_shape=(
            jax.ShapeDtypeStruct((rows, allc, col_count), BF),
            jax.ShapeDtypeStruct((parent_rows, side * chans, col_count // 2), BF),
            jax.ShapeDtypeStruct((parent_rows, side * chans, col_count // 2), BF),
        ),
        in_specs=[smem, hbm, hbm] + [vmem] * 5,
        out_specs=(hbm, vmem, vmem),
        scratch_shapes=[
            pltpu.VMEM((2, rows // BLK + 1, chans, BLK, col_count), BF),
            pltpu.VMEM((rows + 16, 3 * allc, col_count), BF),
            pltpu.VMEM((rows + side, 3 * allc, col_count), BF),
            pltpu.VMEM((rows, allc, col_count), BF),
            pltpu.VMEM((tile_rows + 2 * side, col_count), F32),
            pltpu.VMEM((2, allc, col_count), F32),
            pltpu.VMEM((2, allc, col_count), F32),
            pltpu.SemaphoreType.DMA((2, rows // BLK + 1)),
            pltpu.SemaphoreType.DMA,
        ],
        compiler_params=limit(34),
        name="conv",
    )(place, features, feat_oth, outer, tile_valid, w1, w2, wm)

    m_recv = lax.ppermute(m_oth, "chan", swap)
    all_rows = side * chans + 8
    packed = pl.pallas_call(
        functools.partial(pack_kernel, side, slots),
        out_shape=jax.ShapeDtypeStruct((blocks, all_rows, lanes), BF),
        in_specs=[smem, vmem, vmem, vmem],
        out_specs=vmem,
        scratch_shapes=[
            pltpu.VMEM((2 * parent_rows, side * chans, lanes), BF),
            pltpu.VMEM((side, side * chans, lanes), BF),
            pltpu.VMEM((blocks, side * chans, lanes), BF),
            pltpu.VMEM((parents_dev * side, lanes), BF if fold == 1 else jnp.int32),
        ],
        compiler_params=limit(16),
        name="pack",
    )(place, parent_owner[None, :], m_own, m_recv)

    def to_peers(x):
        if fold > 1:
            x = x.reshape(blocks, all_rows, fold, lanes // fold)
            x = x.transpose(0, 2, 1, 3).reshape(devices, all_rows, lanes // fold)
        x = lax.all_to_all(x, "tiles", split_axis=0, concat_axis=0, tiled=True)
        if fold > 1:
            x = x.reshape(blocks, fold, all_rows, lanes // fold)
            x = x.transpose(0, 2, 1, 3).reshape(blocks, all_rows, lanes)
        return x

    got = to_peers(packed)
    held, e_oth = pl.pallas_call(
        restore_kernel,
        out_shape=(
            jax.ShapeDtypeStruct((chans, row_count, col_count), BF),
            jax.ShapeDtypeStruct((chans, rows, col_count), BF),
        ),
        in_specs=[smem, vmem, hbm],
        out_specs=(hbm, vmem),
        scratch_shapes=[pltpu.VMEM((chans, rows, col_count), BF), pltpu.SemaphoreType.DMA],
        compiler_params=limit(12),
        name="restore",
    )(place, es, packed)
    e_recv = lax.ppermute(e_oth, "chan", swap)
    enhanced = pl.pallas_call(
        fill_kernel,
        out_shape=jax.ShapeDtypeStruct((chans, row_count, col_count), BF),
        in_specs=[smem, vmem, hbm],
        out_specs=hbm,
        scratch_shapes=[pltpu.SemaphoreType.DMA],
        input_output_aliases={2: 0},
        compiler_params=limit(6),
        name="fill",
    )(place, e_recv, held)
    room = pl.cdiv(own_cap, lanes) * lanes
    parents = pl.pallas_call(
        functools.partial(unpack_kernel, side, slots),
        out_shape=jax.ShapeDtypeStruct((chans, side * side, own_cap), BF),
        in_specs=[smem, vmem],
        out_specs=vmem,
        scratch_shapes=[
            pltpu.VMEM((side, side * chans, room), BF),
            pltpu.VMEM((2, side, side * chans, lanes), BF),
        ],
        compiler_params=limit(24),
        name="unpack",
    )(place, got)
    return enhanced, jnp.swapaxes(parents, 1, 2)


def solution(mesh):
    return jax.shard_map(
        on_device,
        mesh=mesh,
        in_specs=(
            P("chan", "tiles", None),
            P("tiles", None),
            P("tiles"),
            P(None, "chan", None),
            P(None, "chan", None),
            P(None, None, "chan"),
        ),
        out_specs=(P("chan", "tiles", None), P("chan", "tiles", None)),
        check_vma=False,
    )
```

```python
import functools

import jax
import jax.numpy as jnp
from jax import lax
from jax.experimental import pallas as pl
from jax.experimental.pallas import tpu as pltpu
from jax.sharding import PartitionSpec as P

BF = jnp.bfloat16
F32 = jnp.float32
HALO = 4
BLK = 16


def iota(shape, dim):
    return lax.broadcasted_iota(jnp.int32, shape, dim)


def div(x, n):
    return x >> (n.bit_length() - 1) if n & (n - 1) == 0 else lax.div(x, jnp.int32(n))


def mod(x, n):
    return x & (n - 1) if n & (n - 1) == 0 else lax.rem(x, jnp.int32(n))


def ones_where(cond):
    return jnp.where(cond, 1.0, 0.0).astype(BF)


def mm(a, b):
    return jnp.dot(a, b, preferred_element_type=F32)


def mm_nt(a, b):
    return lax.dot_general(a, b, (((1,), (1,)), ((), ())), preferred_element_type=F32)


def swap_matrix(outer, inner):
    n = outer * inner
    row, col = iota((n, n), 0), iota((n, n), 1)
    return ones_where((mod(row, inner) == div(col, outer)) & (div(row, inner) == mod(col, outer)))


def shifted(x, amount):
    lanes = 128
    parts = [x[:, at : at + lanes] for at in range(0, x.shape[1], lanes)]
    turned = [pltpu.roll(p, amount % lanes, 1) for p in parts]
    lane = iota(parts[0].shape, 1)
    zero = jnp.zeros_like(parts[0])
    outs = []
    for n in range(len(parts)):
        if amount > 0:
            edge = turned[n - 1] if n else zero
            outs.append(jnp.where(lane < amount, edge, turned[n]))
        else:
            edge = turned[n + 1] if n + 1 < len(parts) else zero
            outs.append(jnp.where(lane >= lanes + amount, edge, turned[n]))
    return jnp.concatenate(outs, axis=1)


def widen_matrix(tiles_c, cols, side):
    return ones_where(div(iota((tiles_c, cols), 1), side) == iota((tiles_c, cols), 0))


def as_bf(x):
    return x.astype(F32).astype(BF)


def edges_kernel(
    side, place_ref, feat_hbm, valid_ref, wa_ref, wb_ref, wc_ref, send_ref, keep_ref, edge, sems
):
    core = place_ref[0]
    chans, feat_rows, cols = feat_hbm.shape
    copies = []
    for n, at in enumerate((0, feat_rows - BLK)):
        copy = pltpu.make_async_copy(feat_hbm.at[:, at : at + BLK, :], edge.at[n], sems.at[n])
        copy.start()
        copies.append(copy)
    flat = chans * HALO
    lanes = send_ref.shape[1]
    at = flat * cols // lanes
    for ref in (wa_ref, wb_ref, wc_ref):
        taps, outs, ins = ref.shape
        body = ref[...].reshape(taps * outs, ins)
        send_ref[at : at + taps * outs, :] = jnp.concatenate(
            [body, jnp.zeros((taps * outs, lanes - ins), BF)], axis=1
        )
        at += taps * outs
    tiles_r, tiles_c = valid_ref.shape
    masks = mm(as_bf(valid_ref[...]), widen_matrix(tiles_c, cols, side))
    for n in range(cols // lanes):
        send_ref[at + n * tiles_r : at + (n + 1) * tiles_r, :] = masks[
            :, n * lanes : (n + 1) * lanes
        ].astype(BF)
    row, col = iota((flat, chans * BLK), 0), iota((flat, chans * BLK), 1)
    same = div(row, HALO) == div(col, BLK)
    spot = mod(iota((flat, cols), 0), HALO)
    made = []
    for n in range(2):
        if n == 0:
            hit = same & (mod(row, HALO) == mod(col, BLK)) & (mod(row, HALO) < HALO - 1)
            flag, line = spot == HALO - 1, masks[0:1]
        else:
            hit = same & (mod(row, HALO) + BLK - HALO == mod(col, BLK)) & (mod(row, HALO) > 0)
            flag, line = spot == 0, masks[tiles_r - 1 : tiles_r]
        take = ones_where(hit)
        copies[n].wait()
        body = mm(take, edge[n].reshape(chans * BLK, cols))
        made.append(jnp.where(flag, jnp.broadcast_to(line, (flat, cols)), body).astype(BF))
    low = core == 0
    send = jnp.where(low, made[1], made[0])
    keep = jnp.where(low, made[0], made[1])
    for n in range(cols // lanes):
        send_ref[n * flat : (n + 1) * flat, :] = send[:, n * lanes : (n + 1) * lanes]
        keep_ref[n * flat : (n + 1) * flat, :] = keep[:, n * lanes : (n + 1) * lanes]


def weights_kernel(at, chans, place_ref, own_ref, oth_ref, w1_ref, w2_ref, wm_ref, mask_ref):
    core = place_ref[0]
    allc = 2 * chans

    def tap(k):
        return [ref[at + k * chans : at + (k + 1) * chans, 0:allc] for ref in (own_ref, oth_ref)]

    for dst, base in ((w1_ref, 0), (w2_ref, 9)):
        total = None
        for b in range(3):
            tall = jnp.concatenate(sum([tap(base + 3 * a + b) for a in range(3)], []), axis=0)
            src, pos = iota((allc, 3 * allc), 0), iota((allc, 3 * allc), 1)
            place = ones_where(pos == b * allc + mod(src + chans * core, allc))
            part = mm(tall, place)
            total = part if total is None else total + part
        dst[...] = total.astype(BF)
    tall = jnp.concatenate(
        sum([tap(18 + 2 * a + b) for b in range(2) for a in range(2)], []), axis=0
    )
    order = ones_where(iota((allc, allc), 1) == mod(iota((allc, allc), 0) + chans * core, allc))
    wm_ref[...] = mm_nt(order, tall).astype(BF)
    tiles_r = mask_ref.shape[0]
    lanes = own_ref.shape[1]
    at = own_ref.shape[0] - tiles_r * mask_ref.shape[1] // lanes
    for n in range(mask_ref.shape[1] // lanes):
        part = own_ref[at + n * tiles_r : at + (n + 1) * tiles_r, :]
        mask_ref[:, n * lanes : (n + 1) * lanes] = part.astype(F32)


def put(dst, index, x, amount):
    allc = x.shape[0]
    dst[index, 0:allc, :] = shifted(x, amount).astype(BF)
    dst[index, allc : 2 * allc, :] = x.astype(BF)
    dst[index, 2 * allc : 3 * allc, :] = shifted(x, -amount).astype(BF)


def pick_matrix(cols, side):
    half = cols // 2
    wide = half // side
    lane = iota((cols, cols), 1)
    spot = mod(lane, half)
    want = 2 * (mod(spot, wide) * side + div(spot, wide)) + div(lane, half)
    return ones_where(iota((cols, cols), 0) == want)


def merge_pairs(wm, rows_of, pairs, turn, half):
    rhs = []
    for n in pairs:
        sp = rows_of(n)
        rhs.append(jnp.concatenate([sp[:, :half], sp[:, half:]], axis=0))
    both = mm(wm, jnp.concatenate(rhs, axis=1))
    return [pltpu.roll(both[:, n * half : (n + 1) * half], turn, 1) for n in range(2)]


def conv_kernel(
    side,
    place_ref,
    own_hbm,
    oth_hbm,
    masks_ref,
    w1,
    w2,
    wm,
    es_hbm,
    mown_ref,
    moth_ref,
    xa_ref,
    ha_ref,
    ea_ref,
    feat,
    xs,
    hs,
    es_ref,
    mask,
    pa_ref,
    pb_ref,
    in_sems,
    out_sem,
):
    core = place_ref[0]
    rows, allc, cols = es_ref.shape
    chans = allc // 2
    main = rows // BLK
    copies = []
    for m in range(main + 1):
        at = rows - BLK * core if m == main else rows * core + BLK * m
        for n, ref in enumerate((own_hbm, oth_hbm)):
            copy = pltpu.make_async_copy(
                ref.at[:, pl.ds(pl.multiple_of(at, BLK), BLK), :], feat.at[n, m], in_sems.at[n, m]
            )
            copy.start()
            copies.append(copy)

    tiles_r = masks_ref.shape[0]
    mask[...] = jnp.zeros(mask.shape, F32)
    mask[pl.ds(side, tiles_r), :] = masks_ref[...]

    first_row = 5
    outer_start = jnp.where(core == 0, first_row - HALO, first_row + rows)
    for r in range(HALO):
        xs[outer_start + r] = jnp.zeros(xs.shape[1:], BF)
    xs[0] = jnp.zeros(xs.shape[1:], BF)
    turn = swap_matrix(BLK, BLK)
    few = HALO * BLK
    row, col = iota((few, BLK * BLK), 0), iota((few, BLK * BLK), 1)
    turn_mid = ones_where(
        (mod(row, BLK) == div(col, BLK)) & (div(row, BLK) + (BLK - HALO) * core == mod(col, BLK))
    )
    mid_start = jnp.where(core == 0, first_row + rows, first_row - HALO)
    for m in range(main + 1):
        for copy in copies[2 * m : 2 * m + 2]:
            copy.wait()
        parts = []
        for n in range(2):
            for ch in range(0, chans, BLK):
                block = feat[n, m, ch : ch + BLK].reshape(BLK * BLK, cols)
                parts.append(mm(turn_mid if m == main else turn, block))
        at = mid_start if m == main else first_row + m * BLK
        for r in range(HALO if m == main else BLK):
            x = jnp.concatenate([p[r * BLK : (r + 1) * BLK] for p in parts], axis=0)
            put(xs, at + r, x, 1)

    base = side + core * (rows // side)
    total_steps = rows // side + 1
    tiles = 3 if total_steps % 3 == 0 else 1
    group = tiles * side

    def lines(step, ahead):
        return [mask[pl.ds(base + step * tiles + k - 1, 1), :] for k in range(tiles + ahead)]

    pa_ref[...] = jnp.zeros(pa_ref.shape, F32)
    pb_ref[...] = jnp.zeros(pb_ref.shape, F32)

    def first(step, carry):
        pa, pb = pa_ref[0], pb_ref[0]
        flag = lines(step, 1)
        for j in range(group):
            q = step * group + j
            y = mm(w1[...], xs[q])
            total = pa + y[2 * allc :]
            pa = pb + y[allc : 2 * allc]
            pb = y[:allc]
            h = jnp.maximum(total * flag[(j + 2) // side], 0.0)
            put(hs, q, h.astype(BF), 2)
        pa_ref[0] = pa
        pb_ref[0] = pb
        return carry

    lax.fori_loop(0, total_steps // tiles, first, 0)

    pa_ref[0] = jnp.zeros((allc, cols), F32)
    pb_ref[0] = jnp.zeros((allc, cols), F32)

    def second(step, carry):
        pa, pb = [pa_ref[0], pa_ref[1]], [pb_ref[0], pb_ref[1]]
        flag = lines(step, 0)
        for j in range(group):
            q = step * group + j
            i = j % 2
            z = mm(w2[...], hs[q])
            total = pa[i] + z[2 * allc :]
            pa[i] = pb[i] + z[allc : 2 * allc]
            pb[i] = z[:allc]
            x = xs[jnp.maximum(q - 3, 0), allc : 2 * allc, :].astype(F32)
            es_ref[jnp.maximum(q - side, 0)] = (flag[j // side] * (x + total)).astype(BF)
        for i in range(2):
            pa_ref[i] = pa[i]
            pb_ref[i] = pb[i]
        return carry

    lax.fori_loop(0, total_steps // tiles, second, 0)

    out = pltpu.make_async_copy(es_ref, es_hbm.at[pl.ds(0, rows)], out_sem)
    out.start()

    for k in range(3):
        xa_ref[k] = xs[first_row + (rows - 3) * core + k]
    for k in range(4):
        ha_ref[k] = hs[jnp.where(core == 0, 7, rows + 1) + k]
    ea_ref[0] = es_ref[jnp.where(core == 0, 3, rows - 4)]

    half = cols // 2
    wide = half // side
    pick = pick_matrix(cols, side)
    picked = hs.reshape(hs.shape[0] * hs.shape[1], cols)
    for tile in range(rows // side):
        tall = es_ref[tile * side : (tile + 1) * side].reshape(side * allc, cols)
        picked[tile * side * allc : (tile + 1) * side * allc, :] = mm(tall, pick).astype(BF)
    for tile in range(rows // side):
        g = tile // 2 + core * (rows // (2 * side))

        def rows_of(k, tile=tile):
            at = (tile * side + 2 * k) * allc
            return picked[at : at + 2 * allc, :]

        for k in range(0, side // 2, 2):
            for n, piece in enumerate(merge_pairs(wm[...], rows_of, (k, k + 1), g * wide, half)):
                u = (side // 2) * (tile % 2) + k + n
                mown_ref[tile // 2, u * chans : (u + 1) * chans, :] = piece[:chans].astype(BF)
                moth_ref[tile // 2, u * chans : (u + 1) * chans, :] = piece[chans:].astype(BF)
    out.wait()


def border_kernel(
    rows,
    place_ref,
    outer_ref,
    masks_ref,
    w1,
    w2,
    wm,
    xa_ref,
    ha_ref,
    ea_ref,
    mown_in,
    moth_in,
    es_in,
    es_hbm,
    mown_ref,
    moth_ref,
    x5,
    h7,
    e4,
    sem,
):
    core = place_ref[0]
    _, allc, cols = ea_ref.shape
    chans = allc // 2
    lanes = outer_ref.shape[1]
    tiles_r = masks_ref.shape[0]
    masks = masks_ref[...]
    top = core == 0
    turn4 = swap_matrix(HALO, chans)
    flat = HALO * chans
    pieces = [outer_ref[k * flat : (k + 1) * flat, :] for k in range(2 * cols // lanes)]
    oth, own = [
        mm(turn4, jnp.concatenate(pieces[n * cols // lanes : (n + 1) * cols // lanes], axis=1))
        for n in range(2)
    ]
    halo = [
        jnp.concatenate([p[r * chans : (r + 1) * chans] for p in (own, oth)], axis=0)
        for r in range(HALO)
    ]
    outer_mask = jnp.where(top, halo[0][0:1], halo[HALO - 1][0:1])
    tile_mask = jnp.where(top, masks[0:1], masks[tiles_r - 1 : tiles_r])
    for k in range(3):
        put(x5, jnp.where(top, k, k + 2), jnp.where(top, halo[k + 1], halo[k]), 1)
    for k in range(2):
        x5[jnp.where(top, k + 3, k)] = xa_ref[jnp.where(top, k, k + 1)]
    for k in range(4):
        h7[jnp.where(top, k + 3, k)] = ha_ref[k]
    y = [mm(w1[...], x5[k]) for k in range(5)]
    for k in range(3):
        total = y[k][:allc] + y[k + 1][allc : 2 * allc] + y[k + 2][2 * allc :]
        if k == 1:
            line = outer_mask
        else:
            line = jnp.where(top if k == 0 else core == 1, outer_mask, tile_mask)
        h = jnp.maximum(total * line, 0.0)
        put(h7, jnp.where(top, k, k + 4), h, 2)
    z = [mm(w2[...], h7[k]) for k in range(7)]
    e4[jnp.where(top, 3, 0)] = ea_ref[0]
    for k in range(3):
        total = z[k][:allc] + z[k + 2][allc : 2 * allc] + z[k + 4][2 * allc :]
        x = xa_ref[k, allc : 2 * allc, :].astype(F32)
        e4[jnp.where(top, k, k + 1)] = (tile_mask * (x + total)).astype(BF)
    copy = pltpu.make_async_copy(
        e4.at[pl.ds(core, 3)], es_hbm.at[pl.ds((rows - 3) * core, 3)], sem
    )
    copy.start()
    mown_ref[...] = mown_in[...]
    moth_ref[...] = moth_in[...]
    half = cols // 2
    parent_rows = mown_ref.shape[0]
    side = mown_ref.shape[1] // chans
    wide = half // side
    s = mm(e4[...].reshape(4 * allc, cols), pick_matrix(cols, side)).astype(BF)
    g = jnp.where(top, 0, 2 * parent_rows - 1)
    at_g = jnp.where(top, 0, parent_rows - 1)

    def rows_of(k):
        return s[k * 2 * allc : (k + 1) * 2 * allc]

    for n, piece in enumerate(merge_pairs(wm[...], rows_of, (0, 1), g * wide, half)):
        u = jnp.where(top, n, side - 2 + n)
        at_u = pl.ds(pl.multiple_of(u * chans, chans), chans)
        mown_ref[at_g, at_u, :] = piece[:chans].astype(BF)
        moth_ref[at_g, at_u, :] = piece[chans:].astype(BF)
    copy.wait()


def restore_kernel(place_ref, es_hbm, after_hbm, enh_hbm, eoth_ref, es_ref, own, sem, in_sems):
    core = place_ref[0]
    rows, allc, cols = es_ref.shape
    chans = allc // 2
    copies = []
    for m in range(rows // BLK):
        at = pl.ds(m * BLK, BLK)
        copies.append(pltpu.make_async_copy(es_hbm.at[at], es_ref.at[at], in_sems.at[m]))
        copies[-1].start()
    turn = swap_matrix(BLK, BLK)
    for m in range(rows // BLK):
        copies[m].wait()
        at = m * BLK
        for c0 in range(0, allc, BLK):
            ref = own if c0 < chans else eoth_ref
            ch = c0 % chans
            block = es_ref[at : at + BLK, c0 : c0 + BLK, :].reshape(BLK * BLK, cols)
            ref[ch : ch + BLK, at : at + BLK, :] = mm(turn, block).astype(BF).reshape(BLK, BLK, cols)
    copy = pltpu.make_async_copy(
        own, enh_hbm.at[:, pl.ds(pl.multiple_of(core * rows, rows), rows), :], sem
    )
    copy.start()
    copy.wait()


def fill_kernel(place_ref, recv_ref, held_hbm, enh_hbm, sem):
    core = place_ref[0]
    rows = recv_ref.shape[1]
    copy = pltpu.make_async_copy(
        recv_ref, enh_hbm.at[:, pl.ds(pl.multiple_of((1 - core) * rows, rows), rows), :], sem
    )
    copy.start()
    copy.wait()


def deal(now, width):
    n = len(now)
    group = div(iota(now[0].shape, 1), width)
    bit = 1
    while bit < n:
        odd = group & bit != 0
        now = [jnp.where(odd, now[(j + bit) % n], now[j]) for j in range(n)]
        bit *= 2
    return now


def pack_kernel(
    side, slots, place_ref, owner_ref, mown_ref, mrecv_ref, out_ref, arr, lhs, mid, code_ref
):
    core, tile = place_ref[0], place_ref[1]
    count = owner_ref.shape[1]
    mine, rows, lanes = mown_ref.shape
    blocks, all_rows, _ = out_ref.shape
    per = side * slots
    wide = lanes // side
    for k in range(mine):
        arr[core * mine + k] = mown_ref[k]
        arr[(1 - core) * mine + k] = mrecv_ref[k]
    line = jnp.broadcast_to(owner_ref[...].astype(F32), (lanes, count))
    owner = jnp.transpose(line).astype(jnp.int32)
    is_owner = owner == iota((count, lanes), 1)
    marks = ones_where(is_owner)
    lower = ones_where(iota((count, count), 0) > iota((count, count), 1))
    earlier = mm(lower, marks)
    within = jnp.sum(jnp.where(is_owner, earlier, 0.0), axis=1, keepdims=True).astype(jnp.int32)
    if per == lanes:
        code = (owner * slots + within).astype(F32).astype(BF)
        code_ref[0:count, :] = code
        code_ref[count : 2 * count, :] = code

        def by_column(step, carry):
            at = pl.ds(pl.multiple_of(step * BLK, BLK), BLK)
            done = deal([arr[g, at, :] for g in range(side)], wide)
            for j in range(side):
                lhs[-j % side, at, :] = done[j]
            return carry

        lax.fori_loop(0, rows // BLK, by_column, 0, unroll=4)
        halves = blocks // side
        lane = iota((1, halves * lanes), 1)
        block, group, slot = div(lane, lanes), div(mod(lane, lanes), wide), mod(lane, wide)
        for i in range(side):
            v = lax.rem(i + side - lax.rem(tile, side), side)
            at = pl.multiple_of(count - wide * v, wide)
            codes = code_ref[pl.ds(at, count), :]
            want = (block * side + mod(group - i + side, side)) * slots + slot
            want = jnp.broadcast_to(want.astype(F32).astype(BF), (count, halves * lanes))
            same = jnp.concatenate([codes] * halves, axis=1) == want
            take = jnp.where(same, jnp.ones_like(want), jnp.zeros_like(want))
            got = mm(lhs[v], take).astype(BF)
            for h in range(halves):
                mid[h * side + i] = got[:, h * lanes : (h + 1) * lanes]
        for h in range(halves):

            def by_owner(step, carry, h=h):
                at = pl.ds(pl.multiple_of(step * BLK, BLK), BLK)
                done = deal([mid[h * side + i, at, :] for i in range(side)], wide)
                for j in range(side):
                    out_ref[h * side + -j % side, at, :] = done[j]
                return carry

            lax.fori_loop(0, rows // BLK, by_owner, 0, unroll=4)
        tally = mm(jnp.ones((all_rows - rows, count), BF), marks)
        for d in range(blocks):
            out_ref[d, rows:all_rows, :] = jnp.broadcast_to(
                tally[:, d : d + 1], (all_rows - rows, lanes)
            ).astype(BF)
    else:
        code = owner * per + within
        lane = iota((wide, lanes), 1)
        for g in range(2 * mine):
            for x in range(side):
                at = (g * side + x) * wide
                code_ref[at : at + wide, :] = (
                    code[g * wide : (g + 1) * wide] + (x - g) % side * slots
                )
        data = jnp.concatenate([arr[g] for g in range(2 * mine)], axis=1)
        lane = iota((count * side, lanes), 1)
        for step in range(0, blocks, 2):
            codes = code_ref[...]
            spots = [ones_where(codes == lane + at * lanes) for at in (step, step + 1)]
            total = mm(data, jnp.concatenate(spots, axis=1)).astype(BF)
            for n in range(2):
                at = step + n
                out_ref[at, 0:rows, :] = total[:, n * lanes : (n + 1) * lanes]
                goal = div(iota((count, lanes), 1) + at * lanes, per)
                tally = mm(jnp.ones((all_rows - rows, count), BF), ones_where(owner == goal))
                out_ref[at, rows:all_rows, :] = tally.astype(BF)


def targets(tallies, lanes, group, slots):
    lane0, lane1 = iota((lanes, lanes), 0), iota((lanes, lanes), 1)
    heads = mod(lane0, group) == 0
    before = ones_where(heads & (div(lane0, group) < div(lane1, group)))
    every = ones_where(heads)
    slot = mod(iota((1, lanes), 1), slots).astype(F32)
    running = jnp.zeros((1, lanes), F32)
    outs = []
    for tally in tallies:
        inside, whole = mm(tally, before)[0:1], mm(tally, every)[0:1]
        live = slot < tally.astype(F32)[0:1]
        outs.append(jnp.where(live, running + inside + slot, -1.0))
        running = running + whole
    return outs


def hits(target, room):
    shape = (room, target.shape[1])
    goal = iota(shape, 0).astype(F32).astype(BF)
    same = goal == jnp.broadcast_to(target.astype(BF), shape)
    return jnp.where(same, jnp.ones_like(goal), jnp.zeros_like(goal))


def unpack_kernel(side, slots, place_ref, got_ref, out_ref, picked, data):
    tile = place_ref[1]
    blocks, all_rows, lanes = got_ref.shape
    chans, cells, cap = out_ref.shape
    rows = side * chans
    per = side * slots
    room = picked.shape[2]
    if per == lanes:
        halves = blocks // side
        group = div(iota((all_rows - rows, lanes), 1), slots)
        tallies = []
        for h in range(halves):
            tally = got_ref[h * side, rows:all_rows, :].astype(F32)
            for s in range(1, side):
                other = got_ref[h * side + s, rows:all_rows, :].astype(F32)
                tally = jnp.where(group == s, other, tally)
            tallies.append(tally.astype(BF))
        spots = targets(tallies, lanes, slots, slots)
        for h in range(halves):

            def turn_rows(step, carry, h=h):
                at = pl.ds(pl.multiple_of(step * BLK, BLK), BLK)
                done = deal([got_ref[h * side + s, at, :] for s in range(side)], slots)
                for j in range(side):
                    data[h, j, at, :] = done[j]
                return carry

            lax.fori_loop(0, rows // BLK, turn_rows, 0, unroll=True)
        for j in range(side):
            v = lax.rem(2 * side - j - lax.rem(tile, side), side)
            left = jnp.concatenate([data[h, j] for h in range(halves)], axis=1)
            right = []
            for spot in spots:
                line = jnp.broadcast_to(spot, (side, lanes))
                line = pltpu.roll(line, (side - j) * slots, 1) if j else line
                right.append(hits(line[0:1], room))
            picked[v] = mm_nt(left, jnp.concatenate(right, axis=1)).astype(BF)
    else:
        tallies = [got_ref[b, rows:all_rows, :] for b in range(blocks)]
        spots = [hits(t, room) for t in targets(tallies, lanes, per, slots)]
        spots = jnp.concatenate(spots, axis=1)
        for v in range(side):
            keep = div(mod(iota((rows, lanes), 1), per), slots) == v
            left = jnp.concatenate(
                [jnp.where(keep, got_ref[b, 0:rows, :], jnp.zeros((rows, lanes), BF)) for b in range(blocks)],
                axis=1,
            )
            picked[v] = mm_nt(left, spots).astype(BF)
    two = BLK // side
    n = BLK * BLK
    row, col = iota((n, n), 0), iota((n, n), 1)
    turn = ones_where(
        (div(row, BLK) == mod(col, BLK))
        & (mod(div(row, side), two) == mod(div(col, BLK), two))
        & (mod(row, side) == div(col, BLK * two))
    )
    for u in range(0, side, two):
        for ch in range(0, chans, BLK):
            block = jnp.concatenate(
                [
                    picked[v, (u + w) * chans + ch : (u + w) * chans + ch + BLK, :]
                    for v in range(side)
                    for w in range(two)
                ],
                axis=0,
            )
            done = mm(turn, block).astype(BF).reshape(BLK, BLK, room)
            out_ref[ch : ch + BLK, u * side : (u + two) * side, :] = done[:, :, :cap]


def on_device(features, tile_valid, parent_owner, w_first, w_second, w_merge):
    chans, row_count, col_count = features.shape
    tile_rows, tile_cols = tile_valid.shape
    side = row_count // tile_rows
    parents_dev = parent_owner.shape[0]
    devices = lax.axis_size("tiles")
    slots = 2 * max(1, parents_dev // devices)
    own_cap = 3 * parents_dev // 2
    rows = row_count // 2
    allc = 2 * chans
    lanes = 128
    blocks = devices * slots * side // lanes
    fold = devices // blocks
    core = lax.axis_index("chan")
    place = jnp.stack([core, lax.axis_index("tiles")]).astype(jnp.int32)
    swap = [(0, 1), (1, 0)]
    vmem = pl.BlockSpec(memory_space=pltpu.VMEM)
    smem = pl.BlockSpec(memory_space=pltpu.SMEM)
    hbm = pl.BlockSpec(memory_space=pltpu.HBM)

    def limit(mib):
        return pltpu.CompilerParams(vmem_limit_bytes=int(mib * 1024) << 10)

    feat_oth = lax.ppermute(features, "chan", swap)
    w_mergt = jnp.swapaxes(w_merge, 1, 2)
    edge_rows = chans * HALO * col_count // lanes
    tap_rows = (w_first.shape[0] + w_second.shape[0] + w_merge.shape[0]) * chans
    mask_rows = tile_rows * col_count // lanes
    send, keep = pl.pallas_call(
        functools.partial(edges_kernel, side),
        out_shape=(
            jax.ShapeDtypeStruct((edge_rows + tap_rows + mask_rows, lanes), BF),
            jax.ShapeDtypeStruct((edge_rows, lanes), BF),
        ),
        in_specs=[smem, hbm] + [vmem] * 4,
        out_specs=(vmem,) * 2,
        scratch_shapes=[
            pltpu.VMEM((2, chans, BLK, col_count), BF),
            pltpu.SemaphoreType.DMA((2,)),
        ],
        compiler_params=limit(63.9),
        name="edges",
    )(place, features, tile_valid, w_first, w_second, w_mergt)
    sent = lax.ppermute(send, "chan", swap)
    cross = [(2 * t + 1, 2 * t + 2) for t in range(devices - 1)]
    cross += [(2 * t, 2 * t - 1) for t in range(1, devices)]
    outer = lax.ppermute(
        jnp.concatenate([keep, sent[:edge_rows]], axis=0), ("tiles", "chan"), cross
    )
    w1, w2, wm, masks = pl.pallas_call(
        functools.partial(weights_kernel, edge_rows, chans),
        out_shape=(
            jax.ShapeDtypeStruct((3 * allc, 3 * allc), BF),
            jax.ShapeDtypeStruct((3 * allc, 3 * allc), BF),
            jax.ShapeDtypeStruct((allc, 4 * allc), BF),
            jax.ShapeDtypeStruct((tile_rows, col_count), F32),
        ),
        in_specs=[smem, vmem, vmem],
        out_specs=(vmem,) * 4,
        compiler_params=limit(6),
        name="weights",
    )(place, send, sent)

    parent_rows = tile_rows // 4
    held_rows = rows * pl.cdiv(44 << 20, rows * allc * col_count * 2)
    es, m_own, m_oth, xa, ha, ea = pl.pallas_call(
        functools.partial(conv_kernel, side),
        out_shape=(
            jax.ShapeDtypeStruct((held_rows, allc, col_count), BF),
            jax.ShapeDtypeStruct((parent_rows, side * chans, col_count // 2), BF),
            jax.ShapeDtypeStruct((parent_rows, side * chans, col_count // 2), BF),
            jax.ShapeDtypeStruct((3, 3 * allc, col_count), BF),
            jax.ShapeDtypeStruct((4, 3 * allc, col_count), BF),
            jax.ShapeDtypeStruct((1, allc, col_count), BF),
        ),
        in_specs=[smem, hbm, hbm] + [vmem] * 4,
        out_specs=(hbm,) + (vmem,) * 5,
        scratch_shapes=[
            pltpu.VMEM((2, rows // BLK + 1, chans, BLK, col_count), BF),
            pltpu.VMEM((rows + 16, 3 * allc, col_count), BF),
            pltpu.VMEM((rows + side, 3 * allc, col_count), BF),
            pltpu.VMEM((rows, allc, col_count), BF),
            pltpu.VMEM((tile_rows + 2 * side, col_count), F32),
            pltpu.VMEM((2, allc, col_count), F32),
            pltpu.VMEM((2, allc, col_count), F32),
            pltpu.SemaphoreType.DMA((2, rows // BLK + 1)),
            pltpu.SemaphoreType.DMA,
        ],
        compiler_params=limit(52),
        name="conv",
    )(place, features, feat_oth, masks, w1, w2, wm)
    es, m_own, m_oth = pl.pallas_call(
        functools.partial(border_kernel, rows),
        out_shape=(
            jax.ShapeDtypeStruct(es.shape, BF),
            jax.ShapeDtypeStruct((parent_rows, side * chans, col_count // 2), BF),
            jax.ShapeDtypeStruct((parent_rows, side * chans, col_count // 2), BF),
        ),
        in_specs=[smem] + [vmem] * 10 + [hbm],
        out_specs=(hbm, vmem, vmem),
        scratch_shapes=[
            pltpu.VMEM((5, 3 * allc, col_count), BF),
            pltpu.VMEM((7, 3 * allc, col_count), BF),
            pltpu.VMEM((4, allc, col_count), BF),
            pltpu.SemaphoreType.DMA,
        ],
        input_output_aliases={11: 0},
        compiler_params=limit(16),
        name="border",
    )(place, outer, masks, w1, w2, wm, xa, ha, ea, m_own, m_oth, es)
    m_recv = lax.ppermute(m_oth, "chan", swap)
    all_rows = side * chans + 8
    packed = pl.pallas_call(
        functools.partial(pack_kernel, side, slots),
        out_shape=jax.ShapeDtypeStruct((blocks, all_rows, lanes), BF),
        in_specs=[smem, vmem, vmem, vmem],
        out_specs=vmem,
        scratch_shapes=[
            pltpu.VMEM((2 * parent_rows, side * chans, lanes), BF),
            pltpu.VMEM((side, side * chans, lanes), BF),
            pltpu.VMEM((blocks, side * chans, lanes), BF),
            pltpu.VMEM((parents_dev * side, lanes), BF if fold == 1 else jnp.int32),
        ],
        compiler_params=limit(16),
        name="pack",
    )(place, parent_owner[None, :], m_own, m_recv)

    def to_peers(x):
        if fold > 1:
            x = x.reshape(blocks, all_rows, fold, lanes // fold)
            x = x.transpose(0, 2, 1, 3).reshape(devices, all_rows, lanes // fold)
        x = lax.all_to_all(x, "tiles", split_axis=0, concat_axis=0, tiled=True)
        if fold > 1:
            x = x.reshape(blocks, fold, all_rows, lanes // fold)
            x = x.transpose(0, 2, 1, 3).reshape(blocks, all_rows, lanes)
        return x

    got = to_peers(packed)
    held, e_oth = pl.pallas_call(
        restore_kernel,
        out_shape=(
            jax.ShapeDtypeStruct((chans, row_count, col_count), BF),
            jax.ShapeDtypeStruct((chans, rows, col_count), BF),
        ),
        in_specs=[smem, hbm, hbm],
        out_specs=(hbm, vmem),
        scratch_shapes=[
            pltpu.VMEM((rows, allc, col_count), BF),
            pltpu.VMEM((chans, rows, col_count), BF),
            pltpu.SemaphoreType.DMA,
            pltpu.SemaphoreType.DMA((rows // BLK,)),
        ],
        compiler_params=limit(12),
        name="restore",
    )(place, es, packed)
    e_recv = lax.ppermute(e_oth, "chan", swap)
    enhanced = pl.pallas_call(
        fill_kernel,
        out_shape=jax.ShapeDtypeStruct((chans, row_count, col_count), BF),
        in_specs=[smem, vmem, hbm],
        out_specs=hbm,
        scratch_shapes=[pltpu.SemaphoreType.DMA],
        input_output_aliases={2: 0},
        compiler_params=limit(6),
        name="fill",
    )(place, e_recv, held)
    room = pl.cdiv(own_cap, lanes) * lanes
    parents = pl.pallas_call(
        functools.partial(unpack_kernel, side, slots),
        out_shape=jax.ShapeDtypeStruct((chans, side * side, own_cap), BF),
        in_specs=[smem, vmem],
        out_specs=vmem,
        scratch_shapes=[
            pltpu.VMEM((side, side * chans, room), BF),
            pltpu.VMEM((2, side, side * chans, lanes), BF),
        ],
        compiler_params=limit(24),
        name="unpack",
    )(place, got)
    return enhanced, jnp.swapaxes(parents, 1, 2)


def solution(mesh):
    return jax.shard_map(
        on_device,
        mesh=mesh,
        in_specs=(
            P("chan", "tiles", None),
            P("tiles", None),
            P("tiles"),
            P(None, "chan", None),
            P(None, "chan", None),
            P(None, None, "chan"),
        ),
        out_specs=(P("chan", "tiles", None), P("chan", "tiles", None)),
        check_vma=False,
    )
```

```python
import functools

import jax
import jax.numpy as jnp
from jax import lax
from jax.experimental import pallas as pl
from jax.experimental.pallas import tpu as pltpu
from jax.sharding import PartitionSpec as P

BF = jnp.bfloat16
F32 = jnp.float32
HALO = 4
BLK = 16


def iota(shape, dim):
    return lax.broadcasted_iota(jnp.int32, shape, dim)


def div(x, n):
    return x >> (n.bit_length() - 1) if n & (n - 1) == 0 else lax.div(x, jnp.int32(n))


def mod(x, n):
    return x & (n - 1) if n & (n - 1) == 0 else lax.rem(x, jnp.int32(n))


def ones_where(cond):
    return jnp.where(cond, 1.0, 0.0).astype(BF)


def mm(a, b):
    return jnp.dot(a, b, preferred_element_type=F32)


def mm_nt(a, b):
    return lax.dot_general(a, b, (((1,), (1,)), ((), ())), preferred_element_type=F32)


def swap_matrix(outer, inner):
    n = outer * inner
    row, col = iota((n, n), 0), iota((n, n), 1)
    return ones_where((mod(row, inner) == div(col, outer)) & (div(row, inner) == mod(col, outer)))


def shifted(x, amount):
    lanes = 128
    parts = [x[:, at : at + lanes] for at in range(0, x.shape[1], lanes)]
    turned = [pltpu.roll(p, amount % lanes, 1) for p in parts]
    lane = iota(parts[0].shape, 1)
    zero = jnp.zeros_like(parts[0])
    outs = []
    for n in range(len(parts)):
        if amount > 0:
            edge = turned[n - 1] if n else zero
            outs.append(jnp.where(lane < amount, edge, turned[n]))
        else:
            edge = turned[n + 1] if n + 1 < len(parts) else zero
            outs.append(jnp.where(lane >= lanes + amount, edge, turned[n]))
    return jnp.concatenate(outs, axis=1)


def widen_matrix(tiles_c, cols, side):
    return ones_where(div(iota((tiles_c, cols), 1), side) == iota((tiles_c, cols), 0))


def as_bf(x):
    return x.astype(F32).astype(BF)


def edges_kernel(side, tiles_r, tiles_c, feat_hbm, extra_ref, send_ref, keep_ref, edge, sems):
    core = lax.axis_index("chan")
    chans, feat_rows, cols = feat_hbm.shape
    copies = []
    for n, at in enumerate((0, feat_rows - BLK)):
        copy = pltpu.make_async_copy(feat_hbm.at[:, at : at + BLK, :], edge.at[n], sems.at[n])
        copy.start()
        copies.append(copy)
    flat = chans * HALO
    lanes = send_ref.shape[1]
    last = extra_ref.shape[0] - 1
    masks = mm(extra_ref[last, 0:tiles_r, 0:tiles_c], widen_matrix(tiles_c, cols, side))
    row, col = iota((flat, chans * BLK), 0), iota((flat, chans * BLK), 1)
    same = div(row, HALO) == div(col, BLK)
    spot = mod(iota((flat, cols), 0), HALO)
    made = []
    for n in range(2):
        if n == 0:
            hit = same & (mod(row, HALO) == mod(col, BLK)) & (mod(row, HALO) < HALO - 1)
            flag, line = spot == HALO - 1, masks[0:1]
        else:
            hit = same & (mod(row, HALO) + BLK - HALO == mod(col, BLK)) & (mod(row, HALO) > 0)
            flag, line = spot == 0, masks[tiles_r - 1 : tiles_r]
        take = ones_where(hit)
        copies[n].wait()
        body = mm(take, edge[n].reshape(chans * BLK, cols))
        made.append(jnp.where(flag, jnp.broadcast_to(line, (flat, cols)), body).astype(BF))
    low = core == 0
    send = jnp.where(low, made[1], made[0])
    keep = jnp.where(low, made[0], made[1])
    for n in range(cols // lanes):
        send_ref[n * flat : (n + 1) * flat, :] = send[:, n * lanes : (n + 1) * lanes]
        keep_ref[n * flat : (n + 1) * flat, :] = keep[:, n * lanes : (n + 1) * lanes]


def weights_kernel(side, tiles_c, own_ref, oth_ref, w1_ref, w2_ref, wm_ref, mask_ref):
    core = lax.axis_index("chan")
    chans, allc = own_ref.shape[1:]

    def tap(k):
        return [ref[k] for ref in (own_ref, oth_ref)]

    for dst, base in ((w1_ref, 0), (w2_ref, 9)):
        total = None
        for b in range(3):
            tall = jnp.concatenate(sum([tap(base + 3 * a + b) for a in range(3)], []), axis=0)
            src, pos = iota((allc, 3 * allc), 0), iota((allc, 3 * allc), 1)
            place = ones_where(pos == b * allc + mod(src + chans * core, allc))
            part = mm(tall, place)
            total = part if total is None else total + part
        dst[...] = total.astype(BF)
    tall = jnp.concatenate(
        sum([tap(18 + 2 * a + b) for b in range(2) for a in range(2)], []), axis=0
    )
    order = ones_where(iota((allc, allc), 1) == mod(iota((allc, allc), 0) + chans * core, allc))
    wm_ref[...] = mm_nt(order, tall).astype(BF)
    tiles_r, cols = mask_ref.shape
    last = own_ref.shape[0] - 1
    mask_ref[...] = mm(own_ref[last, 0:tiles_r, 0:tiles_c], widen_matrix(tiles_c, cols, side))


def put(dst, index, x, amount):
    allc = x.shape[0]
    dst[index, 0:allc, :] = shifted(x, amount).astype(BF)
    dst[index, allc : 2 * allc, :] = x.astype(BF)
    dst[index, 2 * allc : 3 * allc, :] = shifted(x, -amount).astype(BF)


def pick_matrix(cols, side):
    half = cols // 2
    wide = half // side
    lane = iota((cols, cols), 1)
    spot = mod(lane, half)
    want = 2 * (mod(spot, wide) * side + div(spot, wide)) + div(lane, half)
    return ones_where(iota((cols, cols), 0) == want)


def merge_pairs(wm, rows_of, pairs, turn, half):
    rhs = []
    for n in pairs:
        sp = rows_of(n)
        rhs.append(jnp.concatenate([sp[:, :half], sp[:, half:]], axis=0))
    both = mm(wm, jnp.concatenate(rhs, axis=1))
    return [pltpu.roll(both[:, n * half : (n + 1) * half], turn, 1) for n in range(2)]


def conv_kernel(
    side,
    own_ref,
    oth_ref,
    masks_ref,
    w1,
    w2,
    wm,
    es_hbm,
    mown_ref,
    moth_ref,
    xa_ref,
    ha_ref,
    ea_ref,
    xs,
    hs,
    es_ref,
    mask,
    picked,
    out_sem,
):
    core = lax.axis_index("chan")
    rows, allc, cols = es_ref.shape
    chans = allc // 2
    main = rows // BLK
    tiles_r = masks_ref.shape[0]
    mask[...] = jnp.zeros(mask.shape, F32)
    mask[pl.ds(side, tiles_r), :] = masks_ref[...]

    first_row = 5
    outer_start = jnp.where(core == 0, first_row - HALO, first_row + rows)
    for r in range(HALO):
        xs[outer_start + r] = jnp.zeros(xs.shape[1:], BF)
    zero_row = jnp.zeros(xs.shape[1:], BF)
    xs[0] = zero_row
    turn = swap_matrix(BLK, BLK)
    few = HALO * BLK
    row, col = iota((few, BLK * BLK), 0), iota((few, BLK * BLK), 1)
    turn_mid = ones_where(
        (mod(row, BLK) == div(col, BLK)) & (div(row, BLK) + (BLK - HALO) * core == mod(col, BLK))
    )
    half = cols // 2
    wide = half // side
    pick = pick_matrix(cols, side)
    base = side + core * (rows // side)
    tiles = rows // side

    def lay_block(m):
        at = rows - BLK * core if m == main else rows * core + BLK * m
        parts = []
        for ref in (own_ref, oth_ref):
            for ch in range(0, chans, BLK):
                block = ref[ch : ch + BLK, pl.ds(pl.multiple_of(at, BLK), BLK), :]
                parts.append(mm(turn_mid if m == main else turn, block.reshape(BLK * BLK, cols)))
        return parts

    def lay_row(parts, r, at):
        put(xs, at, jnp.concatenate([p[r * BLK : (r + 1) * BLK] for p in parts], axis=0), 1)

    mid_start = jnp.where(core == 0, first_row + rows, first_row - HALO)
    parts = lay_block(main)
    for r in range(HALO):
        lay_row(parts, r, mid_start + r)

    def line(k):
        return mask[pl.ds(base + k, 1), :]

    none = jnp.zeros((allc, cols), F32)
    first_sums = [none, none]
    second_sums = [[none, none], [none, none]]

    def first(q):
        pa, pb = first_sums
        y = mm(w1[...], xs[q])
        total = pa + y[2 * allc :]
        first_sums[:] = [pb + y[allc : 2 * allc], y[:allc]]
        h = jnp.maximum(total * line((q + 2) // side - 1), 0.0)
        put(hs, q, h.astype(BF), 2)

    def second(q):
        pa, pb = second_sums[q % 2]
        z = mm(w2[...], hs[q])
        total = pa + z[2 * allc :]
        second_sums[q % 2] = [pb + z[allc : 2 * allc], z[:allc]]
        if q >= side:
            x = xs[q - 3, allc : 2 * allc, :].astype(F32)
            es_ref[q - side] = (line(q // side - 1) * (x + total)).astype(BF)

    def pick_tile(tile):
        tall = es_ref[tile * side : (tile + 1) * side].reshape(side * allc, cols)
        picked[tile * side * allc : (tile + 1) * side * allc, :] = mm(tall, pick).astype(BF)

    def merge_tile(tile, k):
        g = tile // 2 + core * (rows // (2 * side))

        def rows_of(n):
            at = (tile * side + 2 * n) * allc
            return picked[at : at + 2 * allc, :]

        for n, piece in enumerate(merge_pairs(wm[...], rows_of, (k, k + 1), g * wide, half)):
            u = (side // 2) * (tile % 2) + k + n
            mown_ref[tile // 2, u * chans : (u + 1) * chans, :] = piece[:chans].astype(BF)
            moth_ref[tile // 2, u * chans : (u + 1) * chans, :] = piece[chans:].astype(BF)

    outs = []
    lag = 4
    total_rows = rows + side
    for s in range(-1, total_rows + 3 * lag + 2 * side):
        if 0 <= s < rows:
            if s % BLK == 0:
                parts = lay_block(s // BLK)
            lay_row(parts, s % BLK, first_row + s)
        q = s + first_row - lag
        if 0 <= q < total_rows:
            first(q)
        q -= lag
        if 0 <= q < total_rows:
            second(q)
        done = q - 2 * side
        if done >= 0 and done % side == 2 and done // side < tiles:
            at = pl.ds(done // side * side, side)
            out = pltpu.make_async_copy(es_ref.at[at], es_hbm.at[at], out_sem.at[done // side])
            out.start()
            outs.append(out)
            pick_tile(done // side)
        if done >= 0 and done % side in (4, 6) and done // side < tiles:
            merge_tile(done // side, 0 if done % side == 4 else 2)

    for k in range(3):
        xa_ref[k] = xs[first_row + (rows - 3) * core + k]
    for k in range(4):
        ha_ref[k] = hs[jnp.where(core == 0, 7, rows + 1) + k]
    ea_ref[0] = es_ref[jnp.where(core == 0, 3, rows - 4)]
    for out in outs:
        out.wait()


def border_kernel(
    rows,
    outer_ref,
    masks_ref,
    w1,
    w2,
    wm,
    xa_ref,
    ha_ref,
    ea_ref,
    mown_in,
    moth_in,
    es_in,
    es_hbm,
    mown_ref,
    moth_ref,
    x5,
    h7,
    e4,
    sem,
):
    core = lax.axis_index("chan")
    _, allc, cols = ea_ref.shape
    chans = allc // 2
    lanes = outer_ref.shape[1]
    tiles_r = masks_ref.shape[0]
    masks = masks_ref[...]
    top = core == 0
    turn4 = swap_matrix(HALO, chans)
    flat = HALO * chans
    pieces = [outer_ref[k * flat : (k + 1) * flat, :] for k in range(2 * cols // lanes)]
    oth, own = [
        mm(turn4, jnp.concatenate(pieces[n * cols // lanes : (n + 1) * cols // lanes], axis=1))
        for n in range(2)
    ]
    halo = [
        jnp.concatenate([p[r * chans : (r + 1) * chans] for p in (own, oth)], axis=0)
        for r in range(HALO)
    ]
    outer_mask = jnp.where(top, halo[0][0:1], halo[HALO - 1][0:1])
    tile_mask = jnp.where(top, masks[0:1], masks[tiles_r - 1 : tiles_r])
    for k in range(3):
        put(x5, jnp.where(top, k, k + 2), jnp.where(top, halo[k + 1], halo[k]), 1)
    for k in range(2):
        x5[jnp.where(top, k + 3, k)] = xa_ref[jnp.where(top, k, k + 1)]
    for k in range(4):
        h7[jnp.where(top, k + 3, k)] = ha_ref[k]
    y = [mm(w1[...], x5[k]) for k in range(5)]
    for k in range(3):
        total = y[k][:allc] + y[k + 1][allc : 2 * allc] + y[k + 2][2 * allc :]
        if k == 1:
            line = outer_mask
        else:
            line = jnp.where(top if k == 0 else core == 1, outer_mask, tile_mask)
        h = jnp.maximum(total * line, 0.0)
        put(h7, jnp.where(top, k, k + 4), h, 2)
    z = [mm(w2[...], h7[k]) for k in range(7)]
    e4[jnp.where(top, 3, 0)] = ea_ref[0]
    for k in range(3):
        total = z[k][:allc] + z[k + 2][allc : 2 * allc] + z[k + 4][2 * allc :]
        x = xa_ref[k, allc : 2 * allc, :].astype(F32)
        e4[jnp.where(top, k, k + 1)] = (tile_mask * (x + total)).astype(BF)
    copy = pltpu.make_async_copy(
        e4.at[pl.ds(core, 3)], es_hbm.at[pl.ds((rows - 3) * core, 3)], sem
    )
    copy.start()
    mown_ref[...] = mown_in[...]
    moth_ref[...] = moth_in[...]
    half = cols // 2
    parent_rows = mown_ref.shape[0]
    side = mown_ref.shape[1] // chans
    wide = half // side
    s = mm(e4[...].reshape(4 * allc, cols), pick_matrix(cols, side)).astype(BF)
    g = jnp.where(top, 0, 2 * parent_rows - 1)
    at_g = jnp.where(top, 0, parent_rows - 1)

    def rows_of(k):
        return s[k * 2 * allc : (k + 1) * 2 * allc]

    for n, piece in enumerate(merge_pairs(wm[...], rows_of, (0, 1), g * wide, half)):
        u = jnp.where(top, n, side - 2 + n)
        at_u = pl.ds(pl.multiple_of(u * chans, chans), chans)
        mown_ref[at_g, at_u, :] = piece[:chans].astype(BF)
        moth_ref[at_g, at_u, :] = piece[chans:].astype(BF)
    copy.wait()


def restore_kernel(es_hbm, after_hbm, enh_hbm, eoth_ref, es_ref, own, sem, in_sems):
    core = lax.axis_index("chan")
    rows, allc, cols = es_ref.shape
    chans = allc // 2
    copies = []
    for m in range(rows // BLK):
        at = pl.ds(m * BLK, BLK)
        copies.append(pltpu.make_async_copy(es_hbm.at[at], es_ref.at[at], in_sems.at[m]))
        copies[-1].start()
    turn = swap_matrix(BLK, BLK)
    for m in range(rows // BLK):
        copies[m].wait()
        at = m * BLK
        for c0 in range(0, allc, BLK):
            ref = own if c0 < chans else eoth_ref
            ch = c0 % chans
            block = es_ref[at : at + BLK, c0 : c0 + BLK, :].reshape(BLK * BLK, cols)
            ref[ch : ch + BLK, at : at + BLK, :] = mm(turn, block).astype(BF).reshape(BLK, BLK, cols)
    copy = pltpu.make_async_copy(
        own, enh_hbm.at[:, pl.ds(pl.multiple_of(core * rows, rows), rows), :], sem
    )
    copy.start()
    copy.wait()


def fill_kernel(recv_ref, held_hbm, enh_hbm, sem):
    core = lax.axis_index("chan")
    rows = recv_ref.shape[1]
    copy = pltpu.make_async_copy(
        recv_ref, enh_hbm.at[:, pl.ds(pl.multiple_of((1 - core) * rows, rows), rows), :], sem
    )
    copy.start()
    copy.wait()


def deal(now, width):
    n = len(now)
    group = div(iota(now[0].shape, 1), width)
    bit = 1
    while bit < n:
        odd = group & bit != 0
        now = [jnp.where(odd, now[(j + bit) % n], now[j]) for j in range(n)]
        bit *= 2
    return now


def pack_kernel(
    side, slots, owner_ref, mown_ref, mrecv_ref, out_ref, arr, lhs, mid, code_ref
):
    core, tile = lax.axis_index("chan"), lax.axis_index("tiles")
    count = owner_ref.shape[1]
    mine, rows, lanes = mown_ref.shape
    blocks, all_rows, _ = out_ref.shape
    per = side * slots
    wide = lanes // side
    for k in range(mine):
        arr[core * mine + k] = mown_ref[k]
        arr[(1 - core) * mine + k] = mrecv_ref[k]
    line = jnp.broadcast_to(owner_ref[...].astype(F32), (lanes, count))
    owner = jnp.transpose(line).astype(jnp.int32)
    is_owner = owner == iota((count, lanes), 1)
    marks = ones_where(is_owner)
    lower = ones_where(iota((count, count), 0) > iota((count, count), 1))
    earlier = mm(lower, marks)
    within = jnp.sum(jnp.where(is_owner, earlier, 0.0), axis=1, keepdims=True).astype(jnp.int32)
    if per == lanes:
        code = (owner * slots + within).astype(F32).astype(BF)
        code_ref[0:count, :] = code
        code_ref[count : 2 * count, :] = code

        def by_column(step, carry):
            at = pl.ds(pl.multiple_of(step * BLK, BLK), BLK)
            done = deal([arr[g, at, :] for g in range(side)], wide)
            for j in range(side):
                lhs[-j % side, at, :] = done[j]
            return carry

        lax.fori_loop(0, rows // BLK, by_column, 0, unroll=4)
        halves = blocks // side
        lane = iota((1, halves * lanes), 1)
        block, group, slot = div(lane, lanes), div(mod(lane, lanes), wide), mod(lane, wide)
        for i in range(side):
            v = lax.rem(i + side - lax.rem(tile, side), side)
            at = pl.multiple_of(count - wide * v, wide)
            codes = code_ref[pl.ds(at, count), :]
            want = (block * side + mod(group - i + side, side)) * slots + slot
            want = jnp.broadcast_to(want.astype(F32).astype(BF), (count, halves * lanes))
            same = jnp.concatenate([codes] * halves, axis=1) == want
            take = jnp.where(same, jnp.ones_like(want), jnp.zeros_like(want))
            got = mm(lhs[v], take).astype(BF)
            for h in range(halves):
                mid[h * side + i] = got[:, h * lanes : (h + 1) * lanes]
        for h in range(halves):

            def by_owner(step, carry, h=h):
                at = pl.ds(pl.multiple_of(step * BLK, BLK), BLK)
                done = deal([mid[h * side + i, at, :] for i in range(side)], wide)
                for j in range(side):
                    out_ref[h * side + -j % side, at, :] = done[j]
                return carry

            lax.fori_loop(0, rows // BLK, by_owner, 0, unroll=4)
        tally = mm(jnp.ones((all_rows - rows, count), BF), marks)
        for d in range(blocks):
            out_ref[d, rows:all_rows, :] = jnp.broadcast_to(
                tally[:, d : d + 1], (all_rows - rows, lanes)
            ).astype(BF)
    else:
        code = owner * per + within
        lane = iota((wide, lanes), 1)
        for g in range(2 * mine):
            for x in range(side):
                at = (g * side + x) * wide
                code_ref[at : at + wide, :] = (
                    code[g * wide : (g + 1) * wide] + (x - g) % side * slots
                )
        data = jnp.concatenate([arr[g] for g in range(2 * mine)], axis=1)
        lane = iota((count * side, lanes), 1)
        for step in range(0, blocks, 2):
            codes = code_ref[...]
            spots = [ones_where(codes == lane + at * lanes) for at in (step, step + 1)]
            total = mm(data, jnp.concatenate(spots, axis=1)).astype(BF)
            for n in range(2):
                at = step + n
                out_ref[at, 0:rows, :] = total[:, n * lanes : (n + 1) * lanes]
                goal = div(iota((count, lanes), 1) + at * lanes, per)
                tally = mm(jnp.ones((all_rows - rows, count), BF), ones_where(owner == goal))
                out_ref[at, rows:all_rows, :] = tally.astype(BF)


def targets(tallies, lanes, group, slots):
    lane0, lane1 = iota((lanes, lanes), 0), iota((lanes, lanes), 1)
    heads = mod(lane0, group) == 0
    before = ones_where(heads & (div(lane0, group) < div(lane1, group)))
    every = ones_where(heads)
    slot = mod(iota((1, lanes), 1), slots).astype(F32)
    running = jnp.zeros((1, lanes), F32)
    outs = []
    for tally in tallies:
        inside, whole = mm(tally, before)[0:1], mm(tally, every)[0:1]
        live = slot < tally.astype(F32)[0:1]
        outs.append(jnp.where(live, running + inside + slot, -1.0))
        running = running + whole
    return outs


def hits(target, room):
    shape = (room, target.shape[1])
    goal = iota(shape, 0).astype(F32).astype(BF)
    same = goal == jnp.broadcast_to(target.astype(BF), shape)
    return jnp.where(same, jnp.ones_like(goal), jnp.zeros_like(goal))


def unpack_kernel(side, slots, got_ref, out_ref, picked, data):
    tile = lax.axis_index("tiles")
    blocks, all_rows, lanes = got_ref.shape
    chans, cells, cap = out_ref.shape
    rows = side * chans
    per = side * slots
    room = picked.shape[2]
    if per == lanes:
        halves = blocks // side
        group = div(iota((all_rows - rows, lanes), 1), slots)
        tallies = []
        for h in range(halves):
            tally = got_ref[h * side, rows:all_rows, :].astype(F32)
            for s in range(1, side):
                other = got_ref[h * side + s, rows:all_rows, :].astype(F32)
                tally = jnp.where(group == s, other, tally)
            tallies.append(tally.astype(BF))
        spots = targets(tallies, lanes, slots, slots)
        for h in range(halves):

            def turn_rows(step, carry, h=h):
                at = pl.ds(pl.multiple_of(step * BLK, BLK), BLK)
                done = deal([got_ref[h * side + s, at, :] for s in range(side)], slots)
                for j in range(side):
                    data[h, j, at, :] = done[j]
                return carry

            lax.fori_loop(0, rows // BLK, turn_rows, 0, unroll=True)
        for j in range(side):
            v = lax.rem(2 * side - j - lax.rem(tile, side), side)
            left = jnp.concatenate([data[h, j] for h in range(halves)], axis=1)
            right = []
            for spot in spots:
                line = jnp.broadcast_to(spot, (side, lanes))
                line = pltpu.roll(line, (side - j) * slots, 1) if j else line
                right.append(hits(line[0:1], room))
            picked[v] = mm_nt(left, jnp.concatenate(right, axis=1)).astype(BF)
    else:
        tallies = [got_ref[b, rows:all_rows, :] for b in range(blocks)]
        spots = [hits(t, room) for t in targets(tallies, lanes, per, slots)]
        spots = jnp.concatenate(spots, axis=1)
        for v in range(side):
            keep = div(mod(iota((rows, lanes), 1), per), slots) == v
            left = jnp.concatenate(
                [jnp.where(keep, got_ref[b, 0:rows, :], jnp.zeros((rows, lanes), BF)) for b in range(blocks)],
                axis=1,
            )
            picked[v] = mm_nt(left, spots).astype(BF)
    two = BLK // side
    n = BLK * BLK
    row, col = iota((n, n), 0), iota((n, n), 1)
    turn = ones_where(
        (div(row, BLK) == mod(col, BLK))
        & (mod(div(row, side), two) == mod(div(col, BLK), two))
        & (mod(row, side) == div(col, BLK * two))
    )
    for u in range(0, side, two):
        for ch in range(0, chans, BLK):
            block = jnp.concatenate(
                [
                    picked[v, (u + w) * chans + ch : (u + w) * chans + ch + BLK, :]
                    for v in range(side)
                    for w in range(two)
                ],
                axis=0,
            )
            done = mm(turn, block).astype(BF).reshape(BLK, BLK, room)
            out_ref[ch : ch + BLK, u * side : (u + two) * side, :] = done[:, :, :cap]


def on_device(features, tile_valid, parent_owner, w_first, w_second, w_merge):
    chans, row_count, col_count = features.shape
    tile_rows, tile_cols = tile_valid.shape
    side = row_count // tile_rows
    parents_dev = parent_owner.shape[0]
    devices = lax.axis_size("tiles")
    slots = 2 * max(1, parents_dev // devices)
    own_cap = 3 * parents_dev // 2
    rows = row_count // 2
    allc = 2 * chans
    lanes = 128
    blocks = devices * slots * side // lanes
    fold = devices // blocks
    swap = [(0, 1), (1, 0)]
    vmem = pl.BlockSpec(memory_space=pltpu.VMEM)
    hbm = pl.BlockSpec(memory_space=pltpu.HBM)

    def limit(mib):
        return pltpu.CompilerParams(vmem_limit_bytes=int(mib * 1024) << 10)

    feat_oth = lax.ppermute(features, "chan", swap)
    flags = jnp.pad(tile_valid.astype(BF), ((0, chans - tile_rows), (0, allc - tile_cols)))
    extra = jnp.concatenate([w_first, w_second, jnp.swapaxes(w_merge, 1, 2), flags[None]], axis=0)
    extra_oth = lax.ppermute(extra, "chan", swap)
    edge_rows = chans * HALO * col_count // lanes
    send, keep = pl.pallas_call(
        functools.partial(edges_kernel, side, tile_rows, tile_cols),
        out_shape=(jax.ShapeDtypeStruct((edge_rows, lanes), BF),) * 2,
        in_specs=[hbm, vmem],
        out_specs=(vmem,) * 2,
        scratch_shapes=[
            pltpu.VMEM((2, chans, BLK, col_count), BF),
            pltpu.SemaphoreType.DMA((2,)),
        ],
        compiler_params=limit(52),
        name="edges",
    )(features, extra)
    sent = lax.ppermute(send, "chan", swap)
    cross = [(2 * t + 1, 2 * t + 2) for t in range(devices - 1)]
    cross += [(2 * t, 2 * t - 1) for t in range(1, devices)]
    outer = lax.ppermute(jnp.concatenate([keep, sent], axis=0), ("tiles", "chan"), cross)
    w1, w2, wm, masks = pl.pallas_call(
        functools.partial(weights_kernel, side, tile_cols),
        out_shape=(
            jax.ShapeDtypeStruct((3 * allc, 3 * allc), BF),
            jax.ShapeDtypeStruct((3 * allc, 3 * allc), BF),
            jax.ShapeDtypeStruct((allc, 4 * allc), BF),
            jax.ShapeDtypeStruct((tile_rows, col_count), F32),
        ),
        in_specs=[vmem, vmem],
        out_specs=(vmem,) * 4,
        compiler_params=limit(6),
        name="weights",
    )(extra, extra_oth)

    parent_rows = tile_rows // 4
    held_rows = rows * pl.cdiv(44 << 20, rows * allc * col_count * 2)
    es, m_own, m_oth, xa, ha, ea = pl.pallas_call(
        functools.partial(conv_kernel, side),
        out_shape=(
            jax.ShapeDtypeStruct((held_rows, allc, col_count), BF),
            jax.ShapeDtypeStruct((parent_rows, side * chans, col_count // 2), BF),
            jax.ShapeDtypeStruct((parent_rows, side * chans, col_count // 2), BF),
            jax.ShapeDtypeStruct((3, 3 * allc, col_count), BF),
            jax.ShapeDtypeStruct((4, 3 * allc, col_count), BF),
            jax.ShapeDtypeStruct((1, allc, col_count), BF),
        ),
        in_specs=[vmem] * 6,
        out_specs=(hbm,) + (vmem,) * 5,
        scratch_shapes=[
            pltpu.VMEM((rows + 16, 3 * allc, col_count), BF),
            pltpu.VMEM((rows + side, 3 * allc, col_count), BF),
            pltpu.VMEM((rows, allc, col_count), BF),
            pltpu.VMEM((tile_rows + 2 * side, col_count), F32),
            pltpu.VMEM((rows * allc, col_count), BF),
            pltpu.SemaphoreType.DMA((rows // side,)),
        ],
        compiler_params=limit(36),
        name="conv",
    )(features, feat_oth, masks, w1, w2, wm)
    es, m_own, m_oth = pl.pallas_call(
        functools.partial(border_kernel, rows),
        out_shape=(
            jax.ShapeDtypeStruct(es.shape, BF),
            jax.ShapeDtypeStruct((parent_rows, side * chans, col_count // 2), BF),
            jax.ShapeDtypeStruct((parent_rows, side * chans, col_count // 2), BF),
        ),
        in_specs=[vmem] * 10 + [hbm],
        out_specs=(hbm, vmem, vmem),
        scratch_shapes=[
            pltpu.VMEM((5, 3 * allc, col_count), BF),
            pltpu.VMEM((7, 3 * allc, col_count), BF),
            pltpu.VMEM((4, allc, col_count), BF),
            pltpu.SemaphoreType.DMA,
        ],
        input_output_aliases={10: 0},
        compiler_params=limit(16),
        name="border",
    )(outer, masks, w1, w2, wm, xa, ha, ea, m_own, m_oth, es)
    m_recv = lax.ppermute(m_oth, "chan", swap)
    all_rows = side * chans + 8
    packed = pl.pallas_call(
        functools.partial(pack_kernel, side, slots),
        out_shape=jax.ShapeDtypeStruct((blocks, all_rows, lanes), BF),
        in_specs=[vmem, vmem, vmem],
        out_specs=vmem,
        scratch_shapes=[
            pltpu.VMEM((2 * parent_rows, side * chans, lanes), BF),
            pltpu.VMEM((side, side * chans, lanes), BF),
            pltpu.VMEM((blocks, side * chans, lanes), BF),
            pltpu.VMEM((parents_dev * side, lanes), BF if fold == 1 else jnp.int32),
        ],
        compiler_params=limit(16),
        name="pack",
    )(parent_owner[None, :], m_own, m_recv)

    def to_peers(x):
        if fold > 1:
            x = x.reshape(blocks, all_rows, fold, lanes // fold)
            x = x.transpose(0, 2, 1, 3).reshape(devices, all_rows, lanes // fold)
        x = lax.all_to_all(x, "tiles", split_axis=0, concat_axis=0, tiled=True)
        if fold > 1:
            x = x.reshape(blocks, fold, all_rows, lanes // fold)
            x = x.transpose(0, 2, 1, 3).reshape(blocks, all_rows, lanes)
        return x

    got = to_peers(packed)
    held, e_oth = pl.pallas_call(
        restore_kernel,
        out_shape=(
            jax.ShapeDtypeStruct((chans, row_count, col_count), BF),
            jax.ShapeDtypeStruct((chans, rows, col_count), BF),
        ),
        in_specs=[hbm, hbm],
        out_specs=(hbm, vmem),
        scratch_shapes=[
            pltpu.VMEM((rows, allc, col_count), BF),
            pltpu.VMEM((chans, rows, col_count), BF),
            pltpu.SemaphoreType.DMA,
            pltpu.SemaphoreType.DMA((rows // BLK,)),
        ],
        compiler_params=limit(12),
        name="restore",
    )(es, packed)
    e_recv = lax.ppermute(e_oth, "chan", swap)
    enhanced = pl.pallas_call(
        fill_kernel,
        out_shape=jax.ShapeDtypeStruct((chans, row_count, col_count), BF),
        in_specs=[vmem, hbm],
        out_specs=hbm,
        scratch_shapes=[pltpu.SemaphoreType.DMA],
        input_output_aliases={1: 0},
        compiler_params=limit(6),
        name="fill",
    )(e_recv, held)
    room = pl.cdiv(own_cap, lanes) * lanes
    parents = pl.pallas_call(
        functools.partial(unpack_kernel, side, slots),
        out_shape=jax.ShapeDtypeStruct((chans, side * side, own_cap), BF),
        in_specs=[vmem],
        out_specs=vmem,
        scratch_shapes=[
            pltpu.VMEM((side, side * chans, room), BF),
            pltpu.VMEM((2, side, side * chans, lanes), BF),
        ],
        compiler_params=limit(24),
        name="unpack",
    )(got)
    return enhanced, jnp.swapaxes(parents, 1, 2)


def solution(mesh):
    return jax.shard_map(
        on_device,
        mesh=mesh,
        in_specs=(
            P("chan", "tiles", None),
            P("tiles", None),
            P("tiles"),
            P(None, "chan", None),
            P(None, "chan", None),
            P(None, None, "chan"),
        ),
        out_specs=(P("chan", "tiles", None), P("chan", "tiles", None)),
        check_vma=False,
    )
```

```python
import functools

import jax
import jax.numpy as jnp
from jax import lax
from jax.experimental import pallas as pl
from jax.experimental.pallas import tpu as pltpu
from jax.sharding import PartitionSpec as P


BF = jnp.bfloat16
F32 = jnp.float32
HALO = 4
BLK = 16


def iota(shape, dim):
    return lax.broadcasted_iota(jnp.int32, shape, dim)


def div(x, n):
    return x >> (n.bit_length() - 1) if n & (n - 1) == 0 else lax.div(x, jnp.int32(n))


def mod(x, n):
    return x & (n - 1) if n & (n - 1) == 0 else lax.rem(x, jnp.int32(n))


def ones_where(cond):
    return jnp.where(cond, 1.0, 0.0).astype(BF)


def mm(a, b):
    return jnp.dot(a, b, preferred_element_type=F32)


def mm_nt(a, b):
    return lax.dot_general(a, b, (((1,), (1,)), ((), ())), preferred_element_type=F32)


def swap_matrix(outer, inner):
    n = outer * inner
    row, col = iota((n, n), 0), iota((n, n), 1)
    return ones_where((mod(row, inner) == div(col, outer)) & (div(row, inner) == mod(col, outer)))


def shifted(x, amount):
    lanes = 128
    parts = [x[:, at : at + lanes] for at in range(0, x.shape[1], lanes)]
    turned = [pltpu.roll(p, amount % lanes, 1) for p in parts]
    lane = iota(parts[0].shape, 1)
    zero = jnp.zeros_like(parts[0])
    outs = []
    for n in range(len(parts)):
        if amount > 0:
            edge = turned[n - 1] if n else zero
            outs.append(jnp.where(lane < amount, edge, turned[n]))
        else:
            edge = turned[n + 1] if n + 1 < len(parts) else zero
            outs.append(jnp.where(lane >= lanes + amount, edge, turned[n]))
    return jnp.concatenate(outs, axis=1)


def widen_matrix(tiles_c, cols, side):
    return ones_where(div(iota((tiles_c, cols), 1), side) == iota((tiles_c, cols), 0))


def as_bf(x):
    return x.astype(F32).astype(BF)


def edges_kernel(side, feat_hbm, valid_ref, send_ref, keep_ref, masks_ref, edge, sems):
    core = lax.axis_index("chan")
    chans, feat_rows, cols = feat_hbm.shape
    copies = []
    for n, at in enumerate((0, feat_rows - BLK)):
        copy = pltpu.make_async_copy(feat_hbm.at[:, at : at + BLK, :], edge.at[n], sems.at[n])
        copy.start()
        copies.append(copy)
    flat = chans * HALO
    lanes = send_ref.shape[1]
    tiles_r, tiles_c = valid_ref.shape
    masks = mm(as_bf(valid_ref[...]), widen_matrix(tiles_c, cols, side))
    masks_ref[...] = masks
    row, col = iota((flat, chans * BLK), 0), iota((flat, chans * BLK), 1)
    same = div(row, HALO) == div(col, BLK)
    spot = mod(iota((flat, cols), 0), HALO)
    made = []
    for n in range(2):
        if n == 0:
            hit = same & (mod(row, HALO) == mod(col, BLK)) & (mod(row, HALO) < HALO - 1)
            flag, line = spot == HALO - 1, masks[0:1]
        else:
            hit = same & (mod(row, HALO) + BLK - HALO == mod(col, BLK)) & (mod(row, HALO) > 0)
            flag, line = spot == 0, masks[tiles_r - 1 : tiles_r]
        take = ones_where(hit)
        copies[n].wait()
        body = mm(take, edge[n].reshape(chans * BLK, cols))
        made.append(jnp.where(flag, jnp.broadcast_to(line, (flat, cols)), body).astype(BF))
    low = core == 0
    send = jnp.where(low, made[1], made[0])
    keep = jnp.where(low, made[0], made[1])
    for n in range(cols // lanes):
        send_ref[n * flat : (n + 1) * flat, :] = send[:, n * lanes : (n + 1) * lanes]
        keep_ref[n * flat : (n + 1) * flat, :] = keep[:, n * lanes : (n + 1) * lanes]


def weights_kernel(own_ref, oth_ref, w1_ref, w2_ref, wm_ref):
    core = lax.axis_index("chan")
    chans, allc = own_ref.shape[1:]

    def tap(k):
        return [ref[k] for ref in (own_ref, oth_ref)]

    for dst, base in ((w1_ref, 0), (w2_ref, 9)):
        total = None
        for b in range(3):
            tall = jnp.concatenate(sum([tap(base + 3 * a + b) for a in range(3)], []), axis=0)
            src, pos = iota((allc, 3 * allc), 0), iota((allc, 3 * allc), 1)
            place = ones_where(pos == b * allc + mod(src + chans * core, allc))
            part = mm(tall, place)
            total = part if total is None else total + part
        dst[...] = total.astype(BF)
    tall = jnp.concatenate(
        sum([tap(18 + 2 * a + b) for b in range(2) for a in range(2)], []), axis=0
    )
    order = ones_where(iota((allc, allc), 1) == mod(iota((allc, allc), 0) + chans * core, allc))
    wm_ref[...] = mm_nt(order, tall).astype(BF)


def put(dst, index, x, amount):
    allc = x.shape[0]
    dst[index, 0:allc, :] = shifted(x, amount).astype(BF)
    dst[index, allc : 2 * allc, :] = x.astype(BF)
    dst[index, 2 * allc : 3 * allc, :] = shifted(x, -amount).astype(BF)


def pick_matrix(cols, side):
    half = cols // 2
    wide = half // side
    lane = iota((cols, cols), 1)
    spot = mod(lane, half)
    want = 2 * (mod(spot, wide) * side + div(spot, wide)) + div(lane, half)
    return ones_where(iota((cols, cols), 0) == want)


def merge_pairs(wm, rows_of, pairs, turn, half):
    rhs = []
    for n in pairs:
        sp = rows_of(n)
        rhs.append(jnp.concatenate([sp[:, :half], sp[:, half:]], axis=0))
    both = mm(wm, jnp.concatenate(rhs, axis=1))
    return [pltpu.roll(both[:, n * half : (n + 1) * half], turn, 1) for n in range(2)]


def conv_kernel(
    side,
    own_ref,
    oth_ref,
    masks_ref,
    w1,
    w2,
    wm,
    es_hbm,
    mown_ref,
    moth_ref,
    xa_ref,
    ha_ref,
    ea_ref,
    xs,
    hs,
    es_ref,
    mask,
    picked,
    out_sem,
):
    core = lax.axis_index("chan")
    rows, allc, cols = es_ref.shape
    chans = allc // 2
    main = rows // BLK
    tiles_r = masks_ref.shape[0]
    mask[...] = jnp.zeros(mask.shape, F32)
    mask[pl.ds(side, tiles_r), :] = masks_ref[...]

    first_row = 5
    outer_start = jnp.where(core == 0, first_row - HALO, first_row + rows)
    for r in range(HALO):
        xs[outer_start + r] = jnp.zeros(xs.shape[1:], BF)
    zero_row = jnp.zeros(xs.shape[1:], BF)
    xs[0] = zero_row
    turn = swap_matrix(BLK, BLK)
    few = HALO * BLK
    row, col = iota((few, BLK * BLK), 0), iota((few, BLK * BLK), 1)
    turn_mid = ones_where(
        (mod(row, BLK) == div(col, BLK)) & (div(row, BLK) + (BLK - HALO) * core == mod(col, BLK))
    )
    half = cols // 2
    wide = half // side
    pick = pick_matrix(cols, side)
    base = side + core * (rows // side)
    tiles = rows // side

    def lay_block(m):
        at = rows - BLK * core if m == main else rows * core + BLK * m
        parts = []
        for ref in (own_ref, oth_ref):
            for ch in range(0, chans, BLK):
                block = ref[ch : ch + BLK, pl.ds(pl.multiple_of(at, BLK), BLK), :]
                parts.append(mm(turn_mid if m == main else turn, block.reshape(BLK * BLK, cols)))
        return parts

    def lay_row(parts, r, at):
        put(xs, at, jnp.concatenate([p[r * BLK : (r + 1) * BLK] for p in parts], axis=0), 1)

    mid_start = jnp.where(core == 0, first_row + rows, first_row - HALO)
    parts = lay_block(main)
    for r in range(HALO):
        lay_row(parts, r, mid_start + r)

    def line(k):
        return mask[pl.ds(base + k, 1), :]

    none = jnp.zeros((allc, cols), F32)
    first_sums = [none, none]
    second_sums = [[none, none], [none, none]]

    def first(q):
        pa, pb = first_sums
        y = mm(w1[...], xs[q])
        total = pa + y[2 * allc :]
        first_sums[:] = [pb + y[allc : 2 * allc], y[:allc]]
        h = jnp.maximum(total * line((q + 2) // side - 1), 0.0)
        put(hs, q, h.astype(BF), 2)

    def second(q):
        pa, pb = second_sums[q % 2]
        z = mm(w2[...], hs[q])
        total = pa + z[2 * allc :]
        second_sums[q % 2] = [pb + z[allc : 2 * allc], z[:allc]]
        if q >= side:
            x = xs[q - 3, allc : 2 * allc, :].astype(F32)
            es_ref[q - side] = (line(q // side - 1) * (x + total)).astype(BF)

    def pick_tile(tile):
        tall = es_ref[tile * side : (tile + 1) * side].reshape(side * allc, cols)
        picked[tile * side * allc : (tile + 1) * side * allc, :] = mm(tall, pick).astype(BF)

    def merge_tile(tile, k):
        g = tile // 2 + core * (rows // (2 * side))

        def rows_of(n):
            at = (tile * side + 2 * n) * allc
            return picked[at : at + 2 * allc, :]

        for n, piece in enumerate(merge_pairs(wm[...], rows_of, (k, k + 1), g * wide, half)):
            u = (side // 2) * (tile % 2) + k + n
            mown_ref[tile // 2, u * chans : (u + 1) * chans, :] = piece[:chans].astype(BF)
            moth_ref[tile // 2, u * chans : (u + 1) * chans, :] = piece[chans:].astype(BF)

    outs = []
    lag = 4
    total_rows = rows + side
    for s in range(-1, total_rows + 3 * lag + 2 * side):
        if 0 <= s < rows:
            if s % BLK == 0:
                parts = lay_block(s // BLK)
            lay_row(parts, s % BLK, first_row + s)
        q = s + first_row - lag
        if 0 <= q < total_rows:
            first(q)
        q -= lag
        if 0 <= q < total_rows:
            second(q)
        done = q - 2 * side
        if done >= 0 and done % side == 2 and done // side < tiles:
            at = pl.ds(done // side * side, side)
            out = pltpu.make_async_copy(es_ref.at[at], es_hbm.at[at], out_sem.at[done // side])
            out.start()
            outs.append(out)
            pick_tile(done // side)
        if done >= 0 and done % side in (4, 6) and done // side < tiles:
            merge_tile(done // side, 0 if done % side == 4 else 2)

    for k in range(3):
        xa_ref[k] = xs[first_row + (rows - 3) * core + k]
    for k in range(4):
        ha_ref[k] = hs[jnp.where(core == 0, 7, rows + 1) + k]
    ea_ref[0] = es_ref[jnp.where(core == 0, 3, rows - 4)]
    for out in outs:
        out.wait()


def border_kernel(
    rows,
    devices,
    outer_ref,
    masks_ref,
    w1,
    w2,
    wm,
    xa_ref,
    ha_ref,
    ea_ref,
    mown_in,
    moth_in,
    es_in,
    es_hbm,
    mown_ref,
    moth_ref,
    x5,
    h7,
    e4,
    sem,
):
    core = lax.axis_index("chan")
    _, allc, cols = ea_ref.shape
    chans = allc // 2
    lanes = outer_ref.shape[1]
    tiles_r = masks_ref.shape[0]
    masks = masks_ref[...]
    top = core == 0
    turn4 = swap_matrix(HALO, chans)
    flat = HALO * chans
    pieces = [outer_ref[k * flat : (k + 1) * flat, :] for k in range(2 * cols // lanes)]
    oth, own = [
        mm(turn4, jnp.concatenate(pieces[n * cols // lanes : (n + 1) * cols // lanes], axis=1))
        for n in range(2)
    ]
    place = lax.axis_index("tiles")
    inside = place != jnp.where(top, 0, devices - 1)
    own, oth = jnp.where(inside, own, 0.0), jnp.where(inside, oth, 0.0)
    halo = [
        jnp.concatenate([p[r * chans : (r + 1) * chans] for p in (own, oth)], axis=0)
        for r in range(HALO)
    ]
    outer_mask = jnp.where(top, halo[0][0:1], halo[HALO - 1][0:1])
    tile_mask = jnp.where(top, masks[0:1], masks[tiles_r - 1 : tiles_r])
    for k in range(3):
        put(x5, jnp.where(top, k, k + 2), jnp.where(top, halo[k + 1], halo[k]), 1)
    for k in range(2):
        x5[jnp.where(top, k + 3, k)] = xa_ref[jnp.where(top, k, k + 1)]
    for k in range(4):
        h7[jnp.where(top, k + 3, k)] = ha_ref[k]
    y = [mm(w1[...], x5[k]) for k in range(5)]
    for k in range(3):
        total = y[k][:allc] + y[k + 1][allc : 2 * allc] + y[k + 2][2 * allc :]
        if k == 1:
            line = outer_mask
        else:
            line = jnp.where(top if k == 0 else core == 1, outer_mask, tile_mask)
        h = jnp.maximum(total * line, 0.0)
        put(h7, jnp.where(top, k, k + 4), h, 2)
    z = [mm(w2[...], h7[k]) for k in range(7)]
    e4[jnp.where(top, 3, 0)] = ea_ref[0]
    for k in range(3):
        total = z[k][:allc] + z[k + 2][allc : 2 * allc] + z[k + 4][2 * allc :]
        x = xa_ref[k, allc : 2 * allc, :].astype(F32)
        e4[jnp.where(top, k, k + 1)] = (tile_mask * (x + total)).astype(BF)
    copy = pltpu.make_async_copy(
        e4.at[pl.ds(core, 3)], es_hbm.at[pl.ds((rows - 3) * core, 3)], sem
    )
    copy.start()
    mown_ref[...] = mown_in[...]
    moth_ref[...] = moth_in[...]
    half = cols // 2
    parent_rows = mown_ref.shape[0]
    side = mown_ref.shape[1] // chans
    wide = half // side
    s = mm(e4[...].reshape(4 * allc, cols), pick_matrix(cols, side)).astype(BF)
    g = jnp.where(top, 0, 2 * parent_rows - 1)
    at_g = jnp.where(top, 0, parent_rows - 1)

    def rows_of(k):
        return s[k * 2 * allc : (k + 1) * 2 * allc]

    for n, piece in enumerate(merge_pairs(wm[...], rows_of, (0, 1), g * wide, half)):
        u = jnp.where(top, n, side - 2 + n)
        at_u = pl.ds(pl.multiple_of(u * chans, chans), chans)
        mown_ref[at_g, at_u, :] = piece[:chans].astype(BF)
        moth_ref[at_g, at_u, :] = piece[chans:].astype(BF)
    copy.wait()


def restore_kernel(es_hbm, after_hbm, enh_hbm, eoth_ref, es_ref, own, sem, in_sems):
    core = lax.axis_index("chan")
    rows, allc, cols = es_ref.shape
    chans = allc // 2
    copies = []
    for m in range(rows // BLK):
        at = pl.ds(m * BLK, BLK)
        copies.append(pltpu.make_async_copy(es_hbm.at[at], es_ref.at[at], in_sems.at[m]))
        copies[-1].start()
    turn = swap_matrix(BLK, BLK)
    for m in range(rows // BLK):
        copies[m].wait()
        at = m * BLK
        for c0 in range(0, allc, BLK):
            ref = own if c0 < chans else eoth_ref
            ch = c0 % chans
            block = es_ref[at : at + BLK, c0 : c0 + BLK, :].reshape(BLK * BLK, cols)
            ref[ch : ch + BLK, at : at + BLK, :] = mm(turn, block).astype(BF).reshape(BLK, BLK, cols)
    copy = pltpu.make_async_copy(
        own, enh_hbm.at[:, pl.ds(pl.multiple_of(core * rows, rows), rows), :], sem
    )
    copy.start()
    copy.wait()


def fill_kernel(recv_ref, held_hbm, enh_hbm, sem):
    core = lax.axis_index("chan")
    rows = recv_ref.shape[1]
    copy = pltpu.make_async_copy(
        recv_ref, enh_hbm.at[:, pl.ds(pl.multiple_of((1 - core) * rows, rows), rows), :], sem
    )
    copy.start()
    copy.wait()


def deal(now, width):
    n = len(now)
    group = div(iota(now[0].shape, 1), width)
    bit = 1
    while bit < n:
        odd = group & bit != 0
        now = [jnp.where(odd, now[(j + bit) % n], now[j]) for j in range(n)]
        bit *= 2
    return now


def pack_kernel(
    side, slots, owner_ref, mown_ref, mrecv_ref, out_ref, arr, lhs, mid, code_ref
):
    core, tile = lax.axis_index("chan"), lax.axis_index("tiles")
    count = owner_ref.shape[1]
    mine, rows, lanes = mown_ref.shape
    blocks, all_rows, _ = out_ref.shape
    per = side * slots
    wide = lanes // side
    for k in range(mine):
        arr[core * mine + k] = mown_ref[k]
        arr[(1 - core) * mine + k] = mrecv_ref[k]
    line = jnp.broadcast_to(owner_ref[...].astype(F32), (lanes, count))
    owner = jnp.transpose(line).astype(jnp.int32)
    is_owner = owner == iota((count, lanes), 1)
    marks = ones_where(is_owner)
    lower = ones_where(iota((count, count), 0) > iota((count, count), 1))
    earlier = mm(lower, marks)
    within = jnp.sum(jnp.where(is_owner, earlier, 0.0), axis=1, keepdims=True).astype(jnp.int32)
    if per == lanes:
        code = (owner * slots + within).astype(F32).astype(BF)
        code_ref[0:count, :] = code
        code_ref[count : 2 * count, :] = code

        def by_column(step, carry):
            at = pl.ds(pl.multiple_of(step * BLK, BLK), BLK)
            done = deal([arr[g, at, :] for g in range(side)], wide)
            for j in range(side):
                lhs[-j % side, at, :] = done[j]
            return carry

        lax.fori_loop(0, rows // BLK, by_column, 0, unroll=4)
        halves = blocks // side
        lane = iota((1, halves * lanes), 1)
        block, group, slot = div(lane, lanes), div(mod(lane, lanes), wide), mod(lane, wide)
        for i in range(side):
            v = lax.rem(i + side - lax.rem(tile, side), side)
            at = pl.multiple_of(count - wide * v, wide)
            codes = code_ref[pl.ds(at, count), :]
            want = (block * side + mod(group - i + side, side)) * slots + slot
            want = jnp.broadcast_to(want.astype(F32).astype(BF), (count, halves * lanes))
            same = jnp.concatenate([codes] * halves, axis=1) == want
            take = jnp.where(same, jnp.ones_like(want), jnp.zeros_like(want))
            got = mm(lhs[v], take).astype(BF)
            for h in range(halves):
                mid[h * side + i] = got[:, h * lanes : (h + 1) * lanes]
        for h in range(halves):

            def by_owner(step, carry, h=h):
                at = pl.ds(pl.multiple_of(step * BLK, BLK), BLK)
                done = deal([mid[h * side + i, at, :] for i in range(side)], wide)
                for j in range(side):
                    out_ref[h * side + -j % side, at, :] = done[j]
                return carry

            lax.fori_loop(0, rows // BLK, by_owner, 0, unroll=4)
        tally = mm(jnp.ones((all_rows - rows, count), BF), marks)
        for d in range(blocks):
            out_ref[d, rows:all_rows, :] = jnp.broadcast_to(
                tally[:, d : d + 1], (all_rows - rows, lanes)
            ).astype(BF)
    else:
        code = owner * per + within
        lane = iota((wide, lanes), 1)
        for g in range(2 * mine):
            for x in range(side):
                at = (g * side + x) * wide
                code_ref[at : at + wide, :] = (
                    code[g * wide : (g + 1) * wide] + (x - g) % side * slots
                )
        data = jnp.concatenate([arr[g] for g in range(2 * mine)], axis=1)
        lane = iota((count * side, lanes), 1)
        for step in range(0, blocks, 2):
            codes = code_ref[...]
            spots = [ones_where(codes == lane + at * lanes) for at in (step, step + 1)]
            total = mm(data, jnp.concatenate(spots, axis=1)).astype(BF)
            for n in range(2):
                at = step + n
                out_ref[at, 0:rows, :] = total[:, n * lanes : (n + 1) * lanes]
                goal = div(iota((count, lanes), 1) + at * lanes, per)
                tally = mm(jnp.ones((all_rows - rows, count), BF), ones_where(owner == goal))
                out_ref[at, rows:all_rows, :] = tally.astype(BF)


def targets(tallies, lanes, group, slots):
    lane0, lane1 = iota((lanes, lanes), 0), iota((lanes, lanes), 1)
    heads = mod(lane0, group) == 0
    before = ones_where(heads & (div(lane0, group) < div(lane1, group)))
    every = ones_where(heads)
    slot = mod(iota((1, lanes), 1), slots).astype(F32)
    running = jnp.zeros((1, lanes), F32)
    outs = []
    for tally in tallies:
        inside, whole = mm(tally, before)[0:1], mm(tally, every)[0:1]
        live = slot < tally.astype(F32)[0:1]
        outs.append(jnp.where(live, running + inside + slot, -1.0))
        running = running + whole
    return outs


def hits(target, room):
    shape = (room, target.shape[1])
    goal = iota(shape, 0).astype(F32).astype(BF)
    same = goal == jnp.broadcast_to(target.astype(BF), shape)
    return jnp.where(same, jnp.ones_like(goal), jnp.zeros_like(goal))


def unpack_kernel(side, slots, got_ref, out_ref, picked, data):
    tile = lax.axis_index("tiles")
    blocks, all_rows, lanes = got_ref.shape
    chans, _, cap = out_ref.shape
    rows = side * chans
    per = side * slots
    room = picked.shape[2]
    if per == lanes:
        halves = blocks // side
        group = div(iota((all_rows - rows, lanes), 1), slots)
        tallies = []
        for h in range(halves):
            tally = got_ref[h * side, rows:all_rows, :].astype(F32)
            for s in range(1, side):
                other = got_ref[h * side + s, rows:all_rows, :].astype(F32)
                tally = jnp.where(group == s, other, tally)
            tallies.append(tally.astype(BF))
        spots = targets(tallies, lanes, slots, slots)
        for h in range(halves):

            def turn_rows(step, carry, h=h):
                at = pl.ds(pl.multiple_of(step * BLK, BLK), BLK)
                done = deal([got_ref[h * side + s, at, :] for s in range(side)], slots)
                for j in range(side):
                    data[h, j, at, :] = done[j]
                return carry

            lax.fori_loop(0, rows // BLK, turn_rows, 0, unroll=True)
        for j in range(side):
            v = lax.rem(2 * side - j - lax.rem(tile, side), side)
            left = jnp.concatenate([data[h, j] for h in range(halves)], axis=1)
            right = []
            for spot in spots:
                line = jnp.broadcast_to(spot, (side, lanes))
                line = pltpu.roll(line, (side - j) * slots, 1) if j else line
                right.append(hits(line[0:1], room))
            picked[v] = mm_nt(left, jnp.concatenate(right, axis=1)).astype(BF)
    else:
        tallies = [got_ref[b, rows:all_rows, :] for b in range(blocks)]
        spots = [hits(t, room) for t in targets(tallies, lanes, per, slots)]
        spots = jnp.concatenate(spots, axis=1)
        for v in range(side):
            keep = div(mod(iota((rows, lanes), 1), per), slots) == v
            left = jnp.concatenate(
                [jnp.where(keep, got_ref[b, 0:rows, :], jnp.zeros((rows, lanes), BF)) for b in range(blocks)],
                axis=1,
            )
            picked[v] = mm_nt(left, spots).astype(BF)
    two = BLK // side
    n = BLK * BLK
    row, col = iota((n, n), 0), iota((n, n), 1)
    turn = ones_where(
        (div(row, BLK) == mod(col, BLK))
        & (mod(div(row, side), two) == mod(div(col, BLK), two))
        & (mod(row, side) == div(col, BLK * two))
    )
    for u in range(0, side, two):
        for ch in range(0, chans, BLK):
            block = jnp.concatenate(
                [
                    picked[v, (u + w) * chans + ch : (u + w) * chans + ch + BLK, :]
                    for v in range(side)
                    for w in range(two)
                ],
                axis=0,
            )
            done = mm(turn, block).astype(BF).reshape(BLK, BLK, room)
            out_ref[ch : ch + BLK, u * side : (u + two) * side, :] = done[:, :, :cap]


def on_device(features, tile_valid, parent_owner, w_first, w_second, w_merge):
    chans, row_count, col_count = features.shape
    tile_rows, _ = tile_valid.shape
    side = row_count // tile_rows
    parents_dev = parent_owner.shape[0]
    devices = lax.axis_size("tiles")
    slots = 2 * max(1, parents_dev // devices)
    own_cap = 3 * parents_dev // 2
    rows = row_count // 2
    allc = 2 * chans
    lanes = 128
    blocks = devices * slots * side // lanes
    fold = devices // blocks
    swap = [(0, 1), (1, 0)]
    vmem = pl.BlockSpec(memory_space=pltpu.VMEM)
    hbm = pl.BlockSpec(memory_space=pltpu.HBM)

    def limit(mib):
        return pltpu.CompilerParams(vmem_limit_bytes=int(mib * 1024) << 10)

    feat_oth = lax.ppermute(features, "chan", swap)
    edge_rows = chans * HALO * col_count // lanes
    send, keep, masks = pl.pallas_call(
        functools.partial(edges_kernel, side),
        out_shape=(
            jax.ShapeDtypeStruct((edge_rows, lanes), BF),
            jax.ShapeDtypeStruct((edge_rows, lanes), BF),
            jax.ShapeDtypeStruct((tile_rows, col_count), F32),
        ),
        in_specs=[hbm, vmem],
        out_specs=(vmem,) * 3,
        scratch_shapes=[
            pltpu.VMEM((2, chans, BLK, col_count), BF),
            pltpu.SemaphoreType.DMA((2,)),
        ],
        compiler_params=limit(52),
        name="edges",
    )(features, tile_valid)
    sent = lax.ppermute(send, "chan", swap)
    extra = jnp.concatenate(
        [w_first, w_second, jnp.swapaxes(w_merge, 1, 2), send[None, :chans, :allc]], axis=0
    )
    extra_oth = lax.ppermute(extra, "chan", swap)
    ends = 2 * devices - 1
    cross = [(2 * t + 1, 2 * t + 2) for t in range(devices - 1)] + [(ends, 0)]
    cross += [(2 * t, 2 * t - 1) for t in range(1, devices)] + [(0, ends)]
    payload = jnp.concatenate([keep, sent], axis=0)
    outer = lax.ppermute(payload, ("tiles", "chan"), cross)
    w1, w2, wm = pl.pallas_call(
        weights_kernel,
        out_shape=(
            jax.ShapeDtypeStruct((3 * allc, 3 * allc), BF),
            jax.ShapeDtypeStruct((3 * allc, 3 * allc), BF),
            jax.ShapeDtypeStruct((allc, 4 * allc), BF),
        ),
        in_specs=[vmem, vmem],
        out_specs=(vmem,) * 3,
        compiler_params=limit(6),
        name="weights",
    )(extra, extra_oth)

    parent_rows = tile_rows // 4
    held_rows = rows * pl.cdiv(44 << 20, rows * allc * col_count * 2)
    es, m_own, m_oth, xa, ha, ea = pl.pallas_call(
        functools.partial(conv_kernel, side),
        out_shape=(
            jax.ShapeDtypeStruct((held_rows, allc, col_count), BF),
            jax.ShapeDtypeStruct((parent_rows, side * chans, col_count // 2), BF),
            jax.ShapeDtypeStruct((parent_rows, side * chans, col_count // 2), BF),
            jax.ShapeDtypeStruct((3, 3 * allc, col_count), BF),
            jax.ShapeDtypeStruct((4, 3 * allc, col_count), BF),
            jax.ShapeDtypeStruct((1, allc, col_count), BF),
        ),
        in_specs=[vmem] * 6,
        out_specs=(hbm,) + (vmem,) * 5,
        scratch_shapes=[
            pltpu.VMEM((rows + 16, 3 * allc, col_count), BF),
            pltpu.VMEM((rows + side, 3 * allc, col_count), BF),
            pltpu.VMEM((rows, allc, col_count), BF),
            pltpu.VMEM((tile_rows + 2 * side, col_count), F32),
            pltpu.VMEM((rows * allc, col_count), BF),
            pltpu.SemaphoreType.DMA((rows // side,)),
        ],
        compiler_params=limit(36),
        name="conv",
    )(features, feat_oth, masks, w1, w2, wm)
    es, m_own, m_oth = pl.pallas_call(
        functools.partial(border_kernel, rows, devices),
        out_shape=(
            jax.ShapeDtypeStruct(es.shape, BF),
            jax.ShapeDtypeStruct((parent_rows, side * chans, col_count // 2), BF),
            jax.ShapeDtypeStruct((parent_rows, side * chans, col_count // 2), BF),
        ),
        in_specs=[vmem] * 10 + [hbm],
        out_specs=(hbm, vmem, vmem),
        scratch_shapes=[
            pltpu.VMEM((5, 3 * allc, col_count), BF),
            pltpu.VMEM((7, 3 * allc, col_count), BF),
            pltpu.VMEM((4, allc, col_count), BF),
            pltpu.SemaphoreType.DMA,
        ],
        input_output_aliases={10: 0},
        compiler_params=limit(16),
        name="border",
    )(outer, masks, w1, w2, wm, xa, ha, ea, m_own, m_oth, es)
    m_recv = lax.ppermute(m_oth, "chan", swap)
    all_rows = side * chans + 8
    packed = pl.pallas_call(
        functools.partial(pack_kernel, side, slots),
        out_shape=jax.ShapeDtypeStruct((blocks, all_rows, lanes), BF),
        in_specs=[vmem, vmem, vmem],
        out_specs=vmem,
        scratch_shapes=[
            pltpu.VMEM((2 * parent_rows, side * chans, lanes), BF),
            pltpu.VMEM((side, side * chans, lanes), BF),
            pltpu.VMEM((blocks, side * chans, lanes), BF),
            pltpu.VMEM((parents_dev * side, lanes), BF if fold == 1 else jnp.int32),
        ],
        compiler_params=limit(16),
        name="pack",
    )(parent_owner[None, :], m_own, m_recv)

    def to_peers(x):
        if fold > 1:
            x = x.reshape(blocks, all_rows, fold, lanes // fold)
            x = x.transpose(0, 2, 1, 3).reshape(devices, all_rows, lanes // fold)
        x = lax.all_to_all(x, "tiles", split_axis=0, concat_axis=0, tiled=True)
        if fold > 1:
            x = x.reshape(blocks, fold, all_rows, lanes // fold)
            x = x.transpose(0, 2, 1, 3).reshape(blocks, all_rows, lanes)
        return x

    got = to_peers(packed)
    held, e_oth = pl.pallas_call(
        restore_kernel,
        out_shape=(
            jax.ShapeDtypeStruct((chans, row_count, col_count), BF),
            jax.ShapeDtypeStruct((chans, rows, col_count), BF),
        ),
        in_specs=[hbm, hbm],
        out_specs=(hbm, vmem),
        scratch_shapes=[
            pltpu.VMEM((rows, allc, col_count), BF),
            pltpu.VMEM((chans, rows, col_count), BF),
            pltpu.SemaphoreType.DMA,
            pltpu.SemaphoreType.DMA((rows // BLK,)),
        ],
        compiler_params=limit(12),
        name="restore",
    )(es, packed)
    e_recv = lax.ppermute(e_oth, "chan", swap)
    enhanced = pl.pallas_call(
        fill_kernel,
        out_shape=jax.ShapeDtypeStruct((chans, row_count, col_count), BF),
        in_specs=[vmem, hbm],
        out_specs=hbm,
        scratch_shapes=[pltpu.SemaphoreType.DMA],
        input_output_aliases={1: 0},
        compiler_params=limit(6),
        name="fill",
    )(e_recv, held)
    room = pl.cdiv(own_cap, lanes) * lanes
    parents = pl.pallas_call(
        functools.partial(unpack_kernel, side, slots),
        out_shape=jax.ShapeDtypeStruct((chans, side * side, own_cap), BF),
        in_specs=[vmem],
        out_specs=vmem,
        scratch_shapes=[
            pltpu.VMEM((side, side * chans, room), BF),
            pltpu.VMEM((2, side, side * chans, lanes), BF),
        ],
        compiler_params=limit(24),
        name="unpack",
    )(got)
    return enhanced, jnp.swapaxes(parents, 1, 2)


def solution(mesh):
    return jax.shard_map(
        on_device,
        mesh=mesh,
        in_specs=(
            P("chan", "tiles", None),
            P("tiles", None),
            P("tiles"),
            P(None, "chan", None),
            P(None, "chan", None),
            P(None, None, "chan"),
        ),
        out_specs=(P("chan", "tiles", None), P("chan", "tiles", None)),
        check_vma=False,
    )
```

```python
import functools

import jax
import jax.numpy as jnp
from jax import lax
from jax.experimental import pallas as pl
from jax.experimental.pallas import tpu as pltpu
from jax.sharding import PartitionSpec as P


BF = jnp.bfloat16
F32 = jnp.float32
HALO = 4
BLK = 16


def iota(shape, dim):
    return lax.broadcasted_iota(jnp.int32, shape, dim)


def div(x, n):
    return x >> (n.bit_length() - 1) if n & (n - 1) == 0 else lax.div(x, jnp.int32(n))


def mod(x, n):
    return x & (n - 1) if n & (n - 1) == 0 else lax.rem(x, jnp.int32(n))


def ones_where(cond):
    return jnp.where(cond, 1.0, 0.0).astype(BF)


def mm(a, b):
    return jnp.dot(a, b, preferred_element_type=F32)


def mm_nt(a, b):
    return lax.dot_general(a, b, (((1,), (1,)), ((), ())), preferred_element_type=F32)


def swap_matrix(outer, inner):
    n = outer * inner
    row, col = iota((n, n), 0), iota((n, n), 1)
    return ones_where((mod(row, inner) == div(col, outer)) & (div(row, inner) == mod(col, outer)))


def shifted(x, amount):
    lanes = 128
    parts = [x[:, at : at + lanes] for at in range(0, x.shape[1], lanes)]
    turned = [pltpu.roll(p, amount % lanes, 1) for p in parts]
    lane = iota(parts[0].shape, 1)
    zero = jnp.zeros_like(parts[0])
    outs = []
    for n in range(len(parts)):
        if amount > 0:
            edge = turned[n - 1] if n else zero
            outs.append(jnp.where(lane < amount, edge, turned[n]))
        else:
            edge = turned[n + 1] if n + 1 < len(parts) else zero
            outs.append(jnp.where(lane >= lanes + amount, edge, turned[n]))
    return jnp.concatenate(outs, axis=1)


def widen_matrix(tiles_c, cols, side):
    return ones_where(div(iota((tiles_c, cols), 1), side) == iota((tiles_c, cols), 0))


def as_bf(x):
    return x.astype(F32).astype(BF)


def edges_kernel(side, feat_hbm, valid_ref, send_ref, keep_ref, masks_ref, edge, sems):
    core = lax.axis_index("chan")
    chans, feat_rows, cols = feat_hbm.shape
    copies = []
    for n, at in enumerate((0, feat_rows - BLK)):
        copy = pltpu.make_async_copy(feat_hbm.at[:, at : at + BLK, :], edge.at[n], sems.at[n])
        copy.start()
        copies.append(copy)
    flat = chans * HALO
    lanes = send_ref.shape[1]
    tiles_r, tiles_c = valid_ref.shape
    masks = mm(as_bf(valid_ref[...]), widen_matrix(tiles_c, cols, side))
    masks_ref[...] = masks
    row, col = iota((flat, chans * BLK), 0), iota((flat, chans * BLK), 1)
    same = div(row, HALO) == div(col, BLK)
    spot = mod(iota((flat, cols), 0), HALO)
    made = []
    for n in range(2):
        if n == 0:
            hit = same & (mod(row, HALO) == mod(col, BLK)) & (mod(row, HALO) < HALO - 1)
            flag, line = spot == HALO - 1, masks[0:1]
        else:
            hit = same & (mod(row, HALO) + BLK - HALO == mod(col, BLK)) & (mod(row, HALO) > 0)
            flag, line = spot == 0, masks[tiles_r - 1 : tiles_r]
        take = ones_where(hit)
        copies[n].wait()
        body = mm(take, edge[n].reshape(chans * BLK, cols))
        made.append(jnp.where(flag, jnp.broadcast_to(line, (flat, cols)), body).astype(BF))
    low = core == 0
    send = jnp.where(low, made[1], made[0])
    keep = jnp.where(low, made[0], made[1])
    for n in range(cols // lanes):
        send_ref[n * flat : (n + 1) * flat, :] = send[:, n * lanes : (n + 1) * lanes]
        keep_ref[n * flat : (n + 1) * flat, :] = keep[:, n * lanes : (n + 1) * lanes]


def weights_kernel(own_ref, oth_ref, w1_ref, w2_ref, wm_ref):
    core = lax.axis_index("chan")
    chans, allc = own_ref.shape[1:]

    def tap(k):
        return [ref[k] for ref in (own_ref, oth_ref)]

    for dst, base in ((w1_ref, 0), (w2_ref, 9)):
        total = None
        for b in range(3):
            tall = jnp.concatenate(sum([tap(base + 3 * a + b) for a in range(3)], []), axis=0)
            src, pos = iota((allc, 3 * allc), 0), iota((allc, 3 * allc), 1)
            place = ones_where(pos == b * allc + mod(src + chans * core, allc))
            part = mm(tall, place)
            total = part if total is None else total + part
        dst[...] = total.astype(BF)
    tall = jnp.concatenate(
        sum([tap(18 + 2 * a + b) for b in range(2) for a in range(2)], []), axis=0
    )
    order = ones_where(iota((allc, allc), 1) == mod(iota((allc, allc), 0) + chans * core, allc))
    wm_ref[...] = mm_nt(order, tall).astype(BF)


def put(dst, index, x, amount):
    allc = x.shape[0]
    dst[index, 0:allc, :] = shifted(x, amount).astype(BF)
    dst[index, allc : 2 * allc, :] = x.astype(BF)
    dst[index, 2 * allc : 3 * allc, :] = shifted(x, -amount).astype(BF)


def pick_matrix(cols, side):
    half = cols // 2
    wide = half // side
    lane = iota((cols, cols), 1)
    spot = mod(lane, half)
    want = 2 * (mod(spot, wide) * side + div(spot, wide)) + div(lane, half)
    return ones_where(iota((cols, cols), 0) == want)


def merge_pairs(wm, rows_of, pairs, turn, half):
    rhs = []
    for n in pairs:
        sp = rows_of(n)
        rhs.append(jnp.concatenate([sp[:, :half], sp[:, half:]], axis=0))
    both = mm(wm, jnp.concatenate(rhs, axis=1))
    return [pltpu.roll(both[:, n * half : (n + 1) * half], turn, 1) for n in range(2)]


def conv_kernel(
    side,
    own_ref,
    oth_ref,
    masks_ref,
    w1,
    w2,
    wm,
    es_hbm,
    mown_ref,
    moth_ref,
    xa_ref,
    ha_ref,
    ea_ref,
    xs,
    hs,
    es_ref,
    mask,
    picked,
    out_sem,
):
    core = lax.axis_index("chan")
    rows, allc, cols = es_ref.shape
    chans = allc // 2
    main = rows // BLK
    tiles_r = masks_ref.shape[0]
    mask[...] = jnp.zeros(mask.shape, F32)
    mask[pl.ds(side, tiles_r), :] = masks_ref[...]

    first_row = 5
    outer_start = jnp.where(core == 0, first_row - HALO, first_row + rows)
    for r in range(HALO):
        xs[outer_start + r] = jnp.zeros(xs.shape[1:], BF)
    zero_row = jnp.zeros(xs.shape[1:], BF)
    xs[0] = zero_row
    turn = swap_matrix(BLK, BLK)
    few = HALO * BLK
    row, col = iota((few, BLK * BLK), 0), iota((few, BLK * BLK), 1)
    turn_mid = ones_where(
        (mod(row, BLK) == div(col, BLK)) & (div(row, BLK) + (BLK - HALO) * core == mod(col, BLK))
    )
    half = cols // 2
    wide = half // side
    pick = pick_matrix(cols, side)
    base = side + core * (rows // side)
    tiles = rows // side

    def lay_block(m):
        at = rows - BLK * core if m == main else rows * core + BLK * m
        parts = []
        for ref in (own_ref, oth_ref):
            for ch in range(0, chans, BLK):
                block = ref[ch : ch + BLK, pl.ds(pl.multiple_of(at, BLK), BLK), :]
                parts.append(mm(turn_mid if m == main else turn, block.reshape(BLK * BLK, cols)))
        return parts

    def lay_row(parts, r, at):
        put(xs, at, jnp.concatenate([p[r * BLK : (r + 1) * BLK] for p in parts], axis=0), 1)

    mid_start = jnp.where(core == 0, first_row + rows, first_row - HALO)
    parts = lay_block(main)
    for r in range(HALO):
        lay_row(parts, r, mid_start + r)

    def line(k):
        return mask[pl.ds(base + k, 1), :]

    none = jnp.zeros((allc, cols), F32)
    first_sums = [none, none]
    second_sums = [[none, none], [none, none]]

    def first(q):
        pa, pb = first_sums
        y = mm(w1[...], xs[q])
        total = pa + y[2 * allc :]
        first_sums[:] = [pb + y[allc : 2 * allc], y[:allc]]
        h = jnp.maximum(total * line((q + 2) // side - 1), 0.0)
        put(hs, q, h.astype(BF), 2)

    def second(q):
        pa, pb = second_sums[q % 2]
        z = mm(w2[...], hs[q])
        total = pa + z[2 * allc :]
        second_sums[q % 2] = [pb + z[allc : 2 * allc], z[:allc]]
        if q >= side:
            x = xs[q - 3, allc : 2 * allc, :].astype(F32)
            es_ref[q - side] = (line(q // side - 1) * (x + total)).astype(BF)

    def pick_tile(tile):
        tall = es_ref[tile * side : (tile + 1) * side].reshape(side * allc, cols)
        picked[tile * side * allc : (tile + 1) * side * allc, :] = mm(tall, pick).astype(BF)

    def merge_tile(tile, k):
        g = tile // 2 + core * (rows // (2 * side))

        def rows_of(n):
            at = (tile * side + 2 * n) * allc
            return picked[at : at + 2 * allc, :]

        for n, piece in enumerate(merge_pairs(wm[...], rows_of, (k, k + 1), g * wide, half)):
            u = (side // 2) * (tile % 2) + k + n
            mown_ref[tile // 2, u * chans : (u + 1) * chans, :] = piece[:chans].astype(BF)
            moth_ref[tile // 2, u * chans : (u + 1) * chans, :] = piece[chans:].astype(BF)

    outs = []
    lag = 4
    total_rows = rows + side
    for s in range(-1, total_rows + 3 * lag + 2 * side):
        if 0 <= s < rows:
            if s % BLK == 0:
                parts = lay_block(s // BLK)
            lay_row(parts, s % BLK, first_row + s)
        q = s + first_row - lag
        if 0 <= q < total_rows:
            first(q)
        q -= lag
        if 0 <= q < total_rows:
            second(q)
        done = q - 2 * side
        if done >= 0 and done % side == 2 and done // side < tiles:
            at = pl.ds(done // side * side, side)
            out = pltpu.make_async_copy(es_ref.at[at], es_hbm.at[at], out_sem.at[done // side])
            out.start()
            outs.append(out)
            pick_tile(done // side)
        if done >= 0 and done % side in (4, 6) and done // side < tiles:
            merge_tile(done // side, 0 if done % side == 4 else 2)

    for k in range(3):
        xa_ref[k] = xs[first_row + (rows - 3) * core + k]
    for k in range(4):
        ha_ref[k] = hs[jnp.where(core == 0, 7, rows + 1) + k]
    ea_ref[0] = es_ref[jnp.where(core == 0, 3, rows - 4)]
    for out in outs:
        out.wait()


def border_kernel(
    rows,
    outer_ref,
    masks_ref,
    w1,
    w2,
    wm,
    xa_ref,
    ha_ref,
    ea_ref,
    mown_in,
    moth_in,
    es_in,
    es_hbm,
    mown_ref,
    moth_ref,
    x5,
    h7,
    e4,
    sem,
):
    core = lax.axis_index("chan")
    _, allc, cols = ea_ref.shape
    chans = allc // 2
    lanes = outer_ref.shape[1]
    tiles_r = masks_ref.shape[0]
    masks = masks_ref[...]
    top = core == 0
    turn4 = swap_matrix(HALO, chans)
    flat = HALO * chans
    pieces = [outer_ref[k * flat : (k + 1) * flat, :] for k in range(2 * cols // lanes)]
    oth, own = [
        mm(turn4, jnp.concatenate(pieces[n * cols // lanes : (n + 1) * cols // lanes], axis=1))
        for n in range(2)
    ]
    halo = [
        jnp.concatenate([p[r * chans : (r + 1) * chans] for p in (own, oth)], axis=0)
        for r in range(HALO)
    ]
    outer_mask = jnp.where(top, halo[0][0:1], halo[HALO - 1][0:1])
    tile_mask = jnp.where(top, masks[0:1], masks[tiles_r - 1 : tiles_r])
    for k in range(3):
        put(x5, jnp.where(top, k, k + 2), jnp.where(top, halo[k + 1], halo[k]), 1)
    for k in range(2):
        x5[jnp.where(top, k + 3, k)] = xa_ref[jnp.where(top, k, k + 1)]
    for k in range(4):
        h7[jnp.where(top, k + 3, k)] = ha_ref[k]
    y = [mm(w1[...], x5[k]) for k in range(5)]
    for k in range(3):
        total = y[k][:allc] + y[k + 1][allc : 2 * allc] + y[k + 2][2 * allc :]
        if k == 1:
            line = outer_mask
        else:
            line = jnp.where(top if k == 0 else core == 1, outer_mask, tile_mask)
        h = jnp.maximum(total * line, 0.0)
        put(h7, jnp.where(top, k, k + 4), h, 2)
    z = [mm(w2[...], h7[k]) for k in range(7)]
    e4[jnp.where(top, 3, 0)] = ea_ref[0]
    for k in range(3):
        total = z[k][:allc] + z[k + 2][allc : 2 * allc] + z[k + 4][2 * allc :]
        x = xa_ref[k, allc : 2 * allc, :].astype(F32)
        e4[jnp.where(top, k, k + 1)] = (tile_mask * (x + total)).astype(BF)
    copy = pltpu.make_async_copy(
        e4.at[pl.ds(core, 3)], es_hbm.at[pl.ds((rows - 3) * core, 3)], sem
    )
    copy.start()
    mown_ref[...] = mown_in[...]
    moth_ref[...] = moth_in[...]
    half = cols // 2
    parent_rows = mown_ref.shape[0]
    side = mown_ref.shape[1] // chans
    wide = half // side
    s = mm(e4[...].reshape(4 * allc, cols), pick_matrix(cols, side)).astype(BF)
    g = jnp.where(top, 0, 2 * parent_rows - 1)
    at_g = jnp.where(top, 0, parent_rows - 1)

    def rows_of(k):
        return s[k * 2 * allc : (k + 1) * 2 * allc]

    for n, piece in enumerate(merge_pairs(wm[...], rows_of, (0, 1), g * wide, half)):
        u = jnp.where(top, n, side - 2 + n)
        at_u = pl.ds(pl.multiple_of(u * chans, chans), chans)
        mown_ref[at_g, at_u, :] = piece[:chans].astype(BF)
        moth_ref[at_g, at_u, :] = piece[chans:].astype(BF)
    copy.wait()


def restore_kernel(es_hbm, after_hbm, enh_hbm, eoth_ref, es_ref, own, sem, in_sems):
    core = lax.axis_index("chan")
    rows, allc, cols = es_ref.shape
    chans = allc // 2
    copies = []
    for m in range(rows // BLK):
        at = pl.ds(m * BLK, BLK)
        copies.append(pltpu.make_async_copy(es_hbm.at[at], es_ref.at[at], in_sems.at[m]))
        copies[-1].start()
    turn = swap_matrix(BLK, BLK)
    for m in range(rows // BLK):
        copies[m].wait()
        at = m * BLK
        for c0 in range(0, allc, BLK):
            ref = own if c0 < chans else eoth_ref
            ch = c0 % chans
            block = es_ref[at : at + BLK, c0 : c0 + BLK, :].reshape(BLK * BLK, cols)
            ref[ch : ch + BLK, at : at + BLK, :] = mm(turn, block).astype(BF).reshape(BLK, BLK, cols)
    copy = pltpu.make_async_copy(
        own, enh_hbm.at[:, pl.ds(pl.multiple_of(core * rows, rows), rows), :], sem
    )
    copy.start()
    copy.wait()


def fill_kernel(recv_ref, held_hbm, enh_hbm, sem):
    core = lax.axis_index("chan")
    rows = recv_ref.shape[1]
    copy = pltpu.make_async_copy(
        recv_ref, enh_hbm.at[:, pl.ds(pl.multiple_of((1 - core) * rows, rows), rows), :], sem
    )
    copy.start()
    copy.wait()


def deal(now, width):
    n = len(now)
    group = div(iota(now[0].shape, 1), width)
    bit = 1
    while bit < n:
        odd = jnp.where(group & bit != 0, 1.0, 0.0).astype(BF) > jnp.bfloat16(0.5)
        now = [jnp.where(odd, now[(j + bit) % n], now[j]) for j in range(n)]
        bit *= 2
    return now


def pack_kernel(
    side, slots, owner_ref, mown_ref, mrecv_ref, out_hbm, out_ref, arr, lhs, mid, code_ref, sems
):
    core, tile = lax.axis_index("chan"), lax.axis_index("tiles")
    count = owner_ref.shape[1]
    mine, rows, lanes = mown_ref.shape
    blocks, all_rows, _ = out_ref.shape
    per = side * slots
    wide = lanes // side
    copies = []

    def send_out(at, n):
        part = pl.ds(at, n)
        copies.append(
            pltpu.make_async_copy(out_ref.at[part], out_hbm.at[part], sems.at[len(copies)])
        )
        copies[-1].start()

    for k in range(mine):
        arr[core * mine + k] = mown_ref[k]
        arr[(1 - core) * mine + k] = mrecv_ref[k]
    line = jnp.broadcast_to(owner_ref[...].astype(F32), (lanes, count))
    owner = jnp.transpose(line).astype(jnp.int32)
    is_owner = owner == iota((count, lanes), 1)
    marks = ones_where(is_owner)
    lower = ones_where(iota((count, count), 0) > iota((count, count), 1))
    earlier = mm(lower, marks)
    within = jnp.sum(jnp.where(is_owner, earlier, 0.0), axis=1, keepdims=True).astype(jnp.int32)
    if per == lanes:
        code = (owner * slots + within).astype(F32).astype(BF)
        code_ref[0:count, :] = code
        code_ref[count : 2 * count, :] = code

        def by_column(step, carry):
            at = pl.ds(pl.multiple_of(step * BLK, BLK), BLK)
            done = deal([arr[g, at, :] for g in range(side)], wide)
            for j in range(side):
                lhs[-j % side, at, :] = done[j]
            return carry

        lax.fori_loop(0, rows // BLK, by_column, 0, unroll=4)
        halves = blocks // side
        lane = iota((1, halves * lanes), 1)
        block, group, slot = div(lane, lanes), div(mod(lane, lanes), wide), mod(lane, wide)
        for i in range(side):
            v = lax.rem(i + side - lax.rem(tile, side), side)
            at = pl.multiple_of(count - wide * v, wide)
            codes = code_ref[pl.ds(at, count), :]
            want = (block * side + mod(group - i + side, side)) * slots + slot
            want = jnp.broadcast_to(want.astype(F32).astype(BF), (count, halves * lanes))
            same = jnp.concatenate([codes] * halves, axis=1) == want
            take = jnp.where(same, jnp.ones_like(want), jnp.zeros_like(want))
            got = mm(lhs[v], take).astype(BF)
            for h in range(halves):
                mid[h * side + i] = got[:, h * lanes : (h + 1) * lanes]
        tally = mm(jnp.ones((all_rows - rows, count), BF), marks)
        for d in range(blocks):
            out_ref[d, rows:all_rows, :] = jnp.broadcast_to(
                tally[:, d : d + 1], (all_rows - rows, lanes)
            ).astype(BF)
        for h in range(halves):
            for r in range(0, rows, BLK):
                done = deal([mid[h * side + i, r : r + BLK, :] for i in range(side)], wide)
                for j in range(side):
                    out_ref[h * side + -j % side, r : r + BLK, :] = done[j]
            send_out(h * side, side)
    else:
        code = owner * per + within
        lane = iota((wide, lanes), 1)
        for g in range(2 * mine):
            for x in range(side):
                at = (g * side + x) * wide
                code_ref[at : at + wide, :] = (
                    code[g * wide : (g + 1) * wide] + (x - g) % side * slots
                )
        data = jnp.concatenate([arr[g] for g in range(2 * mine)], axis=1)
        lane = iota((count * side, lanes), 1)
        for step in range(0, blocks, 2):
            codes = code_ref[...]
            spots = [ones_where(codes == lane + at * lanes) for at in (step, step + 1)]
            total = mm(data, jnp.concatenate(spots, axis=1)).astype(BF)
            for n in range(2):
                at = step + n
                out_ref[at, 0:rows, :] = total[:, n * lanes : (n + 1) * lanes]
                goal = div(iota((count, lanes), 1) + at * lanes, per)
                tally = mm(jnp.ones((all_rows - rows, count), BF), ones_where(owner == goal))
                out_ref[at, rows:all_rows, :] = tally.astype(BF)
        send_out(0, blocks)
    for copy in copies:
        copy.wait()


def targets(tallies, lanes, group, slots):
    lane0, lane1 = iota((lanes, lanes), 0), iota((lanes, lanes), 1)
    heads = mod(lane0, group) == 0
    before = ones_where(heads & (div(lane0, group) < div(lane1, group)))
    every = ones_where(heads)
    slot = mod(iota((1, lanes), 1), slots).astype(F32)
    running = jnp.zeros((1, lanes), F32)
    outs = []
    for tally in tallies:
        inside, whole = mm(tally, before)[0:1], mm(tally, every)[0:1]
        live = slot < tally.astype(F32)[0:1]
        outs.append(jnp.where(live, running + inside + slot, -1.0))
        running = running + whole
    return outs


def hits(target, room):
    shape = (room, target.shape[1])
    goal = iota(shape, 0).astype(F32).astype(BF)
    same = goal == jnp.broadcast_to(target.astype(BF), shape)
    return jnp.where(same, jnp.ones_like(goal), jnp.zeros_like(goal))


def unpack_kernel(side, slots, got_ref, out_hbm, out_ref, picked, data, column, sems):
    tile = lax.axis_index("tiles")
    blocks, all_rows, lanes = got_ref.shape
    chans, _, cap = out_ref.shape
    copies = []
    rows = side * chans
    per = side * slots
    room = picked.shape[2]
    if per == lanes:
        halves = blocks // side
        group = div(iota((all_rows - rows, lanes), 1), slots)
        tallies = []
        for h in range(halves):
            tally = got_ref[h * side, rows:all_rows, :].astype(F32)
            for s in range(1, side):
                other = got_ref[h * side + s, rows:all_rows, :].astype(F32)
                tally = jnp.where(group == s, other, tally)
            tallies.append(tally.astype(BF))
        for h, spot in enumerate(targets(tallies, lanes, slots, slots)):
            turned = jnp.transpose(jnp.broadcast_to(spot, (lanes, lanes))).astype(BF)
            column[h, 0:lanes, :] = turned
            column[h, lanes : 2 * lanes, :] = turned
        for h in range(halves):

            def turn_rows(step, carry, h=h):
                at = pl.ds(pl.multiple_of(step * BLK, BLK), BLK)
                done = deal([got_ref[h * side + s, at, :] for s in range(side)], slots)
                for j in range(side):
                    data[h, j, at, :] = done[j]
                return carry

            lax.fori_loop(0, rows // BLK, turn_rows, 0, unroll=True)
        for j in range(side):
            v = lax.rem(2 * side - j - lax.rem(tile, side), side)
            left = jnp.concatenate([data[h, j] for h in range(halves)], axis=1)
            right = []
            for h in range(halves):
                spot = column[h, j * slots : j * slots + lanes, :]
                parts = []
                for at in range(0, room, lanes):
                    goal = (iota((1, lanes), 1) + at).astype(F32).astype(BF)
                    same = spot == jnp.broadcast_to(goal, (lanes, lanes))
                    parts.append(jnp.where(same, jnp.ones_like(spot), jnp.zeros_like(spot)))
                right.append(jnp.concatenate(parts, axis=1))
            picked[v] = mm(left, jnp.concatenate(right, axis=0)).astype(BF)
    else:
        tallies = [got_ref[b, rows:all_rows, :] for b in range(blocks)]
        spots = [hits(t, room) for t in targets(tallies, lanes, per, slots)]
        spots = jnp.concatenate(spots, axis=1)
        for v in range(side):
            keep = div(mod(iota((rows, lanes), 1), per), slots) == v
            left = jnp.concatenate(
                [jnp.where(keep, got_ref[b, 0:rows, :], jnp.zeros((rows, lanes), BF)) for b in range(blocks)],
                axis=1,
            )
            picked[v] = mm_nt(left, spots).astype(BF)
    two = BLK // side
    n = BLK * BLK
    row, col = iota((n, n), 0), iota((n, n), 1)
    turn = ones_where(
        (div(row, BLK) == mod(col, BLK))
        & (mod(div(row, side), two) == mod(div(col, BLK), two))
        & (mod(row, side) == div(col, BLK * two))
    )
    for ch in range(0, chans, BLK):
        for u in range(0, side, two):
            block = jnp.concatenate(
                [
                    picked[v, (u + w) * chans + ch : (u + w) * chans + ch + BLK, :]
                    for v in range(side)
                    for w in range(two)
                ],
                axis=0,
            )
            done = mm(turn, block).astype(BF).reshape(BLK, BLK, room)
            out_ref[ch : ch + BLK, u * side : (u + two) * side, :] = done[:, :, :cap]
        part = pl.ds(ch, BLK)
        copies.append(
            pltpu.make_async_copy(out_ref.at[part], out_hbm.at[part], sems.at[ch // BLK])
        )
        copies[-1].start()
    for copy in copies:
        copy.wait()


def on_device(features, tile_valid, parent_owner, w_first, w_second, w_merge):
    chans, row_count, col_count = features.shape
    tile_rows, _ = tile_valid.shape
    side = row_count // tile_rows
    parents_dev = parent_owner.shape[0]
    devices = lax.axis_size("tiles")
    slots = 2 * max(1, parents_dev // devices)
    own_cap = 3 * parents_dev // 2
    rows = row_count // 2
    allc = 2 * chans
    lanes = 128
    blocks = devices * slots * side // lanes
    fold = devices // blocks
    swap = [(0, 1), (1, 0)]
    vmem = pl.BlockSpec(memory_space=pltpu.VMEM)
    hbm = pl.BlockSpec(memory_space=pltpu.HBM)

    def limit(mib):
        return pltpu.CompilerParams(vmem_limit_bytes=int(mib * 1024) << 10)

    feat_oth = lax.ppermute(features, "chan", swap)
    edge_rows = chans * HALO * col_count // lanes
    send, keep, masks = pl.pallas_call(
        functools.partial(edges_kernel, side),
        out_shape=(
            jax.ShapeDtypeStruct((edge_rows, lanes), BF),
            jax.ShapeDtypeStruct((edge_rows, lanes), BF),
            jax.ShapeDtypeStruct((tile_rows, col_count), F32),
        ),
        in_specs=[hbm, vmem],
        out_specs=(vmem,) * 3,
        scratch_shapes=[
            pltpu.VMEM((2, chans, BLK, col_count), BF),
            pltpu.SemaphoreType.DMA((2,)),
        ],
        compiler_params=limit(52),
        name="edges",
    )(features, tile_valid)
    sent = lax.ppermute(send, "chan", swap)
    extra = jnp.concatenate(
        [w_first, w_second, jnp.swapaxes(w_merge, 1, 2), send[None, :chans, :allc]], axis=0
    )
    extra_oth = lax.ppermute(extra, "chan", swap)
    cross = [(2 * t + 1, 2 * t + 2) for t in range(devices - 1)]
    cross += [(2 * t, 2 * t - 1) for t in range(1, devices)]
    payload = jnp.concatenate([keep, sent], axis=0)
    outer = lax.ppermute(payload, ("tiles", "chan"), cross)
    w1, w2, wm = pl.pallas_call(
        weights_kernel,
        out_shape=(
            jax.ShapeDtypeStruct((3 * allc, 3 * allc), BF),
            jax.ShapeDtypeStruct((3 * allc, 3 * allc), BF),
            jax.ShapeDtypeStruct((allc, 4 * allc), BF),
        ),
        in_specs=[vmem, vmem],
        out_specs=(vmem,) * 3,
        compiler_params=limit(6),
        name="weights",
    )(extra, extra_oth)

    parent_rows = tile_rows // 4
    held_rows = rows * pl.cdiv(44 << 20, rows * allc * col_count * 2)
    es, m_own, m_oth, xa, ha, ea = pl.pallas_call(
        functools.partial(conv_kernel, side),
        out_shape=(
            jax.ShapeDtypeStruct((held_rows, allc, col_count), BF),
            jax.ShapeDtypeStruct((parent_rows, side * chans, col_count // 2), BF),
            jax.ShapeDtypeStruct((parent_rows, side * chans, col_count // 2), BF),
            jax.ShapeDtypeStruct((3, 3 * allc, col_count), BF),
            jax.ShapeDtypeStruct((4, 3 * allc, col_count), BF),
            jax.ShapeDtypeStruct((1, allc, col_count), BF),
        ),
        in_specs=[vmem] * 6,
        out_specs=(hbm,) + (vmem,) * 5,
        scratch_shapes=[
            pltpu.VMEM((rows + 16, 3 * allc, col_count), BF),
            pltpu.VMEM((rows + side, 3 * allc, col_count), BF),
            pltpu.VMEM((rows, allc, col_count), BF),
            pltpu.VMEM((tile_rows + 2 * side, col_count), F32),
            pltpu.VMEM((rows * allc, col_count), BF),
            pltpu.SemaphoreType.DMA((rows // side,)),
        ],
        compiler_params=limit(36),
        name="conv",
    )(features, feat_oth, masks, w1, w2, wm)
    es, m_own, m_oth = pl.pallas_call(
        functools.partial(border_kernel, rows),
        out_shape=(
            jax.ShapeDtypeStruct(es.shape, BF),
            jax.ShapeDtypeStruct((parent_rows, side * chans, col_count // 2), BF),
            jax.ShapeDtypeStruct((parent_rows, side * chans, col_count // 2), BF),
        ),
        in_specs=[vmem] * 10 + [hbm],
        out_specs=(hbm, vmem, vmem),
        scratch_shapes=[
            pltpu.VMEM((5, 3 * allc, col_count), BF),
            pltpu.VMEM((7, 3 * allc, col_count), BF),
            pltpu.VMEM((4, allc, col_count), BF),
            pltpu.SemaphoreType.DMA,
        ],
        input_output_aliases={10: 0},
        compiler_params=limit(16),
        name="border",
    )(outer, masks, w1, w2, wm, xa, ha, ea, m_own, m_oth, es)
    m_recv = lax.ppermute(m_oth, "chan", swap)
    all_rows = side * chans + 8
    packed = pl.pallas_call(
        functools.partial(pack_kernel, side, slots),
        out_shape=jax.ShapeDtypeStruct((blocks, all_rows, lanes), BF),
        in_specs=[vmem, vmem, vmem],
        out_specs=hbm,
        scratch_shapes=[
            pltpu.VMEM((blocks, all_rows, lanes), BF),
            pltpu.VMEM((2 * parent_rows, side * chans, lanes), BF),
            pltpu.VMEM((side, side * chans, lanes), BF),
            pltpu.VMEM((blocks, side * chans, lanes), BF),
            pltpu.VMEM((parents_dev * side, lanes), BF if fold == 1 else jnp.int32),
            pltpu.SemaphoreType.DMA((max(1, blocks // side),)),
        ],
        compiler_params=limit(16),
        name="pack",
    )(parent_owner[None, :], m_own, m_recv)

    def to_peers(x):
        if fold > 1:
            x = x.reshape(blocks, all_rows, fold, lanes // fold)
            x = x.transpose(0, 2, 1, 3).reshape(devices, all_rows, lanes // fold)
        x = lax.all_to_all(x, "tiles", split_axis=0, concat_axis=0, tiled=True)
        if fold > 1:
            x = x.reshape(blocks, fold, all_rows, lanes // fold)
            x = x.transpose(0, 2, 1, 3).reshape(blocks, all_rows, lanes)
        return x

    got = to_peers(packed)
    held, e_oth = pl.pallas_call(
        restore_kernel,
        out_shape=(
            jax.ShapeDtypeStruct((chans, row_count, col_count), BF),
            jax.ShapeDtypeStruct((chans, rows, col_count), BF),
        ),
        in_specs=[hbm, hbm],
        out_specs=(hbm, vmem),
        scratch_shapes=[
            pltpu.VMEM((rows, allc, col_count), BF),
            pltpu.VMEM((chans, rows, col_count), BF),
            pltpu.SemaphoreType.DMA,
            pltpu.SemaphoreType.DMA((rows // BLK,)),
        ],
        compiler_params=limit(12),
        name="restore",
    )(es, packed)
    e_recv = lax.ppermute(e_oth, "chan", swap)
    enhanced = pl.pallas_call(
        fill_kernel,
        out_shape=jax.ShapeDtypeStruct((chans, row_count, col_count), BF),
        in_specs=[vmem, hbm],
        out_specs=hbm,
        scratch_shapes=[pltpu.SemaphoreType.DMA],
        input_output_aliases={1: 0},
        compiler_params=limit(6),
        name="fill",
    )(e_recv, held)
    room = pl.cdiv(own_cap, lanes) * lanes
    parents = pl.pallas_call(
        functools.partial(unpack_kernel, side, slots),
        out_shape=jax.ShapeDtypeStruct((chans, side * side, own_cap), BF),
        in_specs=[vmem],
        out_specs=hbm,
        scratch_shapes=[
            pltpu.VMEM((chans, side * side, own_cap), BF),
            pltpu.VMEM((side, side * chans, room), BF),
            pltpu.VMEM((2, side, side * chans, lanes), BF),
            pltpu.VMEM((2, 2 * lanes, lanes), BF),
            pltpu.SemaphoreType.DMA((chans // BLK,)),
        ],
        compiler_params=limit(24),
        name="unpack",
    )(got)
    return enhanced, jnp.swapaxes(parents, 1, 2)


def solution(mesh):
    return jax.shard_map(
        on_device,
        mesh=mesh,
        in_specs=(
            P("chan", "tiles", None),
            P("tiles", None),
            P("tiles"),
            P(None, "chan", None),
            P(None, "chan", None),
            P(None, None, "chan"),
        ),
        out_specs=(P("chan", "tiles", None), P("chan", "tiles", None)),
        check_vma=False,
    )
```

```python
import functools

import jax
import jax.numpy as jnp
from jax import lax
from jax.experimental import pallas as pl
from jax.experimental.pallas import tpu as pltpu
from jax.sharding import PartitionSpec as P


BF = jnp.bfloat16
F32 = jnp.float32
HALO = 4
BLK = 16
EMPTY = 1e30


def iota(shape, dim):
    return lax.broadcasted_iota(jnp.int32, shape, dim)


def div(x, n):
    return x >> (n.bit_length() - 1) if n & (n - 1) == 0 else lax.div(x, jnp.int32(n))


def mod(x, n):
    return x & (n - 1) if n & (n - 1) == 0 else lax.rem(x, jnp.int32(n))


def ones_where(cond):
    return jnp.where(cond, 1.0, 0.0).astype(BF)


def mm(a, b):
    return jnp.dot(a, b, preferred_element_type=F32)


def mm_nt(a, b):
    return lax.dot_general(a, b, (((1,), (1,)), ((), ())), preferred_element_type=F32)


def swap_matrix(outer, inner):
    n = outer * inner
    row, col = iota((n, n), 0), iota((n, n), 1)
    return ones_where((mod(row, inner) == div(col, outer)) & (div(row, inner) == mod(col, outer)))


def shifted(x, amount):
    lanes = 128
    parts = [x[:, at : at + lanes] for at in range(0, x.shape[1], lanes)]
    turned = [pltpu.roll(p, amount % lanes, 1) for p in parts]
    lane = iota(parts[0].shape, 1)
    zero = jnp.zeros_like(parts[0])
    outs = []
    for n in range(len(parts)):
        if amount > 0:
            edge = turned[n - 1] if n else zero
            outs.append(jnp.where(lane < amount, edge, turned[n]))
        else:
            edge = turned[n + 1] if n + 1 < len(parts) else zero
            outs.append(jnp.where(lane >= lanes + amount, edge, turned[n]))
    return jnp.concatenate(outs, axis=1)


def widen_matrix(tiles_c, cols, side):
    return ones_where(div(iota((tiles_c, cols), 1), side) == iota((tiles_c, cols), 0))


def as_bf(x):
    return x.astype(F32).astype(BF)


def edges_kernel(side, feat_hbm, valid_ref, send_ref, keep_ref, masks_ref, edge, sems):
    core = lax.axis_index("chan")
    chans, feat_rows, cols = feat_hbm.shape
    copies = []
    for n, at in enumerate((0, feat_rows - BLK)):
        copy = pltpu.make_async_copy(feat_hbm.at[:, at : at + BLK, :], edge.at[n], sems.at[n])
        copy.start()
        copies.append(copy)
    flat = chans * HALO
    lanes = send_ref.shape[1]
    tiles_r, tiles_c = valid_ref.shape
    masks = mm(as_bf(valid_ref[...]), widen_matrix(tiles_c, cols, side))
    masks_ref[...] = masks
    row, col = iota((flat, chans * BLK), 0), iota((flat, chans * BLK), 1)
    same = div(row, HALO) == div(col, BLK)
    spot = mod(iota((flat, cols), 0), HALO)
    made = []
    for n in range(2):
        if n == 0:
            hit = same & (mod(row, HALO) == mod(col, BLK)) & (mod(row, HALO) < HALO - 1)
            flag, line = spot == HALO - 1, masks[0:1]
        else:
            hit = same & (mod(row, HALO) + BLK - HALO == mod(col, BLK)) & (mod(row, HALO) > 0)
            flag, line = spot == 0, masks[tiles_r - 1 : tiles_r]
        take = ones_where(hit)
        copies[n].wait()
        body = mm(take, edge[n].reshape(chans * BLK, cols))
        made.append(jnp.where(flag, jnp.broadcast_to(line, (flat, cols)), body).astype(BF))
    low = core == 0
    send = jnp.where(low, made[1], made[0])
    keep = jnp.where(low, made[0], made[1])
    for n in range(cols // lanes):
        send_ref[n * flat : (n + 1) * flat, :] = send[:, n * lanes : (n + 1) * lanes]
        keep_ref[n * flat : (n + 1) * flat, :] = keep[:, n * lanes : (n + 1) * lanes]


def weights_kernel(own_ref, oth_ref, w1_ref, w2_ref, wm_ref):
    core = lax.axis_index("chan")
    chans, allc = own_ref.shape[1:]

    def tap(k):
        return [ref[k] for ref in (own_ref, oth_ref)]

    for dst, base in ((w1_ref, 0), (w2_ref, 9)):
        total = None
        for b in range(3):
            tall = jnp.concatenate(sum([tap(base + 3 * a + b) for a in range(3)], []), axis=0)
            src, pos = iota((allc, 3 * allc), 0), iota((allc, 3 * allc), 1)
            place = ones_where(pos == b * allc + mod(src + chans * core, allc))
            part = mm(tall, place)
            total = part if total is None else total + part
        dst[...] = total.astype(BF)
    tall = jnp.concatenate(
        sum([tap(18 + 2 * a + b) for b in range(2) for a in range(2)], []), axis=0
    )
    order = ones_where(iota((allc, allc), 1) == mod(iota((allc, allc), 0) + chans * core, allc))
    wm_ref[...] = mm_nt(order, tall).astype(BF)


def put(dst, index, x, amount):
    allc = x.shape[0]
    dst[index, 0:allc, :] = shifted(x, amount).astype(BF)
    dst[index, allc : 2 * allc, :] = x.astype(BF)
    dst[index, 2 * allc : 3 * allc, :] = shifted(x, -amount).astype(BF)


def pick_matrix(cols, side):
    half = cols // 2
    wide = half // side
    lane = iota((cols, cols), 1)
    spot = mod(lane, half)
    want = 2 * (mod(spot, wide) * side + div(spot, wide)) + div(lane, half)
    return ones_where(iota((cols, cols), 0) == want)


def merge_pairs(wm, rows_of, pairs, turn, half):
    rhs = []
    for n in pairs:
        sp = rows_of(n)
        rhs.append(jnp.concatenate([sp[:, :half], sp[:, half:]], axis=0))
    both = mm(wm, jnp.concatenate(rhs, axis=1))
    return [pltpu.roll(both[:, n * half : (n + 1) * half], turn, 1) for n in range(2)]


def conv_kernel(
    side,
    own_ref,
    oth_ref,
    masks_ref,
    w1,
    w2,
    wm,
    es_hbm,
    mown_ref,
    moth_ref,
    xa_ref,
    ha_ref,
    ea_ref,
    xs,
    hs,
    es_ref,
    mask,
    picked,
    out_sem,
):
    core = lax.axis_index("chan")
    rows, allc, cols = es_ref.shape
    chans = allc // 2
    main = rows // BLK
    tiles_r = masks_ref.shape[0]
    mask[...] = jnp.zeros(mask.shape, F32)
    mask[pl.ds(side, tiles_r), :] = masks_ref[...]

    first_row = 5
    outer_start = jnp.where(core == 0, first_row - HALO, first_row + rows)
    for r in range(HALO):
        xs[outer_start + r] = jnp.zeros(xs.shape[1:], BF)
    zero_row = jnp.zeros(xs.shape[1:], BF)
    xs[0] = zero_row
    turn = swap_matrix(BLK, BLK)
    few = HALO * BLK
    row, col = iota((few, BLK * BLK), 0), iota((few, BLK * BLK), 1)
    turn_mid = ones_where(
        (mod(row, BLK) == div(col, BLK)) & (div(row, BLK) + (BLK - HALO) * core == mod(col, BLK))
    )
    half = cols // 2
    wide = half // side
    pick = pick_matrix(cols, side)
    base = side + core * (rows // side)
    tiles = rows // side

    def lay_block(m):
        at = rows - BLK * core if m == main else rows * core + BLK * m
        parts = []
        for ref in (own_ref, oth_ref):
            for ch in range(0, chans, BLK):
                block = ref[ch : ch + BLK, pl.ds(pl.multiple_of(at, BLK), BLK), :]
                parts.append(mm(turn_mid if m == main else turn, block.reshape(BLK * BLK, cols)))
        return parts

    def lay_row(parts, r, at):
        put(xs, at, jnp.concatenate([p[r * BLK : (r + 1) * BLK] for p in parts], axis=0), 1)

    mid_start = jnp.where(core == 0, first_row + rows, first_row - HALO)
    parts = lay_block(main)
    for r in range(HALO):
        lay_row(parts, r, mid_start + r)

    def line(k):
        return mask[pl.ds(base + k, 1), :]

    none = jnp.zeros((allc, cols), F32)
    first_sums = [none, none]
    second_sums = [[none, none], [none, none]]

    def first(q):
        pa, pb = first_sums
        y = mm(w1[...], xs[q])
        total = pa + y[2 * allc :]
        first_sums[:] = [pb + y[allc : 2 * allc], y[:allc]]
        h = jnp.maximum(total * line((q + 2) // side - 1), 0.0)
        put(hs, q, h.astype(BF), 2)

    def second(q):
        pa, pb = second_sums[q % 2]
        z = mm(w2[...], hs[q])
        total = pa + z[2 * allc :]
        second_sums[q % 2] = [pb + z[allc : 2 * allc], z[:allc]]
        if q >= side:
            x = xs[q - 3, allc : 2 * allc, :].astype(F32)
            es_ref[q - side] = (line(q // side - 1) * (x + total)).astype(BF)

    def pick_tile(tile):
        tall = es_ref[tile * side : (tile + 1) * side].reshape(side * allc, cols)
        picked[tile * side * allc : (tile + 1) * side * allc, :] = mm(tall, pick).astype(BF)

    def merge_tile(tile, k):
        g = tile // 2 + core * (rows // (2 * side))

        def rows_of(n):
            at = (tile * side + 2 * n) * allc
            return picked[at : at + 2 * allc, :]

        for n, piece in enumerate(merge_pairs(wm[...], rows_of, (k, k + 1), g * wide, half)):
            u = (side // 2) * (tile % 2) + k + n
            mown_ref[tile // 2, u * chans : (u + 1) * chans, :] = piece[:chans].astype(BF)
            moth_ref[tile // 2, u * chans : (u + 1) * chans, :] = piece[chans:].astype(BF)

    outs = []
    lag = 16
    total_rows = rows + side
    for s in range(-1, total_rows + 3 * lag + 2 * side):
        if 0 <= s < rows:
            if s % BLK == 0:
                parts = lay_block(s // BLK)
            lay_row(parts, s % BLK, first_row + s)
        q = s + first_row - lag
        if 0 <= q < total_rows:
            first(q)
        q -= lag
        if 0 <= q < total_rows:
            second(q)
        done = q - 2 * side
        if done >= 0 and done % side == 2 and done // side < tiles:
            at = pl.ds(done // side * side, side)
            out = pltpu.make_async_copy(es_ref.at[at], es_hbm.at[at], out_sem.at[done // side])
            out.start()
            outs.append(out)
            pick_tile(done // side)
        if done >= 0 and done % side in (4, 6) and done // side < tiles:
            merge_tile(done // side, 0 if done % side == 4 else 2)

    for k in range(3):
        xa_ref[k] = xs[first_row + (rows - 3) * core + k]
    for k in range(4):
        ha_ref[k] = hs[jnp.where(core == 0, 7, rows + 1) + k]
    ea_ref[0] = es_ref[jnp.where(core == 0, 3, rows - 4)]
    for out in outs:
        out.wait()


def border_kernel(
    rows,
    side,
    outer_ref,
    masks_ref,
    w1,
    w2,
    wm,
    xa_ref,
    ha_ref,
    ea_ref,
    es_in,
    es_hbm,
    pown_ref,
    poth_ref,
    x5,
    h7,
    e4,
    sem,
):
    core = lax.axis_index("chan")
    _, allc, cols = ea_ref.shape
    chans = allc // 2
    lanes = outer_ref.shape[1]
    tiles_r = masks_ref.shape[0]
    masks = masks_ref[...]
    top = core == 0
    turn4 = swap_matrix(HALO, chans)
    flat = HALO * chans
    pieces = [outer_ref[k * flat : (k + 1) * flat, :] for k in range(2 * cols // lanes)]
    oth, own = [
        mm(turn4, jnp.concatenate(pieces[n * cols // lanes : (n + 1) * cols // lanes], axis=1))
        for n in range(2)
    ]
    halo = [
        jnp.concatenate([p[r * chans : (r + 1) * chans] for p in (own, oth)], axis=0)
        for r in range(HALO)
    ]
    outer_mask = jnp.where(top, halo[0][0:1], halo[HALO - 1][0:1])
    tile_mask = jnp.where(top, masks[0:1], masks[tiles_r - 1 : tiles_r])
    for k in range(3):
        put(x5, jnp.where(top, k, k + 2), jnp.where(top, halo[k + 1], halo[k]), 1)
    for k in range(2):
        x5[jnp.where(top, k + 3, k)] = xa_ref[jnp.where(top, k, k + 1)]
    for k in range(4):
        h7[jnp.where(top, k + 3, k)] = ha_ref[k]
    y = [mm(w1[...], x5[k]) for k in range(5)]
    for k in range(3):
        total = y[k][:allc] + y[k + 1][allc : 2 * allc] + y[k + 2][2 * allc :]
        if k == 1:
            line = outer_mask
        else:
            line = jnp.where(top if k == 0 else core == 1, outer_mask, tile_mask)
        h = jnp.maximum(total * line, 0.0)
        put(h7, jnp.where(top, k, k + 4), h, 2)
    z = [mm(w2[...], h7[k]) for k in range(7)]
    e4[jnp.where(top, 3, 0)] = ea_ref[0]
    for k in range(3):
        total = z[k][:allc] + z[k + 2][allc : 2 * allc] + z[k + 4][2 * allc :]
        x = xa_ref[k, allc : 2 * allc, :].astype(F32)
        e4[jnp.where(top, k, k + 1)] = (tile_mask * (x + total)).astype(BF)
    copy = pltpu.make_async_copy(
        e4.at[pl.ds(core, 3)], es_hbm.at[pl.ds((rows - 3) * core, 3)], sem
    )
    copy.start()
    half = cols // 2
    wide = half // side
    parent_rows = rows // (2 * side)
    s = mm(e4[...].reshape(4 * allc, cols), pick_matrix(cols, side)).astype(BF)
    g = jnp.where(top, 0, 2 * parent_rows - 1)

    def rows_of(k):
        return s[k * 2 * allc : (k + 1) * 2 * allc]

    for n, piece in enumerate(merge_pairs(wm[...], rows_of, (0, 1), g * wide, half)):
        pown_ref[n * chans : (n + 1) * chans, :] = piece[:chans].astype(BF)
        poth_ref[n * chans : (n + 1) * chans, :] = piece[chans:].astype(BF)
    copy.wait()


def restore_kernel(es_hbm, after_hbm, enh_hbm, eoth_ref, es_ref, own, sem, in_sems):
    core = lax.axis_index("chan")
    rows, allc, cols = es_ref.shape
    chans = allc // 2
    copies = []
    for m in range(rows // BLK):
        at = pl.ds(m * BLK, BLK)
        copies.append(pltpu.make_async_copy(es_hbm.at[at], es_ref.at[at], in_sems.at[m]))
        copies[-1].start()
    turn = swap_matrix(BLK, BLK)
    for m in range(rows // BLK):
        copies[m].wait()
        at = m * BLK
        for c0 in range(0, allc, BLK):
            ref = own if c0 < chans else eoth_ref
            ch = c0 % chans
            block = es_ref[at : at + BLK, c0 : c0 + BLK, :].reshape(BLK * BLK, cols)
            ref[ch : ch + BLK, at : at + BLK, :] = mm(turn, block).astype(BF).reshape(BLK, BLK, cols)
    copy = pltpu.make_async_copy(
        own, enh_hbm.at[:, pl.ds(pl.multiple_of(core * rows, rows), rows), :], sem
    )
    copy.start()
    copy.wait()


def fill_kernel(recv_ref, held_hbm, enh_hbm, sem):
    core = lax.axis_index("chan")
    rows = recv_ref.shape[1]
    copy = pltpu.make_async_copy(
        recv_ref, enh_hbm.at[:, pl.ds(pl.multiple_of((1 - core) * rows, rows), rows), :], sem
    )
    copy.start()
    copy.wait()


def deal(now, width):
    n = len(now)
    group = div(iota(now[0].shape, 1), width)
    bit = 1
    while bit < n:
        odd = jnp.where(group & bit != 0, 1.0, 0.0).astype(BF) > jnp.bfloat16(0.5)
        now = [jnp.where(odd, now[(j + bit) % n], now[j]) for j in range(n)]
        bit *= 2
    return now


def pack_kernel(
    side, slots, owner_ref, mown_ref, mrecv_ref, pown_ref, precv_ref, out_hbm, out_ref, arr, lhs, mid, code_ref, sems
):
    core, tile = lax.axis_index("chan"), lax.axis_index("tiles")
    count = owner_ref.shape[1]
    mine, rows, lanes = mown_ref.shape
    blocks, all_rows, _ = out_ref.shape
    per = side * slots
    wide = lanes // side
    copies = []

    def send_out(at, n):
        part = pl.ds(at, n)
        copies.append(
            pltpu.make_async_copy(out_ref.at[part], out_hbm.at[part], sems.at[len(copies)])
        )
        copies[-1].start()

    for k in range(mine):
        arr[core * mine + k] = mown_ref[k]
        arr[(1 - core) * mine + k] = mrecv_ref[k]
    edge = pown_ref.shape[0]
    for ref, mine_is in ((pown_ref, core), (precv_ref, 1 - core)):
        at = pl.ds(pl.multiple_of((rows - edge) * mine_is, edge), edge)
        arr[(2 * mine - 1) * mine_is, at, :] = ref[...]
    line = jnp.broadcast_to(owner_ref[...].astype(F32), (lanes, count))
    owner = jnp.transpose(line).astype(jnp.int32)
    is_owner = owner == iota((count, lanes), 1)
    marks = ones_where(is_owner)
    lower = ones_where(iota((count, count), 0) > iota((count, count), 1))
    earlier = mm(lower, marks)
    within = jnp.sum(jnp.where(is_owner, earlier, 0.0), axis=1, keepdims=True).astype(jnp.int32)
    if per == lanes:
        code = (owner * slots + within).astype(F32).astype(BF)
        code_ref[0:count, :] = code
        code_ref[count : 2 * count, :] = code

        def by_column(step, carry):
            at = pl.ds(pl.multiple_of(step * BLK, BLK), BLK)
            done = deal([arr[g, at, :] for g in range(side)], wide)
            for j in range(side):
                lhs[-j % side, at, :] = done[j]
            return carry

        lax.fori_loop(0, rows // BLK, by_column, 0, unroll=4)
        halves = blocks // side
        lane = iota((1, halves * lanes), 1)
        block, group, slot = div(lane, lanes), div(mod(lane, lanes), wide), mod(lane, wide)
        for i in range(side):
            v = lax.rem(i + side - lax.rem(tile, side), side)
            at = pl.multiple_of(count - wide * v, wide)
            codes = code_ref[pl.ds(at, count), :]
            want = (block * side + mod(group - i + side, side)) * slots + slot
            want = jnp.broadcast_to(want.astype(F32).astype(BF), (count, halves * lanes))
            same = jnp.concatenate([codes] * halves, axis=1) == want
            take = jnp.where(same, jnp.ones_like(want), jnp.zeros_like(want))
            got = mm(lhs[v], take).astype(BF)
            for h in range(halves):
                mid[h * side + i] = got[:, h * lanes : (h + 1) * lanes]
        tally = mm(jnp.ones((side, count), BF), marks)[0:1]
        spot = (iota((BLK, lanes), 0) == 0, mod(iota((BLK, lanes), 1), wide).astype(F32))
        for h in range(halves):
            for r in range(0, rows, BLK):
                done = deal([mid[h * side + i, r : r + BLK, :] for i in range(side)], wide)
                for j in range(side):
                    d = h * side + -j % side
                    value = done[j]
                    if r == 0:
                        empty = spot[0] & (spot[1] >= tally[:, d : d + 1])
                        value = jnp.where(empty, EMPTY, value.astype(F32)).astype(BF)
                    out_ref[d, r : r + BLK, :] = value
            send_out(h * side, side)
    else:
        code = owner * per + within
        lane = iota((wide, lanes), 1)
        for g in range(2 * mine):
            for x in range(side):
                at = (g * side + x) * wide
                code_ref[at : at + wide, :] = (
                    code[g * wide : (g + 1) * wide] + (x - g) % side * slots
                )
        data = jnp.concatenate([arr[g] for g in range(2 * mine)], axis=1)
        lane = iota((count * side, lanes), 1)
        for step in range(0, blocks, 2):
            codes = code_ref[...]
            spots = [ones_where(codes == lane + at * lanes) for at in (step, step + 1)]
            total = mm(data, jnp.concatenate(spots, axis=1)).astype(BF)
            for n in range(2):
                at = step + n
                out_ref[at, 0:rows, :] = total[:, n * lanes : (n + 1) * lanes]
                goal = div(iota((count, lanes), 1) + at * lanes, per)
                tally = mm(jnp.ones((all_rows - rows, count), BF), ones_where(owner == goal))
                out_ref[at, rows:all_rows, :] = tally.astype(BF)
        send_out(0, blocks)
    for copy in copies:
        copy.wait()


def slots_of(live, lanes, slots):
    lane0, lane1 = iota((lanes, lanes), 0), iota((lanes, lanes), 1)
    before = ones_where(div(lane0, slots) < div(lane1, slots))
    every = jnp.ones((lanes, lanes), BF)
    slot = mod(iota((1, lanes), 1), slots).astype(F32)
    running = jnp.zeros((1, lanes), F32)
    outs = []
    for flag in live:
        some = flag.astype(BF)
        inside, whole = mm(some, before)[0:1], mm(some, every)[0:1]
        outs.append(jnp.where(flag[0:1] > 0.5, running + inside + slot, -1.0))
        running = running + whole
    return outs


def targets(tallies, lanes, group, slots):
    lane0, lane1 = iota((lanes, lanes), 0), iota((lanes, lanes), 1)
    heads = mod(lane0, group) == 0
    before = ones_where(heads & (div(lane0, group) < div(lane1, group)))
    every = ones_where(heads)
    slot = mod(iota((1, lanes), 1), slots).astype(F32)
    running = jnp.zeros((1, lanes), F32)
    outs = []
    for tally in tallies:
        inside, whole = mm(tally, before)[0:1], mm(tally, every)[0:1]
        live = slot < tally.astype(F32)[0:1]
        outs.append(jnp.where(live, running + inside + slot, -1.0))
        running = running + whole
    return outs


def hits(target, room):
    shape = (room, target.shape[1])
    goal = iota(shape, 0).astype(F32).astype(BF)
    same = goal == jnp.broadcast_to(target.astype(BF), shape)
    return jnp.where(same, jnp.ones_like(goal), jnp.zeros_like(goal))


def unpack_kernel(side, slots, got_ref, out_hbm, out_ref, picked, data, column, sems):
    tile = lax.axis_index("tiles")
    blocks, all_rows, lanes = got_ref.shape
    chans, _, cap = out_ref.shape
    copies = []
    rows = side * chans
    per = side * slots
    room = picked.shape[2]
    if per == lanes:
        halves = blocks // side
        live = []
        for h in range(halves):
            group = div(iota((side, lanes), 1), slots)
            flag = jnp.zeros((side, lanes), F32)
            for s in range(side):
                mark = got_ref[h * side + s, 0:BLK, :].astype(F32)[0:1]
                full = jnp.where(mark < 0.5 * EMPTY, 1.0, 0.0)
                flag = jnp.where(group == s, jnp.broadcast_to(full, (side, lanes)), flag)
            live.append(flag)
        for h, spot in enumerate(slots_of(live, lanes, slots)):
            turned = jnp.transpose(jnp.broadcast_to(spot, (lanes, lanes))).astype(BF)
            column[h, 0:lanes, :] = turned
            column[h, lanes : 2 * lanes, :] = turned
        for h in range(halves):

            def turn_rows(step, carry, h=h):
                at = pl.ds(pl.multiple_of(step * BLK, BLK), BLK)
                done = deal([got_ref[h * side + s, at, :] for s in range(side)], slots)
                for j in range(side):
                    data[h, j, at, :] = done[j]
                return carry

            lax.fori_loop(0, rows // BLK, turn_rows, 0, unroll=True)
        for j in range(side):
            v = lax.rem(2 * side - j - lax.rem(tile, side), side)
            left = jnp.concatenate([data[h, j] for h in range(halves)], axis=1)
            right = []
            for h in range(halves):
                spot = column[h, j * slots : j * slots + lanes, :]
                parts = []
                for at in range(0, room, lanes):
                    goal = (iota((1, lanes), 1) + at).astype(F32).astype(BF)
                    same = spot == jnp.broadcast_to(goal, (lanes, lanes))
                    parts.append(jnp.where(same, jnp.ones_like(spot), jnp.zeros_like(spot)))
                right.append(jnp.concatenate(parts, axis=1))
            picked[v] = mm(left, jnp.concatenate(right, axis=0)).astype(BF)
    else:
        tallies = [got_ref[b, rows:all_rows, :] for b in range(blocks)]
        spots = [hits(t, room) for t in targets(tallies, lanes, per, slots)]
        spots = jnp.concatenate(spots, axis=1)
        for v in range(side):
            keep = div(mod(iota((rows, lanes), 1), per), slots) == v
            left = jnp.concatenate(
                [jnp.where(keep, got_ref[b, 0:rows, :], jnp.zeros((rows, lanes), BF)) for b in range(blocks)],
                axis=1,
            )
            picked[v] = mm_nt(left, spots).astype(BF)
    two = BLK // side
    n = BLK * BLK
    row, col = iota((n, n), 0), iota((n, n), 1)
    turn = ones_where(
        (div(row, BLK) == mod(col, BLK))
        & (mod(div(row, side), two) == mod(div(col, BLK), two))
        & (mod(row, side) == div(col, BLK * two))
    )
    for ch in range(0, chans, BLK):
        for u in range(0, side, two):
            block = jnp.concatenate(
                [
                    picked[v, (u + w) * chans + ch : (u + w) * chans + ch + BLK, :]
                    for v in range(side)
                    for w in range(two)
                ],
                axis=0,
            )
            done = mm(turn, block).astype(BF).reshape(BLK, BLK, room)
            out_ref[ch : ch + BLK, u * side : (u + two) * side, :] = done[:, :, :cap]
        part = pl.ds(ch, BLK)
        copies.append(
            pltpu.make_async_copy(out_ref.at[part], out_hbm.at[part], sems.at[ch // BLK])
        )
        copies[-1].start()
    for copy in copies:
        copy.wait()


def on_device(features, tile_valid, parent_owner, w_first, w_second, w_merge):
    chans, row_count, col_count = features.shape
    tile_rows, _ = tile_valid.shape
    side = row_count // tile_rows
    parents_dev = parent_owner.shape[0]
    devices = lax.axis_size("tiles")
    slots = 2 * max(1, parents_dev // devices)
    own_cap = 3 * parents_dev // 2
    rows = row_count // 2
    allc = 2 * chans
    lanes = 128
    blocks = devices * slots * side // lanes
    fold = devices // blocks
    swap = [(0, 1), (1, 0)]
    vmem = pl.BlockSpec(memory_space=pltpu.VMEM)
    hbm = pl.BlockSpec(memory_space=pltpu.HBM)

    def limit(mib):
        return pltpu.CompilerParams(vmem_limit_bytes=int(mib * 1024) << 10)

    feat_oth = lax.ppermute(features, "chan", swap)
    edge_rows = chans * HALO * col_count // lanes
    send, keep, masks = pl.pallas_call(
        functools.partial(edges_kernel, side),
        out_shape=(
            jax.ShapeDtypeStruct((edge_rows, lanes), BF),
            jax.ShapeDtypeStruct((edge_rows, lanes), BF),
            jax.ShapeDtypeStruct((tile_rows, col_count), F32),
        ),
        in_specs=[hbm, vmem],
        out_specs=(vmem,) * 3,
        scratch_shapes=[
            pltpu.VMEM((2, chans, BLK, col_count), BF),
            pltpu.SemaphoreType.DMA((2,)),
        ],
        compiler_params=limit(52),
        name="edges",
    )(features, tile_valid)
    sent = lax.ppermute(send, "chan", swap)
    extra = jnp.concatenate(
        [w_first, w_second, jnp.swapaxes(w_merge, 1, 2), send[None, :chans, :allc]], axis=0
    )
    extra_oth = lax.ppermute(extra, "chan", swap)
    cross = [(2 * t + 1, 2 * t + 2) for t in range(devices - 1)]
    cross += [(2 * t, 2 * t - 1) for t in range(1, devices)]
    payload = jnp.concatenate([keep, sent], axis=0)
    outer = lax.ppermute(payload, ("tiles", "chan"), cross)
    w1, w2, wm = pl.pallas_call(
        weights_kernel,
        out_shape=(
            jax.ShapeDtypeStruct((3 * allc, 3 * allc), BF),
            jax.ShapeDtypeStruct((3 * allc, 3 * allc), BF),
            jax.ShapeDtypeStruct((allc, 4 * allc), BF),
        ),
        in_specs=[vmem, vmem],
        out_specs=(vmem,) * 3,
        compiler_params=limit(6),
        name="weights",
    )(extra, extra_oth)

    parent_rows = tile_rows // 4
    held_rows = rows * pl.cdiv(44 << 20, rows * allc * col_count * 2)
    conv = pl.pallas_call(
        functools.partial(conv_kernel, side),
        out_shape=(
            jax.ShapeDtypeStruct((held_rows, allc, col_count), BF),
            jax.ShapeDtypeStruct((parent_rows, side * chans, col_count // 2), BF),
            jax.ShapeDtypeStruct((parent_rows, side * chans, col_count // 2), BF),
            jax.ShapeDtypeStruct((3, 3 * allc, col_count), BF),
            jax.ShapeDtypeStruct((4, 3 * allc, col_count), BF),
            jax.ShapeDtypeStruct((1, allc, col_count), BF),
        ),
        in_specs=[vmem] * 6,
        out_specs=(hbm,) + (vmem,) * 5,
        scratch_shapes=[
            pltpu.VMEM((rows + 16, 3 * allc, col_count), BF),
            pltpu.VMEM((rows + side, 3 * allc, col_count), BF),
            pltpu.VMEM((rows, allc, col_count), BF),
            pltpu.VMEM((tile_rows + 2 * side, col_count), F32),
            pltpu.VMEM((rows * allc, col_count), BF),
            pltpu.SemaphoreType.DMA((rows // side,)),
        ],
        compiler_params=limit(36),
        name="conv",
    )
    es, m_own, m_oth, xa, ha, ea = conv(features, feat_oth, masks, w1, w2, wm)
    m_recv = lax.ppermute(m_oth, "chan", swap)
    es, p_own, p_oth = pl.pallas_call(
        functools.partial(border_kernel, rows, side),
        out_shape=(
            jax.ShapeDtypeStruct(es.shape, BF),
            jax.ShapeDtypeStruct((2 * chans, col_count // 2), BF),
            jax.ShapeDtypeStruct((2 * chans, col_count // 2), BF),
        ),
        in_specs=[vmem] * 8 + [hbm],
        out_specs=(hbm, vmem, vmem),
        scratch_shapes=[
            pltpu.VMEM((5, 3 * allc, col_count), BF),
            pltpu.VMEM((7, 3 * allc, col_count), BF),
            pltpu.VMEM((4, allc, col_count), BF),
            pltpu.SemaphoreType.DMA,
        ],
        input_output_aliases={8: 0},
        compiler_params=limit(16),
        name="border",
    )(outer, masks, w1, w2, wm, xa, ha, ea, es)
    p_recv = lax.ppermute(p_oth, "chan", swap)
    all_rows = side * chans + (8 if fold > 1 else 0)
    packed = pl.pallas_call(
        functools.partial(pack_kernel, side, slots),
        out_shape=jax.ShapeDtypeStruct((blocks, all_rows, lanes), BF),
        in_specs=[vmem] * 5,
        out_specs=hbm,
        scratch_shapes=[
            pltpu.VMEM((blocks, all_rows, lanes), BF),
            pltpu.VMEM((2 * parent_rows, side * chans, lanes), BF),
            pltpu.VMEM((side, side * chans, lanes), BF),
            pltpu.VMEM((blocks, side * chans, lanes), BF),
            pltpu.VMEM((parents_dev * side, lanes), BF if fold == 1 else jnp.int32),
            pltpu.SemaphoreType.DMA((max(1, blocks // side),)),
        ],
        compiler_params=limit(16),
        name="pack",
    )(parent_owner[None, :], m_own, m_recv, p_own, p_recv)

    def to_peers(x):
        if fold > 1:
            x = x.reshape(blocks, all_rows, fold, lanes // fold)
            x = x.transpose(0, 2, 1, 3).reshape(devices, all_rows, lanes // fold)
        x = lax.all_to_all(x, "tiles", split_axis=0, concat_axis=0, tiled=True)
        if fold > 1:
            x = x.reshape(blocks, fold, all_rows, lanes // fold)
            x = x.transpose(0, 2, 1, 3).reshape(blocks, all_rows, lanes)
        return x

    got = to_peers(packed)
    held, e_oth = pl.pallas_call(
        restore_kernel,
        out_shape=(
            jax.ShapeDtypeStruct((chans, row_count, col_count), BF),
            jax.ShapeDtypeStruct((chans, rows, col_count), BF),
        ),
        in_specs=[hbm, hbm],
        out_specs=(hbm, vmem),
        scratch_shapes=[
            pltpu.VMEM((rows, allc, col_count), BF),
            pltpu.VMEM((chans, rows, col_count), BF),
            pltpu.SemaphoreType.DMA,
            pltpu.SemaphoreType.DMA((rows // BLK,)),
        ],
        compiler_params=limit(12),
        name="restore",
    )(es, packed)
    e_recv = lax.ppermute(e_oth, "chan", swap)
    enhanced = pl.pallas_call(
        fill_kernel,
        out_shape=jax.ShapeDtypeStruct((chans, row_count, col_count), BF),
        in_specs=[vmem, hbm],
        out_specs=hbm,
        scratch_shapes=[pltpu.SemaphoreType.DMA],
        input_output_aliases={1: 0},
        compiler_params=limit(6),
        name="fill",
    )(e_recv, held)
    room = pl.cdiv(own_cap, lanes) * lanes
    parents = pl.pallas_call(
        functools.partial(unpack_kernel, side, slots),
        out_shape=jax.ShapeDtypeStruct((chans, side * side, own_cap), BF),
        in_specs=[vmem],
        out_specs=hbm,
        scratch_shapes=[
            pltpu.VMEM((chans, side * side, own_cap), BF),
            pltpu.VMEM((side, side * chans, room), BF),
            pltpu.VMEM((2, side, side * chans, lanes), BF),
            pltpu.VMEM((2, 2 * lanes, lanes), BF),
            pltpu.SemaphoreType.DMA((chans // BLK,)),
        ],
        compiler_params=limit(24),
        name="unpack",
    )(got)
    return enhanced, jnp.swapaxes(parents, 1, 2)


def solution(mesh):
    return jax.shard_map(
        on_device,
        mesh=mesh,
        in_specs=(
            P("chan", "tiles", None),
            P("tiles", None),
            P("tiles"),
            P(None, "chan", None),
            P(None, "chan", None),
            P(None, None, "chan"),
        ),
        out_specs=(P("chan", "tiles", None), P("chan", "tiles", None)),
        check_vma=False,
    )
```
